32 devices in a mesh: seg: 4 (over x, core), wide: 8 (over z, y).
Axes of the slice: x: 2, y: 2, z: 4, core: 2. Of those that a mesh axis runs over, the one named last changes fastest.
Arguments:
- encoded: bfloat16 [4, 4096, 384], P('seg', 'wide'), may hold values from -6 to 6
- targets: float32 [4, 2048, 128], P('seg'), may hold values from -60 to 60
- present: int32 [4, 4], P('seg'), may hold values 0 or 1
- wide_master: float32 [768, 3200], P('wide'), may hold values from -2 to 2
- down_master: float32 [3072, 384], P('wide'), may hold values from -0.15625 to 0.15625
- gain_master: float32 [6144], P('wide'), may hold values from -2 to 2
- wide_first: float32 [768, 3200], P('wide'), may hold values from -3.5762787e-07 to 3.5762787e-07
- down_first: float32 [3072, 384], P('wide'), may hold values from -3.5762787e-07 to 3.5762787e-07
- gain_first: float32 [6144], P('wide'), may hold values from -1.4305115e-06 to 1.4305115e-06
- wide_second: float32 [768, 3200], P('wide'), may hold values from 2.744695e-16 to 1.097878e-15
- down_second: float32 [3072, 384], P('wide'), may hold values from 2.744695e-16 to 1.097878e-15
- gain_second: float32 [6144], P('wide'), may hold values from 4.391512e-15 to 1.7566049e-14
Outputs:
- loss: float32 [], replicated
- grad_norm: float32 [], replicated
- wide_new: float32 [768, 3200], P('wide')
- down_new: float32 [3072, 384], P('wide')
- gain_new: float32 [6144], P('wide')
- wide_first_new: float32 [768, 3200], P('wide')
- down_first_new: float32 [3072, 384], P('wide')
- gain_first_new: float32 [6144], P('wide')
- wide_second_new: float32 [768, 3200], P('wide')
- down_second_new: float32 [3072, 384], P('wide')
- gain_second_new: float32 [6144], P('wide')
- wide_copy: bfloat16 [768, 3200], P('wide')
- down_copy: bfloat16 [3072, 384], P('wide')
- gain_copy: bfloat16 [6144], P('wide')
The draws below stay inside these ranges and needn't reach their ends.
All inputs are finite; a program needn't handle non-finite values. No bound on the sum of `present` on one device may be relied on, other than what follows from the above.
Results may differ from the reference program's by a relative error of at most 0.015.
Values may be sent and summed in bfloat16 or wider, within the bound.
No kernel may reach another device: no remote copies, remote signals or barrier semaphores. Data moves between devices by JAX's collectives and lax.ppermute only.
A program may use at most 192 MiB of HBM per device.

```python
import math
import jax
import jax.numpy as jnp
from jax import lax

D = 384
HEADS = 8
FF = 1536
STEMS = 4
SAMPLES = 32
ADAM_STEP = 10
LENGTH = 2048
SEGS = 4
PARAMS = 3643392


def draw_targets(key, part):
    shape = (SEGS, LENGTH, STEMS, SAMPLES)
    key_one, key_two = jax.random.split(jax.random.fold_in(key, 11))
    base = jnp.clip(jax.random.normal(key_one, shape, jnp.float32), -6.0, 6.0)
    loud = jnp.exp(jax.random.uniform(key_two, (SEGS, 1, STEMS, 1), jnp.float32, -0.7, 0.7))
    ramp = 1.0 + 2.0 * jnp.arange(LENGTH, dtype=jnp.float32) / LENGTH
    return (base * loud * ramp[None, :, None, None]).reshape(SEGS, LENGTH, STEMS * SAMPLES)


def draw_wide_master(key, part):
    columns = 4 * D + FF + STEMS * SAMPLES
    shape = (2 * D, columns)
    key_one = jax.random.fold_in(key, 23)
    base = jnp.clip(jax.random.normal(key_one, shape, jnp.float32), -6.0, 6.0)
    boost = jnp.where(jnp.arange(columns) < 2 * D, 1.7, 1.0)
    return base * boost[None, :] / math.sqrt(D)


def draw_gain_master(key, part):
    key_one, key_two = jax.random.split(jax.random.fold_in(key, 37))
    uniform_part = jax.random.uniform(key_one, (16, D), jnp.float32)
    which = jnp.arange(16) % 8
    is_shift = (which < 6) & (which % 2 == 1)
    gain_value = 0.6 + 0.8 * uniform_part
    shift_value = 0.2 * jnp.clip(jax.random.normal(key_two, (16, D), jnp.float32), -6.0, 6.0)
    return jnp.where(is_shift[:, None], shift_value, gain_value).reshape(16 * D)


def set_ends(drawn, rng, low, largest):
    longest = drawn.shape.index(max(drawn.shape))
    spots = []
    for shift in (0, 1):
        where = [jax.random.randint(jax.random.fold_in(rng, axis), (), 0, length) for axis, length in enumerate(drawn.shape)]
        where[longest] = (where[longest] + shift) % drawn.shape[longest]
        spots.append(tuple(where))
    return drawn.at[spots[0]].set(low).at[spots[1]].set(largest)


def levels(key, extent, cuts, least, largest):
    level, own = 1.0, jax.random.fold_in(key, 6)
    for dim, parts in cuts:
        steps = jnp.exp(jax.random.uniform(jax.random.fold_in(own, dim), (parts,), jnp.float32, least / len(cuts), largest / len(cuts)))
        level = level * jnp.repeat(steps, extent[dim] // parts).reshape([-1 if axis == dim else 1 for axis in range(len(extent))])
    return level


def scatter_about(rng, dims, deviation, bound, shards=(), held_as=jnp.bfloat16):
    result = deviation * jax.random.normal(rng, dims, jnp.float32)
    if shards:
        result = result * levels(rng, dims, shards, -0.22, 0.18)
    return jnp.clip(result, -bound, bound).astype(held_as)


def setup_inputs(seed: int = 0) -> dict:
    streams_of = jax.random.split(jax.random.key(seed), 13)
    encoded = scatter_about(streams_of[0], (SEGS, 2 * LENGTH, D), 1.0, 6.0, ((0, 4), (1, 8)))
    targets = draw_targets(jax.random.fold_in(streams_of[12], 71), 0)
    present = set_ends((jax.random.randint(streams_of[2], (SEGS, STEMS), 0, 4) < 3).astype(jnp.int32), jax.random.fold_in(streams_of[2], 1), 0, 1)
    wide_master = draw_wide_master(jax.random.fold_in(streams_of[12], 71), 0)
    down_master = scatter_about(streams_of[4], (2 * FF, D), FF ** -0.5, 0.15625, ((0, 8),), jnp.float32)
    gain_master = draw_gain_master(jax.random.fold_in(streams_of[12], 71), 0)
    wide_first = scatter_about(streams_of[6], (2 * D, 4 * D + FF + STEMS * SAMPLES), (0.00011 * PARAMS ** -0.5), 3.5762786865234375e-07, ((0, 8),), jnp.float32)
    down_first = scatter_about(streams_of[7], (2 * FF, D), (0.00011 * PARAMS ** -0.5), 3.5762786865234375e-07, ((0, 8),), jnp.float32)
    gain_first = scatter_about(streams_of[8], (16 * D,), (0.00044 * PARAMS ** -0.5), 1.430511474609375e-06, ((0, 8),), jnp.float32)
    wide_second = jnp.clip(jnp.exp(math.log(1.0978780488145171e-15) - 1.3862944 * jax.random.uniform(streams_of[9], (2 * D, 4 * D + FF + STEMS * SAMPLES), jnp.float32) ** levels(streams_of[9], (2 * D, 4 * D + FF + STEMS * SAMPLES), ((0, 8),), -0.2, 0.2)), 2.744695122036293e-16, 1.0978780488145171e-15)
    down_second = jnp.clip(jnp.exp(math.log(1.0978780488145171e-15) - 1.3862944 * jax.random.uniform(streams_of[10], (2 * FF, D), jnp.float32) ** levels(streams_of[10], (2 * FF, D), ((0, 8),), -0.2, 0.2)), 2.744695122036293e-16, 1.0978780488145171e-15)
    gain_second = jnp.clip(jnp.exp(math.log(1.7566048781032274e-14) - 1.3862944 * jax.random.uniform(streams_of[11], (16 * D,), jnp.float32) ** levels(streams_of[11], (16 * D,), ((0, 8),), -0.2, 0.2)), 4.3915121952580686e-15, 1.7566048781032274e-14)
    return {"encoded": encoded, "targets": targets, "present": present, "wide_master": wide_master, "down_master": down_master, "gain_master": gain_master, "wide_first": wide_first, "down_first": down_first, "gain_first": gain_first, "wide_second": wide_second, "down_second": down_second, "gain_second": gain_second}


NORM_EPS = 1e-05
ENERGY_EPS = 1e-05
BETA_ONE = 0.9
BETA_TWO = 0.999
ADAM_EPS = 1e-08
LEARN_RATE = 0.1
GAIN_RATE = 0.5
WEIGHT_DECAY = 0.01
CLIP_LIMIT = 0.001
HIGHEST = lax.Precision.HIGHEST

@jax.custom_vjp
def low(v):
    return lax.optimization_barrier(v.astype(jnp.bfloat16)).astype(jnp.float32)

@jax.custom_vjp
def low_back(v):
    return v

def low_keep(v):
    return (low(v), None)

def low_pass(kept, grad):
    return (grad,)

def back_keep(v):
    return (v, None)

def back_low(kept, grad):
    return (low(grad),)
low.defvjp(low_keep, low_pass)
low_back.defvjp(back_keep, back_low)

def wire(value):
    return low(low_back(value))

def matmul(left, right):
    return jnp.dot(left, right, precision=HIGHEST)

def layer_norm(values, gain, shift):
    centred = values - lax.optimization_barrier(jnp.mean(values, axis=-1, keepdims=True))
    spread = lax.optimization_barrier(jnp.mean(centred * centred, axis=-1, keepdims=True))
    return centred * lax.rsqrt(spread + NORM_EPS) * gain + shift

def attend(queries, key_vals):
    row_count = queries.shape[0]
    head_size = D // HEADS
    keys = key_vals[:, :D].reshape(-1, HEADS, head_size)
    values = key_vals[:, D:].reshape(-1, HEADS, head_size)
    key_block = math.gcd(row_count, 512)

    def one_block(query_block):
        scores = low_back(jnp.einsum('qhd,khd->hqk', query_block, keys, precision=HIGHEST) / math.sqrt(head_size))
        weights = jax.nn.softmax(scores, axis=-1)
        return jnp.einsum('hqk,khd->qhd', low(weights), values, precision=HIGHEST)
    blocks = queries.reshape(row_count // key_block, key_block, HEADS, head_size)
    return lax.map(jax.checkpoint(one_block), blocks).reshape(row_count, D)

def branch_estimate(own_rows, other_rows, wide_all, down_all, gain_all, branch):
    gain_set = gain_all[branch]
    wide_set = wide_all[branch]
    normed = low(layer_norm(own_rows, gain_set[0], gain_set[1]))
    crossed = low(layer_norm(other_rows, gain_set[2], gain_set[3]))
    queries = wire(matmul(normed, wide_set[:, :D]))
    key_vals = wire(matmul(crossed, wide_set[:, D:3 * D]))
    attended = wire(attend(queries, key_vals))
    mid_rows = own_rows + gain_set[6] * low_back(matmul(attended, wide_set[:, 3 * D:4 * D]))
    normed_two = low(layer_norm(mid_rows, gain_set[4], gain_set[5]))
    pre_act = low_back(matmul(normed_two, wide_set[:, 4 * D:4 * D + FF]))
    hidden = wire(jax.nn.gelu(pre_act, approximate=False))
    out_rows = mid_rows + gain_set[7] * low_back(matmul(hidden, down_all[branch]))
    return low_back(matmul(low(out_rows), wide_set[:, 4 * D + FF:]))

def sdr_loss(estimate, seg_target, seg_present):
    errors = (seg_target - estimate).reshape(-1, STEMS, SAMPLES)
    clean = seg_target.reshape(-1, STEMS, SAMPLES)
    err_energy = lax.optimization_barrier(jnp.sum(errors * errors, axis=(0, 2)))
    tgt_energy = lax.optimization_barrier(jnp.sum(clean * clean, axis=(0, 2)))
    ratio = 10.0 / math.log(10.0) * (jnp.log(tgt_energy + ENERGY_EPS) - jnp.log(err_energy + ENERGY_EPS))
    return -jnp.sum(seg_present.astype(jnp.float32) * ratio) / (SEGS * STEMS)

def total_loss(params, encoded, targets, present):
    wide_all = low(params[0]).reshape(2, D, -1)
    down_all = low(params[1]).reshape(2, FF, D)
    gain_all = low(params[2]).reshape(2, 8, D)

    def segment(carry, item):
        seg_rows, seg_target, seg_present = item
        time_rows = seg_rows[:LENGTH]
        spec_rows = seg_rows[LENGTH:]
        estimate = branch_estimate(time_rows, spec_rows, wide_all, down_all, gain_all, 0)
        estimate = estimate + branch_estimate(spec_rows, time_rows, wide_all, down_all, gain_all, 1)
        return (carry + sdr_loss(estimate, seg_target, seg_present), None)
    total, _ = lax.scan(segment, jnp.zeros((), jnp.float32), (encoded, targets, present))
    return total

def adam_update(weight, grad, moment, second, rate):
    moment = BETA_ONE * moment + (1 - BETA_ONE) * grad
    second = BETA_TWO * second + (1 - BETA_TWO) * grad * grad
    fixed_one = moment / (1 - BETA_ONE ** ADAM_STEP)
    fixed_two = second / (1 - BETA_TWO ** ADAM_STEP)
    weight = weight - rate * (fixed_one / (jnp.sqrt(fixed_two) + ADAM_EPS) + WEIGHT_DECAY * weight)
    return (weight, moment, second)

def reference(encoded, targets, present, wide_master, down_master, gain_master, wide_first, down_first, gain_first, wide_second, down_second, gain_second):
    params = (wide_master, down_master, gain_master)
    floats = encoded.astype(jnp.float32)
    loss, pull = jax.vjp(lambda weights: total_loss(weights, floats, targets, present), params)
    grads = pull(jnp.ones((), jnp.float32))[0]
    grad_norm = jnp.sqrt(jnp.sum(grads[0] * grads[0]) + jnp.sum(grads[1] * grads[1]) + jnp.sum(grads[2] * grads[2]))
    factor = jnp.minimum(1.0, CLIP_LIMIT / (grad_norm + 1e-06))
    wide_out = adam_update(wide_master, grads[0] * factor, wide_first, wide_second, LEARN_RATE)
    down_out = adam_update(down_master, grads[1] * factor, down_first, down_second, LEARN_RATE)
    gain_out = adam_update(gain_master, grads[2] * factor, gain_first, gain_second, GAIN_RATE)
    return (loss, grad_norm, wide_out[0], down_out[0], gain_out[0], wide_out[1], down_out[1], gain_out[1], wide_out[2], down_out[2], gain_out[2], wide_out[0].astype(jnp.bfloat16), down_out[0].astype(jnp.bfloat16), gain_out[0].astype(jnp.bfloat16))
```

```python
import math

import jax
import jax.numpy as jnp
from jax import lax
from jax.experimental import pallas as pl
from jax.experimental.pallas import tpu as pltpu
from jax.sharding import PartitionSpec as P

D = 384
HEADS = 8
HEAD = D // HEADS
FF = 1536
STEMS = 4
SAMPLES = 32
OUT = STEMS * SAMPLES
QKV = 3 * D
REST = D + FF + OUT
ADAM_STEP = 10
LANES = 128

NORM_EPS = 1e-05
ENERGY_EPS = 1e-05
BETA_ONE = 0.9
BETA_TWO = 0.999
ADAM_EPS = 1e-08
LEARN_RATE = 0.1
GAIN_RATE = 0.5
WEIGHT_DECAY = 0.01
CLIP_LIMIT = 0.001

BF = jnp.bfloat16
F32 = jnp.float32
SCALE = 1.0 / math.sqrt(HEAD)
LOG_TWO = math.log(2.0)
VMEM_LIMIT = 60 * 2**20


def swap(x, axis, mask):
    return lax.ppermute(x, axis, [(i, i ^ mask) for i in range(lax.axis_size(axis))])


def dot(left, right, left_dim=1, right_dim=0):
    return lax.dot_general(
        left,
        right,
        (((left_dim,), (right_dim,)), ((), ())),
        preferred_element_type=F32,
    )


def unit_rows(values):
    centred = values - jnp.mean(values, axis=-1, keepdims=True)
    spread = jnp.mean(centred * centred, axis=-1, keepdims=True)
    inverse = lax.rsqrt(spread + NORM_EPS)
    return centred * inverse, inverse


def call(kernel, out_shape, flops, moved, **more):
    return pl.pallas_call(
        kernel,
        out_shape=out_shape,
        compiler_params=pltpu.CompilerParams(vmem_limit_bytes=VMEM_LIMIT),
        cost_estimate=pl.CostEstimate(flops=flops, bytes_accessed=moved, transcendentals=0),
        **more,
    )


def sds(shape, dtype):
    return jax.ShapeDtypeStruct(shape, dtype)


def attend_kernel(own, blocks, weights, gains, probs, keys_t, values_t, unit, tops,
                  queries_t, own_unit, weights_t, attended_t, final_top, inverse_total,
                  accum, top):
    step = pl.program_id(0)
    last = pl.num_programs(0) - 1

    @pl.when(step == 0)
    def _():
        weights_t[...] = weights[:, :QKV].T
        hat, _ = unit_rows(own[...].astype(F32))
        own_unit[...] = hat.astype(BF)
        normed = (hat * gains[0:1] + gains[1:2]).astype(BF)
        found = dot(weights_t[:D], normed, 1, 1)
        queries_t[...] = (found * (SCALE / LOG_TWO)).astype(BF)
        accum[...] = jnp.zeros_like(accum)
        top[...] = jnp.full_like(top, -1e30)

    hat, _ = unit_rows(blocks[0].astype(F32))
    unit[0] = hat.astype(BF)
    crossed = (hat * gains[2:3] + gains[3:4]).astype(BF)
    keys_t[0] = dot(weights_t[D : 2 * D], crossed, 1, 1).astype(BF)
    values_t[0] = dot(weights_t[2 * D :], crossed, 1, 1).astype(BF)
    rows = crossed.shape[0]
    ones = jnp.ones((16, rows), BF)
    for h in range(HEADS):
        at = slice(HEAD * h, HEAD * (h + 1))
        wide = slice(64 * h, 64 * (h + 1))
        scores = dot(keys_t[0, at], queries_t[at], 0, 0)
        before = top[h : h + 1]
        newest = jnp.maximum(before, jnp.max(scores, axis=0, keepdims=True))
        top[h : h + 1] = newest
        weight = jnp.exp2(scores - newest).astype(BF)
        probs[0, h] = weight
        values = jnp.concatenate([values_t[0, at], ones], axis=0)
        accum[wide] = accum[wide] * jnp.exp2(before - newest) + dot(values, weight)
    tops[0] = top[...]

    @pl.when(step == last)
    def _():
        final_top[...] = top[...]
        for h in range(HEADS):
            total = accum[64 * h + HEAD : 64 * h + HEAD + 1]
            inverse = 1.0 / total
            inverse_total[h : h + 1] = inverse
            attended_t[HEAD * h : HEAD * (h + 1)] = accum[64 * h : 64 * h + HEAD] * inverse


def attend(own, blocks, weights, gains):
    count, rows, _ = blocks.shape
    whole = lambda *shape: pl.BlockSpec(shape, lambda j: (0,) * len(shape))
    each = lambda *shape: pl.BlockSpec((1,) + shape, lambda j: (j,) + (0,) * len(shape))
    return call(
        attend_kernel,
        (
            sds((count, HEADS, rows, rows), BF),
            sds((count, D, rows), BF),
            sds((count, D, rows), BF),
            sds((count, rows, D), BF),
            sds((count, HEADS, rows), F32),
            sds((D, rows), BF),
            sds((rows, D), BF),
            sds((QKV, D), BF),
            sds((D, rows), F32),
            sds((HEADS, rows), F32),
            sds((HEADS, rows), F32),
        ),
        count * (4 * rows * rows * D * 5 + 4 * rows * D * D),
        count * (HEADS * rows * rows * 2),
        grid=(count,),
        in_specs=[whole(rows, D), each(rows, D), whole(*weights.shape), whole(8, D)],
        out_specs=(
            each(HEADS, rows, rows),
            each(D, rows),
            each(D, rows),
            each(rows, D),
            each(HEADS, rows),
            whole(D, rows),
            whole(rows, D),
            whole(QKV, D),
            whole(D, rows),
            whole(HEADS, rows),
            whole(HEADS, rows),
        ),
        scratch_shapes=[pltpu.VMEM((64 * HEADS, rows), F32), pltpu.VMEM((HEADS, rows), F32)],
    )(own, blocks, weights, gains)


def dense_kernel(inputs, attended_t, rest, down, gains, estimate, branch_out, third,
                 third_inverse, normed_two, slope, hidden, ffn_out, out_rows):
    branch = dot(attended_t[...].astype(BF), rest[:, :D], 0, 0)
    branch_out[...] = branch
    mid = inputs[...].astype(F32) + gains[6:7] * branch
    hat, inverse = unit_rows(mid)
    third[...] = hat
    third_inverse[...] = inverse
    normed = (hat * gains[4:5] + gains[5:6]).astype(BF)
    normed_two[...] = normed
    pre = dot(normed, rest[:, D : D + FF])
    gate = 0.5 * (1.0 + lax.erf(pre * math.sqrt(0.5)))
    hid = (pre * gate).astype(BF)
    hidden[...] = hid
    bell = jnp.exp(-0.5 * pre * pre) * (1.0 / math.sqrt(2.0 * math.pi))
    slope[...] = gate + pre * bell
    ffn = dot(hid, down[...])
    ffn_out[...] = ffn
    out = (mid + gains[7:8] * ffn).astype(BF)
    out_rows[...] = out
    estimate[...] = dot(out, rest[:, D + FF :]).astype(BF)


def dense_forward(inputs, attended_t, rest, down, gains):
    rows = inputs.shape[0]
    return call(
        dense_kernel,
        (
            sds((rows, OUT), BF),
            sds((rows, D), F32),
            sds((rows, D), F32),
            sds((rows, 1), F32),
            sds((rows, D), BF),
            sds((rows, FF), F32),
            sds((rows, FF), BF),
            sds((rows, D), F32),
            sds((rows, D), BF),
        ),
        2 * rows * D * (D + 2 * FF + OUT),
        rows * FF * 8,
    )(inputs, attended_t, rest, down, gains)


def dense_back_kernel(grad_est, rest, down, gains, branch_out, third, third_inverse,
                      slope, ffn_out, grad_ffn, grad_pre, grad_branch, grad_attended_t,
                      grad_gains):
    low = grad_est[...]
    grad_out = dot(low, rest[:, D + FF :], 1, 1)
    grad_gains[3:4] = jnp.sum(grad_out * ffn_out[...], axis=0, keepdims=True)
    ffn = (grad_out * gains[7:8]).astype(BF)
    grad_ffn[...] = ffn
    hidden = dot(ffn, down[...], 1, 1).astype(BF)
    pre = (hidden.astype(F32) * slope[...]).astype(BF)
    grad_pre[...] = pre
    normed = dot(pre, rest[:, D : D + FF], 1, 1)
    hat = third[...]
    grad_gains[0:1] = jnp.sum(normed * hat, axis=0, keepdims=True)
    grad_gains[1:2] = jnp.sum(normed, axis=0, keepdims=True)
    scaled = normed * gains[4:5]
    grad_mid = grad_out + third_inverse[...] * (
        scaled
        - jnp.mean(scaled, axis=-1, keepdims=True)
        - hat * jnp.mean(scaled * hat, axis=-1, keepdims=True)
    )
    grad_gains[2:3] = jnp.sum(grad_mid * branch_out[...], axis=0, keepdims=True)
    branch = (grad_mid * gains[6:7]).astype(BF)
    grad_branch[...] = branch
    grad_attended_t[...] = dot(rest[:, :D], branch, 1, 1).astype(BF)


def dense_back(grad_est, rest, down, gains, branch_out, third, third_inverse, slope, ffn_out):
    rows = grad_est.shape[0]
    return call(
        dense_back_kernel,
        (
            sds((rows, D), BF),
            sds((rows, FF), BF),
            sds((rows, D), BF),
            sds((D, rows), BF),
            sds((4, D), F32),
        ),
        2 * rows * D * (D + 2 * FF + OUT),
        rows * FF * 8,
    )(grad_est, rest, down, gains, branch_out, third, third_inverse, slope, ffn_out)


def dense_weights_kernel(grad_est, grad_ffn, grad_pre, grad_branch, attended_t, normed_two,
                         hidden, out_rows, grad_rest, grad_down):
    grad_rest[:, D + FF :] = dot(out_rows[...], grad_est[...], 0, 0).astype(BF)
    grad_rest[:, D : D + FF] = dot(normed_two[...], grad_pre[...], 0, 0).astype(BF)
    grad_rest[:, :D] = dot(attended_t[...].astype(BF), grad_branch[...]).astype(BF)
    grad_down[...] = dot(hidden[...], grad_ffn[...], 0, 0).astype(BF)


def dense_weights(grad_est, grad_ffn, grad_pre, grad_branch, attended_t, normed_two, hidden,
                  out_rows):
    rows = grad_est.shape[0]
    return call(
        dense_weights_kernel,
        (sds((D, REST), BF), sds((FF, D), BF)),
        2 * rows * D * (D + 2 * FF + OUT),
        rows * FF * 8,
    )(grad_est, grad_ffn, grad_pre, grad_branch, attended_t, normed_two, hidden, out_rows)


def attend_back_kernel(probs, keys_t, values_t, unit, tops, queries_t, own_unit, weights_t,
                       attended_t, final_top, inverse_total, grad_attended_t, gains,
                       grad_weights, grad_gains, delta, grad_queries, grad_kv, moments):
    step = pl.program_id(0)
    last = pl.num_programs(0) - 1
    rows = unit.shape[1]

    @pl.when(step == 0)
    def _():
        for h in range(HEADS):
            at = slice(HEAD * h, HEAD * (h + 1))
            product = grad_attended_t[at].astype(F32) * attended_t[at]
            delta[h : h + 1] = jnp.sum(product, axis=0, keepdims=True)
        grad_queries[...] = jnp.zeros_like(grad_queries)
        moments[...] = jnp.zeros_like(moments)

    factor = jnp.exp2(tops[0] - final_top[...]) * inverse_total[...]
    shift = delta[...] * factor
    for h in range(HEADS):
        at = slice(HEAD * h, HEAD * (h + 1))
        low = slice(D + HEAD * h, D + HEAD * (h + 1))
        grad = (grad_attended_t[at].astype(F32) * factor[h : h + 1]).astype(BF)
        weight = probs[0, h]
        grad_probs = dot(values_t[0, at], grad, 0, 0)
        scores = (weight.astype(F32) * (grad_probs - shift[h : h + 1])).astype(BF)
        grad_queries[at] += dot(keys_t[0, at], scores)
        grad_kv[at] = (dot(queries_t[at], scores, 1, 1) * LOG_TWO).astype(BF)
        grad_kv[low] = dot(grad, weight, 1, 1).astype(BF)
    ones = jnp.ones((rows, LANES), BF)
    moments[D:] += dot(grad_kv[...], jnp.concatenate([unit[0], ones], axis=1))

    @pl.when(step == last)
    def _():
        query = (grad_queries[...] * SCALE).astype(BF)
        moments[:D] = dot(query, jnp.concatenate([own_unit[...], ones], axis=1))
        for first, size, row in ((0, D, 0), (D, 2 * D, 2)):
            at = slice(first, first + size)
            moment = moments[at, :D]
            column = moments[at, D : D + 1]
            weight = weights_t[at].astype(F32)
            grad_gains[row : row + 1] = jnp.sum(weight * moment, axis=0, keepdims=True)
            grad_gains[row + 1 : row + 2] = jnp.sum(weight * column, axis=0, keepdims=True)
            full = moment * gains[row : row + 1] + column * gains[row + 1 : row + 2]
            grad_weights[:, at] = full.T.astype(BF)


def attend_back(saved, grad_attended_t, gains):
    (probs, keys_t, values_t, unit, tops, queries_t, own_unit, weights_t, attended_t,
     final_top, inverse_total) = saved
    count, rows, _ = unit.shape
    whole = lambda *shape: pl.BlockSpec(shape, lambda j: (0,) * len(shape))
    each = lambda *shape: pl.BlockSpec((1,) + shape, lambda j: (j,) + (0,) * len(shape))
    return call(
        attend_back_kernel,
        (sds((D, QKV), BF), sds((4, D), F32)),
        count * (8 * rows * rows * D * 5),
        count * (HEADS * rows * rows * 2),
        grid=(count,),
        in_specs=[
            each(HEADS, rows, rows),
            each(D, rows),
            each(D, rows),
            each(rows, D),
            each(HEADS, rows),
            whole(D, rows),
            whole(rows, D),
            whole(QKV, D),
            whole(D, rows),
            whole(HEADS, rows),
            whole(HEADS, rows),
            whole(D, rows),
            whole(8, D),
        ],
        out_specs=(whole(D, QKV), whole(4, D)),
        scratch_shapes=[
            pltpu.VMEM((HEADS, rows), F32),
            pltpu.VMEM((D, rows), F32),
            pltpu.VMEM((2 * D, rows), BF),
            pltpu.VMEM((QKV, D + LANES), F32),
        ],
    )(probs, keys_t, values_t, unit, tops, queries_t, own_unit, weights_t, attended_t,
      final_top, inverse_total, grad_attended_t, gains)


def bits(size):
    return [1 << k for k in range(size.bit_length() - 1)]


def gather_group(x, position, size):
    stack = x[None]
    for mask in bits(size):
        other = swap(stack, "wide", mask)
        upper = (position & mask) > 0
        stack = jnp.where(
            upper, jnp.concatenate([other, stack], 0), jnp.concatenate([stack, other], 0)
        )
    return stack


def gather_rows(x, position, size, core):
    half = x.shape[0] // 2
    mine = gather_group(lax.dynamic_slice_in_dim(x, core * half, half, 0), position, size)
    other = swap(mine, "seg", 1)
    both = jnp.where(
        core == 0, jnp.stack([mine, other], axis=1), jnp.stack([other, mine], axis=1)
    )
    return both.reshape(size * x.shape[0], x.shape[1])


def reduce_rows(grads, position, size, core):
    rows = grads.shape[0] // size
    pieces = grads.reshape(size, 2, rows // 2, grads.shape[1])
    keep = lax.dynamic_index_in_dim(pieces, core, 1, keepdims=False)
    send = lax.dynamic_index_in_dim(pieces, 1 - core, 1, keepdims=False)
    total = keep.astype(F32) + swap(send, "seg", 1).astype(F32)
    for mask in reversed(bits(size)):
        total = total.astype(BF).reshape((2, mask) + total.shape[1:])
        bit = (position & mask) // mask
        keep = lax.dynamic_index_in_dim(total, bit, 0, keepdims=False)
        send = lax.dynamic_index_in_dim(total, 1 - bit, 0, keepdims=False)
        total = keep.astype(F32) + swap(send, "wide", mask).astype(F32)
    total = total[0]
    for mask in bits(lax.axis_size("seg"))[1:]:
        low = total.astype(BF)
        total = low.astype(F32) + swap(low, "seg", mask).astype(F32)
    mine = total.astype(BF)
    other = swap(mine, "seg", 1)
    both = jnp.where(core == 0, jnp.concatenate([mine, other]), jnp.concatenate([other, mine]))
    return both.astype(F32)


def gain_shape(size):
    count = 8 * D // size
    width = math.gcd(count, LANES)
    return count // width, width


def pack_gains(gains, rows, size):
    tall, across = gain_shape(size)
    block = gains.reshape(-1, tall, across)
    return jnp.pad(block, ((0, 0), (0, rows - tall), (0, LANES - across)))


def unpack_gains(block, size):
    tall, across = gain_shape(size)
    return block[:, :tall, :across].reshape(-1)


def pack_down(down):
    rows = down.shape[-2] // 4
    split = down.reshape(-1, 4, rows, D)
    return jnp.moveaxis(split, 1, 2).reshape(-1, rows, 4 * D)


def unpack_down(block):
    rows = block.shape[-2]
    split = block.reshape(-1, rows, 4, D)
    return jnp.moveaxis(split, 2, 1).reshape(-1, D)


def adam_update(weight, grad, moment, second, rate):
    moment = BETA_ONE * moment + (1 - BETA_ONE) * grad
    second = BETA_TWO * second + (1 - BETA_TWO) * grad * grad
    fixed_one = moment / (1 - BETA_ONE**ADAM_STEP)
    fixed_two = second / (1 - BETA_TWO**ADAM_STEP)
    weight = weight - rate * (fixed_one / (jnp.sqrt(fixed_two) + ADAM_EPS) + WEIGHT_DECAY * weight)
    return (weight, moment, second)


def body(
    encoded,
    targets,
    present,
    wide_master,
    down_master,
    gain_master,
    wide_first,
    down_first,
    gain_first,
    wide_second,
    down_second,
    gain_second,
):
    size = lax.axis_size("wide") // 2
    position = lax.axis_index("wide") % size
    core = lax.axis_index("seg") % 2
    own = encoded[0]
    tokens = own.shape[0]
    rows = wide_master.shape[0]

    far = swap(own, "wide", size)[None]
    for mask in bits(size):
        far = jnp.concatenate([far, swap(far, "wide", mask)], 0)

    first_pack = jnp.concatenate(
        [
            wide_master[:, :QKV].astype(BF),
            pack_gains(gain_master.astype(BF), rows, size)[0],
        ],
        axis=1,
    )
    rest_pack = jnp.concatenate(
        [wide_master[:, QKV:].astype(BF), pack_down(down_master.astype(BF))[0]], axis=1
    )
    first_all = gather_rows(first_pack, position, size, core)
    gains = unpack_gains(first_all[:, QKV:].reshape(size, rows, LANES), size)
    gains = gains.astype(F32).reshape(8, D)
    rest_all = gather_rows(rest_pack, position, size, core)
    rest = rest_all[:, :REST]
    down = unpack_down(rest_all[:, REST:].reshape(size, rows, 4 * D))

    saved = attend(own, far, first_all, gains)
    attended_t = saved[8]
    (est_own, branch_out, third, third_inverse, normed_two, slope, hidden, ffn_out,
     out_rows) = dense_forward(own, attended_t, rest, down, gains)

    estimate = est_own.astype(F32) + swap(est_own, "wide", size).astype(F32)
    mine = lax.dynamic_slice_in_dim(targets[0], position * tokens, tokens, 0)
    errors = mine - estimate
    energy = jnp.stack([jnp.sum(errors * errors, axis=0), jnp.sum(mine * mine, axis=0)])
    energy = jnp.sum(energy.reshape(2, STEMS, SAMPLES), axis=-1)
    for mask in bits(size):
        energy = energy + swap(energy, "wide", mask)
    err_energy, tgt_energy = energy[0], energy[1]
    seg_count = lax.axis_size("seg")
    weight_stem = present[0].astype(F32)
    coeff = 10.0 / math.log(10.0)
    loss = -jnp.sum(
        weight_stem * coeff * (jnp.log(tgt_energy + ENERGY_EPS) - jnp.log(err_energy + ENERGY_EPS))
    ) / (seg_count * STEMS)
    for mask in bits(seg_count):
        loss = loss + swap(loss, "seg", mask)
    per_stem = -coeff * weight_stem / (seg_count * STEMS) / (err_energy + ENERGY_EPS)
    grad_est = (errors * jnp.repeat(2.0 * per_stem, SAMPLES)[None, :]).astype(BF)

    grad_ffn, grad_pre, grad_branch, grad_attended_t, late_gains = dense_back(
        grad_est, rest, down, gains, branch_out, third, third_inverse, slope, ffn_out
    )
    grad_rest, grad_down = dense_weights(
        grad_est, grad_ffn, grad_pre, grad_branch, attended_t, normed_two, hidden, out_rows
    )
    grad_early = jnp.concatenate(
        [grad_rest, pack_down(grad_down.reshape(size, 4 * rows, D)).reshape(-1, 4 * D)], axis=1
    )
    early = reduce_rows(grad_early, position, size, core)

    grad_first, early_gains = attend_back(saved, grad_attended_t, gains)
    grad_gains = jnp.concatenate([early_gains, late_gains], 0).astype(BF).reshape(-1)
    grad_late = jnp.concatenate(
        [grad_first, pack_gains(grad_gains, rows, size).reshape(-1, LANES)], axis=1
    )
    late = reduce_rows(grad_late, position, size, core)

    squares = jnp.sum(early * early) + jnp.sum(late * late)
    for mask in bits(2 * size):
        squares = squares + swap(squares, "wide", mask)
    grad_norm = jnp.sqrt(squares)
    factor = jnp.minimum(1.0, CLIP_LIMIT / (grad_norm + 1e-06))
    grads = (
        jnp.concatenate([late[:, :QKV], early[:, :REST]], axis=1),
        unpack_down(early[None, :, REST:]),
        unpack_gains(late[None, :, QKV:], size),
    )
    masters = (wide_master, down_master, gain_master)
    firsts = (wide_first, down_first, gain_first)
    seconds = (wide_second, down_second, gain_second)
    rates = (LEARN_RATE, LEARN_RATE, GAIN_RATE)
    updated = [
        adam_update(
            masters[index], grads[index] * factor, firsts[index], seconds[index], rates[index]
        )
        for index in range(3)
    ]
    return (
        loss,
        grad_norm,
        *(updated[index][kind] for kind in range(3) for index in range(3)),
        *(updated[index][0].astype(BF) for index in range(3)),
    )


def solution(mesh):
    split, line = P("wide", None), P("wide")
    states = (split, split, line)
    return jax.shard_map(
        body,
        mesh=mesh,
        in_specs=(P("seg", "wide", None), P("seg", None, None), P("seg", None)) + states * 3,
        out_specs=(P(), P()) + states * 4,
        check_vma=False,
    )
```

```python
import functools
import math

import jax
import jax.numpy as jnp
from jax import lax
from jax.experimental import pallas as pl
from jax.experimental.pallas import tpu as pltpu
from jax.sharding import PartitionSpec as P

D = 384
HEADS = 8
HEAD = D // HEADS
FF = 1536
STEMS = 4
SAMPLES = 32
OUT = STEMS * SAMPLES
QKV = 3 * D
REST = D + FF + OUT
ADAM_STEP = 10
LANES = 128

NORM_EPS = 1e-05
ENERGY_EPS = 1e-05
BETA_ONE = 0.9
BETA_TWO = 0.999
ADAM_EPS = 1e-08
LEARN_RATE = 0.1
GAIN_RATE = 0.5
WEIGHT_DECAY = 0.01
CLIP_LIMIT = 0.001

BF = jnp.bfloat16
F32 = jnp.float32
SCALE = 1.0 / math.sqrt(HEAD)
LOG_TWO = math.log(2.0)
VMEM_LIMIT = 14 * 2**20


def swap(x, axis, mask):
    return lax.ppermute(x, axis, [(i, i ^ mask) for i in range(lax.axis_size(axis))])


def dot(left, right, left_dim=1, right_dim=0):
    return lax.dot_general(
        left,
        right,
        (((left_dim,), (right_dim,)), ((), ())),
        preferred_element_type=F32,
    )


def unit_rows(values):
    centred = values - jnp.mean(values, axis=-1, keepdims=True)
    spread = jnp.mean(centred * centred, axis=-1, keepdims=True)
    inverse = lax.rsqrt(spread + NORM_EPS)
    return centred * inverse, inverse


def call(kernel, operands, out_shape, flops, moved, place=(), scratch=()):
    here = pl.BlockSpec(memory_space=pltpu.VMEM)
    small = pl.BlockSpec(memory_space=pltpu.SMEM)
    return pl.pallas_call(
        kernel,
        out_shape=out_shape,
        in_specs=[small] * len(place) + [here] * len(operands),
        out_specs=jax.tree.map(lambda _: here, out_shape),
        scratch_shapes=scratch,
        compiler_params=pltpu.CompilerParams(vmem_limit_bytes=VMEM_LIMIT),
        cost_estimate=pl.CostEstimate(flops=flops, bytes_accessed=moved, transcendentals=0),
    )(*place, *operands)


def sds(shape, dtype):
    return jax.ShapeDtypeStruct(shape, dtype)


def gain_shape(size):
    count = 8 * D // size
    width = math.gcd(count, LANES)
    return count // width, width


def gain_places(size):
    tall, across = gain_shape(size)
    for owner in range(size):
        for row in range(tall):
            flat = (owner * tall + row) * across
            yield owner, row, flat // D, flat % D, across


def pack_kernel(size, place, wide, down, gains, first, rest):
    half = first.shape[0]
    same = place[0] == 0
    picked = jnp.where(same, wide[:half], wide[half:]).astype(BF)
    first[:, :QKV] = picked[:, :QKV]
    rest[:, :REST] = picked[:, QKV:]
    for part in range(4):
        row, other = half * part, half * (4 + part)
        piece = jnp.where(same, down[row : row + half], down[other : other + half])
        rest[:, REST + D * part : REST + D * (part + 1)] = piece.astype(BF)
    first[:, QKV:] = jnp.zeros((half, LANES), BF)
    tall, across = gain_shape(size)
    first[:tall, QKV : QKV + across] = jnp.where(same, gains[...], 0.0).astype(BF)


def pack(place, wide, down, gains, size):
    half = wide.shape[0] // 2
    return call(
        functools.partial(pack_kernel, size),
        (wide, down, gains.reshape(gain_shape(size))),
        (sds((half, QKV + LANES), BF), sds((half, REST + 4 * D), BF)),
        1000,
        4 * (wide.size + down.size),
        place=(place,),
    )


def start_kernel(size, place, own, mine, other, queries_t, own_unit, weights_t, gains, joined):
    core, position = place[0], place[1]
    half = mine.shape[1]
    for owner in range(size):
        slot = owner ^ position
        near, far = mine[slot], other[slot]
        row = 2 * owner * half
        joined[row : row + half] = jnp.where(core == 0, near, far)
        joined[row + half : row + 2 * half] = jnp.where(core == 0, far, near)
    for owner, row, vector, lane, across in gain_places(size):
        at = 2 * owner * half + row
        gains[vector : vector + 1, lane : lane + across] = joined[
            at : at + 1, QKV : QKV + across
        ].astype(F32)
    weights_t[...] = joined[:, :QKV].T
    hat, _ = unit_rows(own[...].astype(F32))
    own_unit[...] = hat.astype(BF)
    normed = (hat * gains[0:1] + gains[1:2]).astype(BF)
    found = dot(weights_t[:D], normed, 1, 1)
    queries_t[...] = (found * (SCALE / LOG_TWO)).astype(BF)


def start(place, own, mine, other, size):
    rows = own.shape[0]
    return call(
        functools.partial(start_kernel, size),
        (own, mine, other),
        (sds((D, rows), BF), sds((rows, D), BF), sds((QKV, D), BF), sds((8, D), F32)),
        2 * rows * D * D,
        rows * D * 8,
        place=(place,),
        scratch=[pltpu.VMEM((D, QKV + LANES), BF)],
    )


def heads_in_step(first, second, third):
    ahead, behind = first(0), None
    for h in range(HEADS):
        found = ahead
        if h + 1 < HEADS:
            ahead = first(h + 1)
        found = second(h, found)
        if behind is not None:
            third(h - 1, behind)
        behind = found
    third(HEADS - 1, behind)


def head_rows(h, offset=0, height=HEAD):
    return slice(offset + height * h, offset + height * (h + 1))


def over_blocks(count, visit):
    if count == 1:
        visit(0)
    else:
        lax.fori_loop(0, count, lambda block, carry: (visit(block), carry)[1], 0)


def attend_kernel(count, carried, *refs):
    queries_t, weights_t, gains = refs[:3]
    blocks = refs[3 : 3 + count]
    refs = refs[3 + count :]
    if carried:
        accum_in, top_in = refs[:2]
        refs = refs[2:]
    probs, keys_t, values_t, unit, tops, accum, top, joined = refs
    if carried:
        accum[...] = accum_in[...]
        top[...] = top_in[...]
    else:
        accum[...] = jnp.zeros_like(accum)
        top[...] = jnp.full_like(top, -1e30)
    for block in range(count):
        joined[block] = blocks[block][...]

    def visit(block):
        hat, _ = unit_rows(joined[block].astype(F32))
        unit[block] = hat.astype(BF)
        crossed = (hat * gains[2:3] + gains[3:4]).astype(BF)
        keys_t[block] = dot(weights_t[D : 2 * D], crossed, 1, 1).astype(BF)
        values_t[block] = dot(weights_t[2 * D :], crossed, 1, 1).astype(BF)
        ones = jnp.ones((16, crossed.shape[0]), BF)

        def score(h):
            return dot(keys_t[block, head_rows(h)], queries_t[head_rows(h)], 0, 0)

        def soften(h, scores):
            before = top[h : h + 1]
            newest = jnp.maximum(before, jnp.max(scores, axis=0, keepdims=True))
            top[h : h + 1] = newest
            weight = jnp.exp2(scores - newest).astype(BF)
            probs[block, h] = weight
            return weight, jnp.exp2(before - newest)

        def gather(h, found):
            weight, fade = found
            tall = head_rows(h, 0, 64)
            values = jnp.concatenate([values_t[block, head_rows(h)], ones], axis=0)
            accum[tall] = accum[tall] * fade + dot(values, weight)

        heads_in_step(score, soften, gather)
        tops[block] = top[...]

    over_blocks(count, visit)


def attend(blocks, queries_t, weights_t, gains, carry):
    count, rows = len(blocks), blocks[0].shape[0]
    tokens = queries_t.shape[1]
    return call(
        functools.partial(attend_kernel, count, carry is not None),
        (queries_t, weights_t, gains, *blocks, *(carry or ())),
        (
            sds((count, HEADS, rows, tokens), BF),
            sds((count, D, rows), BF),
            sds((count, D, rows), BF),
            sds((count, rows, D), BF),
            sds((count, HEADS, tokens), F32),
            sds((64 * HEADS, tokens), F32),
            sds((HEADS, tokens), F32),
        ),
        count * (4 * rows * tokens * D * 5 + 4 * rows * D * D),
        count * (HEADS * rows * tokens * 2),
        scratch=[pltpu.VMEM((count, rows, D), BF)],
    )


def unpack_kernel(size, place, *refs):
    pieces, (rest, down) = refs[: 2 * size], refs[2 * size : 2 * size + 2]
    joined = refs[2 * size + 2]
    core, position = place[0], place[1]
    half = joined.shape[1]
    for side in range(2):
        for other in range(size):
            slot = 2 * (other ^ position) + (side ^ core)
            joined[slot] = pieces[side * size + other][...]
    for owner in range(size):
        for side in range(2):
            slot = 2 * owner + side
            rest[slot * half : (slot + 1) * half] = joined[slot, :, :REST]
            for part in range(4):
                row = (4 * slot + part) * half
                down[row : row + half] = joined[
                    slot, :, REST + D * part : REST + D * (part + 1)
                ]


def unpack(place, pieces, size):
    half, across = pieces[0].shape
    return call(
        functools.partial(unpack_kernel, size),
        tuple(pieces),
        (sds((D, REST), BF), sds((FF, D), BF)),
        1000,
        4 * D * across,
        place=(place,),
        scratch=[pltpu.VMEM((2 * size, half, across), BF)],
    )


def dense_kernel(inputs, accum, rest, down, gains, estimate, attended_t, inverse_total,
                 branch_out, third, third_inverse, normed_two, slope, hidden, ffn_out,
                 out_rows):
    for h in range(HEADS):
        inverse = 1.0 / accum[64 * h + HEAD : 64 * h + HEAD + 1]
        inverse_total[h : h + 1] = inverse
        attended_t[HEAD * h : HEAD * (h + 1)] = accum[64 * h : 64 * h + HEAD] * inverse
    branch = dot(attended_t[...].astype(BF), rest[:, :D], 0, 0)
    branch_out[...] = branch
    mid = inputs[...].astype(F32) + gains[6:7] * branch
    hat, inverse = unit_rows(mid)
    third[...] = hat
    third_inverse[...] = inverse
    normed = (hat * gains[4:5] + gains[5:6]).astype(BF)
    normed_two[...] = normed
    pre = dot(normed, rest[:, D : D + FF])
    gate = 0.5 * (1.0 + lax.erf(pre * math.sqrt(0.5)))
    hid = (pre * gate).astype(BF)
    hidden[...] = hid
    bell = jnp.exp(-0.5 * pre * pre) * (1.0 / math.sqrt(2.0 * math.pi))
    slope[...] = gate + pre * bell
    ffn = dot(hid, down[...])
    ffn_out[...] = ffn
    out = (mid + gains[7:8] * ffn).astype(BF)
    out_rows[...] = out
    estimate[...] = dot(out, rest[:, D + FF :]).astype(BF)


def dense_forward(inputs, accum, rest, down, gains):
    rows = inputs.shape[0]
    return call(
        dense_kernel,
        (inputs, accum, rest, down, gains),
        (
            sds((rows, OUT), BF),
            sds((D, rows), F32),
            sds((HEADS, rows), F32),
            sds((rows, D), F32),
            sds((rows, D), F32),
            sds((rows, 1), F32),
            sds((rows, D), BF),
            sds((rows, FF), F32),
            sds((rows, FF), BF),
            sds((rows, D), F32),
            sds((rows, D), BF),
        ),
        2 * rows * D * (D + 2 * FF + OUT),
        rows * FF * 8,
    )


def error_kernel(place, own, far, targets, errors, energy):
    rows = own.shape[0]
    wanted = targets[pl.ds(pl.multiple_of(place[1] * rows, 8), rows)]
    error = wanted - (own[...].astype(F32) + far[...].astype(F32))
    errors[...] = error
    row = lax.broadcasted_iota(jnp.int32, (8, OUT), 0)
    found = jnp.sum(error * error, axis=0, keepdims=True)
    clean = jnp.sum(wanted * wanted, axis=0, keepdims=True)
    energy[...] = jnp.where(row == 0, found, jnp.where(row == 1, clean, 0.0))


def error_energy(place, own, far, targets):
    rows = own.shape[0]
    return call(
        error_kernel,
        (own, far, targets),
        (sds((rows, OUT), F32), sds((8, OUT), F32)),
        rows * OUT * 8,
        rows * OUT * 12,
        place=(place,),
    )


def stem_sums(values):
    stem = lax.broadcasted_iota(jnp.int32, values.shape, 1) // SAMPLES
    total = jnp.zeros_like(values)
    for k in range(STEMS):
        part = jnp.sum(jnp.where(stem == k, values, 0.0), axis=1, keepdims=True)
        total = jnp.where(stem == k, part, total)
    return total


def dense_back_kernel(segments, present, energy, errors, rest, down, gains, attended_t, branch_out,
                      third, third_inverse, slope, ffn_out, grad_est, grad_ffn, grad_pre,
                      grad_branch, grad_attended_t, delta, grad_gains, loss):
    lane = lax.broadcasted_iota(jnp.int32, (1, OUT), 1)
    counted = jnp.zeros((1, OUT), F32)
    for k in range(STEMS):
        counted = jnp.where(lane // SAMPLES == k, present[0, k].astype(F32), counted)
    counted = counted * (10.0 / math.log(10.0) / (segments * STEMS))
    found = stem_sums(energy[0:1]) + ENERGY_EPS
    clean = stem_sums(energy[1:2]) + ENERGY_EPS
    terms = counted * (jnp.log(found) - jnp.log(clean))
    terms = jnp.where(lane % SAMPLES == 0, terms, 0.0)
    loss[...] = jnp.broadcast_to(jnp.sum(terms, axis=1, keepdims=True), loss.shape)
    low = (errors[...] * (-2.0 * counted / found)).astype(BF)
    grad_est[...] = low
    grad_out = dot(low, rest[:, D + FF :], 1, 1)
    grad_gains[3:4] = jnp.sum(grad_out * ffn_out[...], axis=0, keepdims=True)
    ffn = (grad_out * gains[7:8]).astype(BF)
    grad_ffn[...] = ffn
    hidden = dot(ffn, down[...], 1, 1).astype(BF)
    pre = (hidden.astype(F32) * slope[...]).astype(BF)
    grad_pre[...] = pre
    normed = dot(pre, rest[:, D : D + FF], 1, 1)
    hat = third[...]
    grad_gains[0:1] = jnp.sum(normed * hat, axis=0, keepdims=True)
    grad_gains[1:2] = jnp.sum(normed, axis=0, keepdims=True)
    scaled = normed * gains[4:5]
    grad_mid = grad_out + third_inverse[...] * (
        scaled
        - jnp.mean(scaled, axis=-1, keepdims=True)
        - hat * jnp.mean(scaled * hat, axis=-1, keepdims=True)
    )
    grad_gains[2:3] = jnp.sum(grad_mid * branch_out[...], axis=0, keepdims=True)
    branch = (grad_mid * gains[6:7]).astype(BF)
    grad_branch[...] = branch
    attended = dot(rest[:, :D], branch, 1, 1).astype(BF)
    grad_attended_t[...] = attended
    product = attended.astype(F32) * attended_t[...]
    for h in range(HEADS):
        delta[h : h + 1] = jnp.sum(product[head_rows(h)], axis=0, keepdims=True)


def dense_back(segments, present, energy, errors, rest, down, gains, attended_t, branch_out, third,
               third_inverse, slope, ffn_out):
    rows = errors.shape[0]
    return call(
        functools.partial(dense_back_kernel, segments),
        (energy, errors, rest, down, gains, attended_t, branch_out, third,
         third_inverse, slope, ffn_out),
        (
            sds((rows, OUT), BF),
            sds((rows, D), BF),
            sds((rows, FF), BF),
            sds((rows, D), BF),
            sds((D, rows), BF),
            sds((HEADS, rows), F32),
            sds((4, D), F32),
            sds((8, LANES), F32),
        ),
        2 * rows * D * (D + 2 * FF + OUT),
        rows * FF * 8,
        place=(present,),
    )


def deal(size, place, first, second, keep, send, owner, at):
    slot = owner ^ place[1]
    same = place[0] == 0
    keep[slot, :, at] = jnp.where(same, first, second).astype(BF)
    send[slot, :, at] = jnp.where(same, second, first).astype(BF)


def dense_weights_kernel(size, place, grad_est, grad_ffn, grad_pre, grad_branch, attended_t,
                         normed_two, hidden, out_rows, keep, send, wide, tall):
    half = keep.shape[1]
    wide[:, D + FF :] = dot(out_rows[...], grad_est[...], 0, 0)
    wide[:, D : D + FF] = dot(normed_two[...], grad_pre[...], 0, 0)
    wide[:, :D] = dot(attended_t[...].astype(BF), grad_branch[...])
    tall[...] = dot(hidden[...], grad_ffn[...], 0, 0)
    for owner in range(size):
        row = 2 * owner * half
        deal(
            size, place, wide[row : row + half], wide[row + half : row + 2 * half],
            keep, send, owner, slice(0, REST),
        )
        for part in range(4):
            first = (8 * owner + part) * half
            second = (8 * owner + 4 + part) * half
            deal(
                size, place, tall[first : first + half], tall[second : second + half],
                keep, send, owner, slice(REST + D * part, REST + D * (part + 1)),
            )


def dense_weights(place, grad_est, grad_ffn, grad_pre, grad_branch, attended_t, normed_two,
                  hidden, out_rows, size):
    rows = grad_est.shape[0]
    piece = (size, D // size // 2, REST + 4 * D)
    return call(
        functools.partial(dense_weights_kernel, size),
        (grad_est, grad_ffn, grad_pre, grad_branch, attended_t, normed_two, hidden, out_rows),
        (sds(piece, BF), sds(piece, BF)),
        2 * rows * D * (D + 2 * FF + OUT),
        rows * FF * 8,
        place=(place,),
        scratch=[pltpu.VMEM((D, REST), F32), pltpu.VMEM((FF, D), F32)],
    )


def attend_back_kernel(carried, probs, keys_t, values_t, tops, queries_t, delta, top,
                       inverse_total, grad_attended_t, *refs):
    if carried:
        refs[1][...] = refs[0][...]
    else:
        refs[0][...] = jnp.zeros_like(refs[0])
    grad_queries, grad_kv = refs[-2:]

    def visit(block):
        factor = jnp.exp2(tops[block] - top[...]) * inverse_total[...]
        shift = delta[...] * factor

        def begin(h):
            grad = grad_attended_t[head_rows(h)].astype(F32) * factor[h : h + 1]
            grad = grad.astype(BF)
            return grad, dot(values_t[block, head_rows(h)], grad, 0, 0)

        def turn(h, found):
            grad, grad_probs = found
            scores = probs[block, h].astype(F32) * (grad_probs - shift[h : h + 1])
            return grad, scores.astype(BF)

        def end(h, found):
            grad, scores = found
            at = head_rows(h)
            grad_queries[at] += dot(keys_t[block, at], scores)
            grad_kv[block, at] = (dot(queries_t[at], scores, 1, 1) * LOG_TWO).astype(BF)
            grad_kv[block, head_rows(h, D)] = dot(grad, probs[block, h], 1, 1).astype(BF)

        heads_in_step(begin, turn, end)

    over_blocks(probs.shape[0], visit)


def attend_back(saved, queries_t, delta, top, inverse_total, grad_attended_t, carry):
    probs, keys_t, values_t, tops = saved
    count, _, rows, tokens = probs.shape
    carry = () if carry is None else (carry,)
    return call(
        functools.partial(attend_back_kernel, len(carry)),
        (probs, keys_t, values_t, tops, queries_t, delta, top, inverse_total,
         grad_attended_t, *carry),
        (sds((D, tokens), F32), sds((count, 2 * D, rows), BF)),
        count * (8 * rows * tokens * D * 5),
        count * (HEADS * rows * tokens * 2),
    )


def finish_kernel(size, groups, place, grad_queries, own_unit, weights_t, gains, late,
                  *refs):
    grads, units = refs[:groups], refs[groups : 2 * groups]
    keep, send, moments, full, grad_gains = refs[2 * groups :]
    rows = own_unit.shape[0]
    ones = jnp.ones((rows, LANES), BF)
    query = (grad_queries[...] * SCALE).astype(BF)
    moments[:D] = dot(query, jnp.concatenate([own_unit[...], ones], axis=1))
    total = None
    for grad, unit in zip(grads, units):
        for block in range(grad.shape[0]):
            term = dot(grad[block], jnp.concatenate([unit[block], ones], axis=1))
            total = term if total is None else total + term
    moments[D:] = total
    for first, size_out, row in ((0, D, 0), (D, 2 * D, 2)):
        at = slice(first, first + size_out)
        moment = moments[at, :D]
        column = moments[at, D : D + 1]
        weight = weights_t[at].astype(F32)
        grad_gains[row : row + 1] = jnp.sum(weight * moment, axis=0, keepdims=True)
        grad_gains[row + 1 : row + 2] = jnp.sum(weight * column, axis=0, keepdims=True)
        product = moment * gains[row : row + 1] + column * gains[row + 1 : row + 2]
        full[:, at] = product.T
    grad_gains[4:8] = late[...]
    half = keep.shape[1]
    for owner in range(size):
        row = 2 * owner * half
        deal(
            size, place, full[row : row + half], full[row + half : row + 2 * half],
            keep, send, owner, slice(0, QKV),
        )
        slot = owner ^ place[1]
        keep[slot, :, QKV:] = jnp.zeros((half, LANES), BF)
        send[slot, :, QKV:] = jnp.zeros((half, LANES), BF)
    same = place[0] == 0
    for owner, row, vector, lane, across in gain_places(size):
        slot = owner ^ place[1]
        value = grad_gains[vector : vector + 1, lane : lane + across]
        at = slice(QKV, QKV + across)
        keep[slot, row : row + 1, at] = jnp.where(same, value, 0.0).astype(BF)
        send[slot, row : row + 1, at] = jnp.where(same, 0.0, value).astype(BF)


def finish(place, grad_queries, own_unit, weights_t, gains, late, grads, units, size):
    rows = own_unit.shape[0]
    piece = (size, D // size // 2, QKV + LANES)
    return call(
        functools.partial(finish_kernel, size, len(grads)),
        (grad_queries, own_unit, weights_t, gains, late, *grads, *units),
        (sds(piece, BF), sds(piece, BF)),
        2 * rows * D * QKV * size,
        rows * D * 2 * size,
        place=(place,),
        scratch=[
            pltpu.VMEM((QKV, D + LANES), F32),
            pltpu.VMEM((D, QKV), F32),
            pltpu.VMEM((8, D), F32),
        ],
    )


def square_kernel(*refs):
    total = jnp.zeros((1, 1), F32)
    for ref in refs[:-1]:
        values = ref[...].astype(F32)
        rows = jnp.sum(values * values, axis=0, keepdims=True)
        total = total + jnp.sum(rows, axis=1, keepdims=True)
    refs[-1][...] = jnp.broadcast_to(total, refs[-1].shape)


def square_sum(*parts):
    size = sum(x.size for x in parts)
    return call(square_kernel, parts, sds((8, LANES), F32), 2 * size, 2 * size)


def bits(size):
    return [1 << k for k in range(size.bit_length() - 1)]


def masks(size):
    return sorted(range(1, size), key=lambda mask: (mask.bit_count(), mask))


def tie(*values):
    return lax.optimization_barrier(values)


def add_low(left, right):
    return (left.astype(F32) + right.astype(F32)).astype(BF)


def core_step(keep, send):
    return add_low(keep, swap(send, "seg", 1))


def scatter_step(total, size):
    received = [swap(total[mask], "wide", mask) for mask in range(1, size)]
    return functools.reduce(jnp.add, [x.astype(F32) for x in [total[0]] + received]).astype(BF)


def segment_step(total):
    for mask in bits(lax.axis_size("seg"))[1:]:
        total = add_low(total, swap(total, "seg", mask))
    return total


def adam_update(weight, grad, moment, second, rate):
    moment = BETA_ONE * moment + (1 - BETA_ONE) * grad
    second = BETA_TWO * second + (1 - BETA_TWO) * grad * grad
    fixed_one = moment / (1 - BETA_ONE**ADAM_STEP)
    fixed_two = second / (1 - BETA_TWO**ADAM_STEP)
    weight = weight - rate * (fixed_one / (jnp.sqrt(fixed_two) + ADAM_EPS) + WEIGHT_DECAY * weight)
    return (weight, moment, second)


def adam_kernel(size, place, squares, early, early_other, late, late_other, *refs):
    masters, firsts, seconds = refs[0:3], refs[3:6], refs[6:9]
    news, new_firsts, new_seconds = refs[9:12], refs[12:15], refs[15:18]
    copies, norm = refs[18:21], refs[21]
    half = early.shape[0]
    same = place[0] == 0
    grad_norm = jnp.sqrt(squares[0:1, 0:1])
    norm[...] = jnp.broadcast_to(grad_norm, norm.shape)
    factor = jnp.minimum(1.0, CLIP_LIMIT / (grad_norm + 1e-06))

    def update(index, rows, lanes, grad, rate):
        at = (rows, lanes)
        found = adam_update(
            masters[index][at], grad * factor, firsts[index][at], seconds[index][at], rate
        )
        news[index][at], new_firsts[index][at], new_seconds[index][at] = found
        copies[index][at] = found[0].astype(BF)

    for side in range(2):
        use_own = same if side == 0 else jnp.logical_not(same)

        def pick(own, other, lanes):
            return jnp.where(use_own, own[:, lanes], other[:, lanes]).astype(F32)

        rows = slice(side * half, (side + 1) * half)
        update(0, rows, slice(0, QKV), pick(late, late_other, slice(0, QKV)), LEARN_RATE)
        update(0, rows, slice(QKV, QKV + REST), pick(early, early_other, slice(0, REST)),
               LEARN_RATE)
        for part in range(4):
            first = (4 * side + part) * half
            lanes = slice(REST + D * part, REST + D * (part + 1))
            update(1, slice(first, first + half), slice(0, D),
                   pick(early, early_other, lanes), LEARN_RATE)
    tall, across = gain_shape(size)
    lanes = slice(QKV, QKV + across)
    grad = jnp.where(same, late[:tall, lanes], late_other[:tall, lanes]).astype(F32)
    update(2, slice(0, tall), slice(0, across), grad, GAIN_RATE)


def adam(place, squares, grads, states, size):
    flat = gain_shape(size)
    states = [x.reshape(flat) if x.ndim == 1 else x for x in states]
    shapes = [x.shape for x in states[:3]]
    count = sum(x.size for x in states[:3])
    return call(
        functools.partial(adam_kernel, size),
        (squares, *grads, *states),
        tuple(sds(x, F32) for x in shapes) * 3
        + tuple(sds(x, BF) for x in shapes)
        + (sds((8, LANES), F32),),
        20 * count,
        28 * count,
        place=(place,),
    )


def adam_update(weight, grad, moment, second, rate):
    moment = BETA_ONE * moment + (1 - BETA_ONE) * grad
    second = BETA_TWO * second + (1 - BETA_TWO) * grad * grad
    fixed_one = moment / (1 - BETA_ONE**ADAM_STEP)
    fixed_two = second / (1 - BETA_TWO**ADAM_STEP)
    weight = weight - rate * (fixed_one / (jnp.sqrt(fixed_two) + ADAM_EPS) + WEIGHT_DECAY * weight)
    return (weight, moment, second)


def body(
    encoded,
    targets,
    present,
    wide_master,
    down_master,
    gain_master,
    wide_first,
    down_first,
    gain_first,
    wide_second,
    down_second,
    gain_second,
):
    size = lax.axis_size("wide") // 2
    position = lax.axis_index("wide") % size
    core = lax.axis_index("seg") % 2
    place = jnp.stack([core, position]).astype(jnp.int32)
    own = encoded[0]
    far = {0: swap(own, "wide", size)}
    first, rest = pack(place, wide_master, down_master, gain_master, size)

    first_mine = jnp.stack([first] + [swap(first, "wide", mask) for mask in range(1, size)])
    first_other = swap(first_mine, "seg", 1)
    queries_t, own_unit, weights_t, gains = start(place, own, first_mine, first_other, size)

    far[0], rest = tie(far[0], rest)
    order = [0] + masks(size)
    for mask in order[1:]:
        far[mask] = swap(far[0], "wide", mask)
    groups = [order[:1]] + [order[k : k + 2] for k in range(1, size, 2)]

    rest_mine = [rest] + [swap(rest, "wide", mask) for mask in range(1, size)]
    rest_other = [swap(x, "seg", 1) for x in rest_mine]

    carry = None
    saved, units = [], []
    for group in groups:
        probs, keys_t, values_t, unit, tops, *carry = attend(
            [far[mask] for mask in group], queries_t, weights_t, gains, carry
        )
        saved.append((probs, keys_t, values_t, tops))
        units.append(unit)
    accum, top = carry

    rest_all, down_all = unpack(place, rest_mine + rest_other, size)
    (est_own, attended_t, inverse_total, branch_out, third, third_inverse, normed_two, slope,
     hidden, ffn_out, out_rows) = dense_forward(own, accum, rest_all, down_all, gains)

    errors, energy = error_energy(place, est_own, swap(est_own, "wide", size), targets[0])
    for mask in bits(size):
        energy = energy + swap(energy, "wide", mask)
    seg_count = lax.axis_size("seg")
    (grad_est, grad_ffn, grad_pre, grad_branch, grad_attended_t, delta, late_gains,
     loss) = dense_back(
        seg_count, present, energy, errors, rest_all, down_all, gains, attended_t, branch_out,
        third, third_inverse, slope, ffn_out,
    )
    keep, send = dense_weights(
        place, grad_est, grad_ffn, grad_pre, grad_branch, attended_t, normed_two, hidden,
        out_rows, size,
    )
    grad_attended_t, keep, send = tie(grad_attended_t, keep, send)

    early = core_step(keep, send)
    grad_queries, grads = None, []
    for k, item in enumerate(saved):
        grad_queries, grad_kv = attend_back(
            item, queries_t, delta, top, inverse_total, grad_attended_t, grad_queries
        )
        grads.append(grad_kv)
        if k == 0:
            grad_queries, early = tie(grad_queries, early)
            early = scatter_step(early, size)
    grad_queries, early = tie(grad_queries, early)
    early = segment_step(early)
    keep, send = finish(
        place, grad_queries, own_unit, weights_t, gains, late_gains, grads, units, size
    )
    keep, send, early = tie(keep, send, early)
    early_other = swap(early, "seg", 1)
    late = core_step(keep, send)
    late, loss = tie(late, loss)
    for mask in bits(seg_count):
        loss = loss + swap(loss, "seg", mask)
    late = scatter_step(late, size)
    late, loss = tie(late, loss)
    late = segment_step(late)
    late_other = swap(late, "seg", 1)

    squares = square_sum(early, early_other, late, late_other)
    for mask in bits(2 * size):
        squares = squares + swap(squares, "wide", mask)
    *updated, grad_norm = adam(
        place,
        squares,
        (early, early_other, late, late_other),
        (wide_master, down_master, gain_master, wide_first, down_first, gain_first,
         wide_second, down_second, gain_second),
        size,
    )
    return (
        loss[0, 0],
        grad_norm[0, 0],
        *(x.reshape(-1) if k % 3 == 2 else x for k, x in enumerate(updated)),
    )


def solution(mesh):
    split, line = P("wide", None), P("wide")
    states = (split, split, line)
    return jax.shard_map(
        body,
        mesh=mesh,
        in_specs=(P("seg", "wide", None), P("seg", None, None), P("seg", None)) + states * 3,
        out_specs=(P(), P()) + states * 4,
        check_vma=False,
    )
```

```python
import functools
import math

import jax
import jax.numpy as jnp
from jax import lax
from jax.experimental import pallas as pl
from jax.experimental.pallas import tpu as pltpu
from jax.sharding import PartitionSpec as P

D = 384
HEADS = 8
HEAD = D // HEADS
FF = 1536
STEMS = 4
SAMPLES = 32
OUT = STEMS * SAMPLES
QKV = 3 * D
REST = D + FF + OUT
ADAM_STEP = 10
LANES = 128

NORM_EPS = 1e-05
ENERGY_EPS = 1e-05
BETA_ONE = 0.9
BETA_TWO = 0.999
ADAM_EPS = 1e-08
LEARN_RATE = 0.1
GAIN_RATE = 0.5
WEIGHT_DECAY = 0.01
CLIP_LIMIT = 0.001

BF = jnp.bfloat16
F32 = jnp.float32
SCALE = 1.0 / math.sqrt(HEAD)
LOG_TWO = math.log(2.0)
VMEM_LIMIT = 14 * 2**20


def swap(x, axis, mask):
    return lax.ppermute(x, axis, [(i, i ^ mask) for i in range(lax.axis_size(axis))])


def dot(left, right, left_dim=1, right_dim=0):
    return lax.dot_general(
        left,
        right,
        (((left_dim,), (right_dim,)), ((), ())),
        preferred_element_type=F32,
    )


def unit_rows(values):
    centred = values - jnp.mean(values, axis=-1, keepdims=True)
    spread = jnp.mean(centred * centred, axis=-1, keepdims=True)
    inverse = lax.rsqrt(spread + NORM_EPS)
    return centred * inverse, inverse


def call(kernel, operands, out_shape, flops, moved, place=(), scratch=()):
    here = pl.BlockSpec(memory_space=pltpu.VMEM)
    small = pl.BlockSpec(memory_space=pltpu.SMEM)
    return pl.pallas_call(
        kernel,
        out_shape=out_shape,
        in_specs=[small] * len(place) + [here] * len(operands),
        out_specs=jax.tree.map(lambda _: here, out_shape),
        scratch_shapes=scratch,
        compiler_params=pltpu.CompilerParams(vmem_limit_bytes=VMEM_LIMIT),
        cost_estimate=pl.CostEstimate(flops=flops, bytes_accessed=moved, transcendentals=0),
    )(*place, *operands)


def sds(shape, dtype):
    return jax.ShapeDtypeStruct(shape, dtype)


def gain_shape(size):
    count = 8 * D // size
    width = math.gcd(count, LANES)
    return count // width, width


def gain_places(size):
    tall, across = gain_shape(size)
    for owner in range(size):
        for row in range(tall):
            flat = (owner * tall + row) * across
            yield owner, row, flat // D, flat % D, across


def pack_kernel(size, place, wide, down, gains, first, rest):
    half = first.shape[0]
    same = place[0] == 0
    picked = jnp.where(same, wide[:half], wide[half:]).astype(BF)
    first[:, :QKV] = picked[:, :QKV]
    rest[:, :REST] = picked[:, QKV:]
    for part in range(4):
        row, other = half * part, half * (4 + part)
        piece = jnp.where(same, down[row : row + half], down[other : other + half])
        rest[:, REST + D * part : REST + D * (part + 1)] = piece.astype(BF)
    first[:, QKV:] = jnp.zeros((half, LANES), BF)
    tall, across = gain_shape(size)
    first[:tall, QKV : QKV + across] = jnp.where(same, gains[...], 0.0).astype(BF)


def pack(place, wide, down, gains, size):
    half = wide.shape[0] // 2
    return call(
        functools.partial(pack_kernel, size),
        (wide, down, gains.reshape(gain_shape(size))),
        (sds((half, QKV + LANES), BF), sds((half, REST + 4 * D), BF)),
        1000,
        4 * (wide.size + down.size),
        place=(place,),
    )


def start_kernel(size, place, own, mine, other, queries_t, own_unit, weights_t, gains, joined):
    core, position = place[0], place[1]
    half = mine.shape[1]
    for owner in range(size):
        slot = owner ^ position
        near, far = mine[slot], other[slot]
        row = 2 * owner * half
        joined[row : row + half] = jnp.where(core == 0, near, far)
        joined[row + half : row + 2 * half] = jnp.where(core == 0, far, near)
    for owner, row, vector, lane, across in gain_places(size):
        at = 2 * owner * half + row
        gains[vector : vector + 1, lane : lane + across] = joined[
            at : at + 1, QKV : QKV + across
        ].astype(F32)
    weights_t[...] = joined[:, :QKV].T
    hat, _ = unit_rows(own[...].astype(F32))
    own_unit[...] = hat.astype(BF)
    normed = (hat * gains[0:1] + gains[1:2]).astype(BF)
    found = dot(weights_t[:D], normed, 1, 1)
    queries_t[...] = (found * (SCALE / LOG_TWO)).astype(BF)


def start(place, own, mine, other, size):
    rows = own.shape[0]
    return call(
        functools.partial(start_kernel, size),
        (own, mine, other),
        (sds((D, rows), BF), sds((rows, D), BF), sds((QKV, D), BF), sds((8, D), F32)),
        2 * rows * D * D,
        rows * D * 8,
        place=(place,),
        scratch=[pltpu.VMEM((D, QKV + LANES), BF)],
    )


def heads_in_step(first, second, third):
    ahead, behind = first(0), None
    for h in range(HEADS):
        found = ahead
        if h + 1 < HEADS:
            ahead = first(h + 1)
        found = second(h, found)
        if behind is not None:
            third(h - 1, behind)
        behind = found
    third(HEADS - 1, behind)


def head_rows(h, offset=0, height=HEAD):
    return slice(offset + height * h, offset + height * (h + 1))


def over_blocks(count, visit):
    if count == 1:
        visit(0)
    else:
        lax.fori_loop(0, count, lambda block, carry: (visit(block), carry)[1], 0)


def attend_kernel(count, carried, *refs):
    queries_t, weights_t, gains = refs[:3]
    blocks = refs[3 : 3 + count]
    refs = refs[3 + count :]
    if carried:
        accum_in, top_in = refs[:2]
        refs = refs[2:]
    probs, keys_t, values_t, unit, tops, accum, top, joined = refs
    if carried:
        accum[...] = accum_in[...]
        top[...] = top_in[...]
    else:
        accum[...] = jnp.zeros_like(accum)
        top[...] = jnp.full_like(top, -1e30)
    for block in range(count):
        joined[block] = blocks[block][...]

    def visit(block):
        hat, _ = unit_rows(joined[block].astype(F32))
        unit[block] = hat.astype(BF)
        crossed = (hat * gains[2:3] + gains[3:4]).astype(BF)
        keys_t[block] = dot(weights_t[D : 2 * D], crossed, 1, 1).astype(BF)
        values_t[block] = dot(weights_t[2 * D :], crossed, 1, 1).astype(BF)
        ones = jnp.ones((16, crossed.shape[0]), BF)

        def score(h):
            return dot(keys_t[block, head_rows(h)], queries_t[head_rows(h)], 0, 0)

        def soften(h, scores):
            before = top[h : h + 1]
            newest = jnp.maximum(before, jnp.max(scores, axis=0, keepdims=True))
            top[h : h + 1] = newest
            weight = jnp.exp2(scores - newest).astype(BF)
            probs[block, h] = weight
            return weight, jnp.exp2(before - newest)

        def gather(h, found):
            weight, fade = found
            tall = head_rows(h, 0, 64)
            values = jnp.concatenate([values_t[block, head_rows(h)], ones], axis=0)
            accum[tall] = accum[tall] * fade + dot(values, weight)

        heads_in_step(score, soften, gather)
        tops[block] = top[...]

    over_blocks(count, visit)


def attend(blocks, queries_t, weights_t, gains, carry):
    count, rows = len(blocks), blocks[0].shape[0]
    tokens = queries_t.shape[1]
    return call(
        functools.partial(attend_kernel, count, carry is not None),
        (queries_t, weights_t, gains, *blocks, *(carry or ())),
        (
            sds((count, HEADS, rows, tokens), BF),
            sds((count, D, rows), BF),
            sds((count, D, rows), BF),
            sds((count, rows, D), BF),
            sds((count, HEADS, tokens), F32),
            sds((64 * HEADS, tokens), F32),
            sds((HEADS, tokens), F32),
        ),
        count * (4 * rows * tokens * D * 5 + 4 * rows * D * D),
        count * (HEADS * rows * tokens * 2),
        scratch=[pltpu.VMEM((count, rows, D), BF)],
    )


def unpack_kernel(size, place, *refs):
    pieces, (rest, down) = refs[: 2 * size], refs[2 * size : 2 * size + 2]
    joined = refs[2 * size + 2]
    core, position = place[0], place[1]
    half = joined.shape[1]
    for side in range(2):
        for other in range(size):
            slot = 2 * (other ^ position) + (side ^ core)
            joined[slot] = pieces[side * size + other][...]
    for owner in range(size):
        for side in range(2):
            slot = 2 * owner + side
            rest[slot * half : (slot + 1) * half] = joined[slot, :, :REST]
            for part in range(4):
                row = (4 * slot + part) * half
                down[row : row + half] = joined[
                    slot, :, REST + D * part : REST + D * (part + 1)
                ]


def unpack(place, pieces, size):
    half, across = pieces[0].shape
    return call(
        functools.partial(unpack_kernel, size),
        tuple(pieces),
        (sds((D, REST), BF), sds((FF, D), BF)),
        1000,
        4 * D * across,
        place=(place,),
        scratch=[pltpu.VMEM((2 * size, half, across), BF)],
    )


def dense_kernel(inputs, accum, rest, down, gains, estimate, attended_t, inverse_total,
                 branch_out, third, third_inverse, normed_two, slope, hidden, ffn_out,
                 out_rows):
    for h in range(HEADS):
        inverse = 1.0 / accum[64 * h + HEAD : 64 * h + HEAD + 1]
        inverse_total[h : h + 1] = inverse
        attended_t[HEAD * h : HEAD * (h + 1)] = accum[64 * h : 64 * h + HEAD] * inverse
    branch = dot(attended_t[...].astype(BF), rest[:, :D], 0, 0)
    branch_out[...] = branch
    mid = inputs[...].astype(F32) + gains[6:7] * branch
    hat, inverse = unit_rows(mid)
    third[...] = hat
    third_inverse[...] = inverse
    normed = (hat * gains[4:5] + gains[5:6]).astype(BF)
    normed_two[...] = normed
    pre = dot(normed, rest[:, D : D + FF])
    gate = 0.5 * (1.0 + lax.erf(pre * math.sqrt(0.5)))
    hid = (pre * gate).astype(BF)
    hidden[...] = hid
    bell = jnp.exp(-0.5 * pre * pre) * (1.0 / math.sqrt(2.0 * math.pi))
    slope[...] = gate + pre * bell
    ffn = dot(hid, down[...])
    ffn_out[...] = ffn
    out = (mid + gains[7:8] * ffn).astype(BF)
    out_rows[...] = out
    estimate[...] = dot(out, rest[:, D + FF :]).astype(BF)


def dense_forward(inputs, accum, rest, down, gains):
    rows = inputs.shape[0]
    return call(
        dense_kernel,
        (inputs, accum, rest, down, gains),
        (
            sds((rows, OUT), BF),
            sds((D, rows), F32),
            sds((HEADS, rows), F32),
            sds((rows, D), F32),
            sds((rows, D), F32),
            sds((rows, 1), F32),
            sds((rows, D), BF),
            sds((rows, FF), F32),
            sds((rows, FF), BF),
            sds((rows, D), F32),
            sds((rows, D), BF),
        ),
        2 * rows * D * (D + 2 * FF + OUT),
        rows * FF * 8,
    )


def error_kernel(place, own, far, targets, errors, energy):
    rows = own.shape[0]
    wanted = targets[pl.ds(pl.multiple_of(place[1] * rows, 8), rows)]
    error = wanted - (own[...].astype(F32) + far[...].astype(F32))
    errors[...] = error
    row = lax.broadcasted_iota(jnp.int32, (8, OUT), 0)
    found = jnp.sum(error * error, axis=0, keepdims=True)
    clean = jnp.sum(wanted * wanted, axis=0, keepdims=True)
    energy[...] = jnp.where(row == 0, found, jnp.where(row == 1, clean, 0.0))


def error_energy(place, own, far, targets):
    rows = own.shape[0]
    return call(
        error_kernel,
        (own, far, targets),
        (sds((rows, OUT), F32), sds((8, OUT), F32)),
        rows * OUT * 8,
        rows * OUT * 12,
        place=(place,),
    )


def ordered_sum(place, values, joined):
    size = joined.shape[0]
    for slot in range(size):
        joined[slot ^ place[1]] = values[slot]
    total = joined[0]
    for slot in range(1, size):
        total = total + joined[slot]
    return total


def stem_sums(values):
    stem = lax.broadcasted_iota(jnp.int32, values.shape, 1) // SAMPLES
    total = jnp.zeros_like(values)
    for k in range(STEMS):
        part = jnp.sum(jnp.where(stem == k, values, 0.0), axis=1, keepdims=True)
        total = jnp.where(stem == k, part, total)
    return total


def dense_back_kernel(segments, place, present, energies, errors, rest, down, gains, attended_t, branch_out,
                      third, third_inverse, slope, ffn_out, grad_est, grad_ffn, grad_pre,
                      grad_branch, grad_attended_t, delta, grad_gains, loss, joined):
    energy = ordered_sum(place, energies, joined)
    lane = lax.broadcasted_iota(jnp.int32, (1, OUT), 1)
    counted = jnp.zeros((1, OUT), F32)
    for k in range(STEMS):
        counted = jnp.where(lane // SAMPLES == k, present[0, k].astype(F32), counted)
    counted = counted * (10.0 / math.log(10.0) / (segments * STEMS))
    found = stem_sums(energy[0:1]) + ENERGY_EPS
    clean = stem_sums(energy[1:2]) + ENERGY_EPS
    terms = counted * (jnp.log(found) - jnp.log(clean))
    terms = jnp.where(lane % SAMPLES == 0, terms, 0.0)
    loss[...] = jnp.broadcast_to(jnp.sum(terms, axis=1, keepdims=True), loss.shape)
    low = (errors[...] * (-2.0 * counted / found)).astype(BF)
    grad_est[...] = low
    grad_out = dot(low, rest[:, D + FF :], 1, 1)
    grad_gains[3:4] = jnp.sum(grad_out * ffn_out[...], axis=0, keepdims=True)
    ffn = (grad_out * gains[7:8]).astype(BF)
    grad_ffn[...] = ffn
    hidden = dot(ffn, down[...], 1, 1).astype(BF)
    pre = (hidden.astype(F32) * slope[...]).astype(BF)
    grad_pre[...] = pre
    normed = dot(pre, rest[:, D : D + FF], 1, 1)
    hat = third[...]
    grad_gains[0:1] = jnp.sum(normed * hat, axis=0, keepdims=True)
    grad_gains[1:2] = jnp.sum(normed, axis=0, keepdims=True)
    scaled = normed * gains[4:5]
    grad_mid = grad_out + third_inverse[...] * (
        scaled
        - jnp.mean(scaled, axis=-1, keepdims=True)
        - hat * jnp.mean(scaled * hat, axis=-1, keepdims=True)
    )
    grad_gains[2:3] = jnp.sum(grad_mid * branch_out[...], axis=0, keepdims=True)
    branch = (grad_mid * gains[6:7]).astype(BF)
    grad_branch[...] = branch
    attended = dot(rest[:, :D], branch, 1, 1).astype(BF)
    grad_attended_t[...] = attended
    product = attended.astype(F32) * attended_t[...]
    for h in range(HEADS):
        delta[h : h + 1] = jnp.sum(product[head_rows(h)], axis=0, keepdims=True)


def dense_back(segments, place, present, energies, errors, rest, down, gains, attended_t, branch_out, third,
               third_inverse, slope, ffn_out):
    rows = errors.shape[0]
    return call(
        functools.partial(dense_back_kernel, segments),
        (energies, errors, rest, down, gains, attended_t, branch_out, third,
         third_inverse, slope, ffn_out),
        (
            sds((rows, OUT), BF),
            sds((rows, D), BF),
            sds((rows, FF), BF),
            sds((rows, D), BF),
            sds((D, rows), BF),
            sds((HEADS, rows), F32),
            sds((4, D), F32),
            sds((8, LANES), F32),
        ),
        2 * rows * D * (D + 2 * FF + OUT),
        rows * FF * 8,
        place=(place, present),
        scratch=[pltpu.VMEM(energies.shape, F32)],
    )


def deal(size, place, first, second, keep, send, owner, at):
    slot = owner ^ place[1]
    same = place[0] == 0
    keep[slot, :, at] = jnp.where(same, first, second).astype(BF)
    send[slot, :, at] = jnp.where(same, second, first).astype(BF)


def dense_weights_kernel(size, place, grad_est, grad_ffn, grad_pre, grad_branch, attended_t,
                         normed_two, hidden, out_rows, keep, send, wide, tall):
    half = keep.shape[1]
    wide[:, D + FF :] = dot(out_rows[...], grad_est[...], 0, 0)
    wide[:, D : D + FF] = dot(normed_two[...], grad_pre[...], 0, 0)
    wide[:, :D] = dot(attended_t[...].astype(BF), grad_branch[...])
    tall[...] = dot(hidden[...], grad_ffn[...], 0, 0)
    for owner in range(size):
        row = 2 * owner * half
        deal(
            size, place, wide[row : row + half], wide[row + half : row + 2 * half],
            keep, send, owner, slice(0, REST),
        )
        for part in range(4):
            first = (8 * owner + part) * half
            second = (8 * owner + 4 + part) * half
            deal(
                size, place, tall[first : first + half], tall[second : second + half],
                keep, send, owner, slice(REST + D * part, REST + D * (part + 1)),
            )


def dense_weights(place, grad_est, grad_ffn, grad_pre, grad_branch, attended_t, normed_two,
                  hidden, out_rows, size):
    rows = grad_est.shape[0]
    piece = (size, D // size // 2, REST + 4 * D)
    return call(
        functools.partial(dense_weights_kernel, size),
        (grad_est, grad_ffn, grad_pre, grad_branch, attended_t, normed_two, hidden, out_rows),
        (sds(piece, BF), sds(piece, BF)),
        2 * rows * D * (D + 2 * FF + OUT),
        rows * FF * 8,
        place=(place,),
        scratch=[pltpu.VMEM((D, REST), F32), pltpu.VMEM((FF, D), F32)],
    )


def attend_back_kernel(carried, probs, keys_t, values_t, tops, queries_t, delta, top,
                       inverse_total, grad_attended_t, *refs):
    if carried:
        refs[1][...] = refs[0][...]
    else:
        refs[0][...] = jnp.zeros_like(refs[0])
    grad_queries, grad_kv = refs[-2:]

    def visit(block):
        factor = jnp.exp2(tops[block] - top[...]) * inverse_total[...]
        shift = delta[...] * factor

        def begin(h):
            grad = grad_attended_t[head_rows(h)].astype(F32) * factor[h : h + 1]
            grad = grad.astype(BF)
            return grad, dot(values_t[block, head_rows(h)], grad, 0, 0)

        def turn(h, found):
            grad, grad_probs = found
            scores = probs[block, h].astype(F32) * (grad_probs - shift[h : h + 1])
            return grad, scores.astype(BF)

        def end(h, found):
            grad, scores = found
            at = head_rows(h)
            grad_queries[at] += dot(keys_t[block, at], scores)
            grad_kv[block, at] = (dot(queries_t[at], scores, 1, 1) * LOG_TWO).astype(BF)
            grad_kv[block, head_rows(h, D)] = dot(grad, probs[block, h], 1, 1).astype(BF)

        heads_in_step(begin, turn, end)

    over_blocks(probs.shape[0], visit)


def attend_back(saved, queries_t, delta, top, inverse_total, grad_attended_t, carry):
    probs, keys_t, values_t, tops = saved
    count, _, rows, tokens = probs.shape
    carry = () if carry is None else (carry,)
    return call(
        functools.partial(attend_back_kernel, len(carry)),
        (probs, keys_t, values_t, tops, queries_t, delta, top, inverse_total,
         grad_attended_t, *carry),
        (sds((D, tokens), F32), sds((count, 2 * D, rows), BF)),
        count * (8 * rows * tokens * D * 5),
        count * (HEADS * rows * tokens * 2),
    )


def finish_kernel(size, groups, place, grad_queries, own_unit, weights_t, gains, late,
                  *refs):
    grads, units = refs[:groups], refs[groups : 2 * groups]
    keep, send, moments, full, grad_gains = refs[2 * groups :]
    rows = own_unit.shape[0]
    ones = jnp.ones((rows, LANES), BF)
    query = (grad_queries[...] * SCALE).astype(BF)
    moments[:D] = dot(query, jnp.concatenate([own_unit[...], ones], axis=1))
    total = None
    for grad, unit in zip(grads, units):
        for block in range(grad.shape[0]):
            term = dot(grad[block], jnp.concatenate([unit[block], ones], axis=1))
            total = term if total is None else total + term
    moments[D:] = total
    for first, size_out, row in ((0, D, 0), (D, 2 * D, 2)):
        at = slice(first, first + size_out)
        moment = moments[at, :D]
        column = moments[at, D : D + 1]
        weight = weights_t[at].astype(F32)
        grad_gains[row : row + 1] = jnp.sum(weight * moment, axis=0, keepdims=True)
        grad_gains[row + 1 : row + 2] = jnp.sum(weight * column, axis=0, keepdims=True)
        product = moment * gains[row : row + 1] + column * gains[row + 1 : row + 2]
        full[:, at] = product.T
    grad_gains[4:8] = late[...]
    half = keep.shape[1]
    for owner in range(size):
        row = 2 * owner * half
        deal(
            size, place, full[row : row + half], full[row + half : row + 2 * half],
            keep, send, owner, slice(0, QKV),
        )
        slot = owner ^ place[1]
        keep[slot, :, QKV:] = jnp.zeros((half, LANES), BF)
        send[slot, :, QKV:] = jnp.zeros((half, LANES), BF)
    same = place[0] == 0
    for owner, row, vector, lane, across in gain_places(size):
        slot = owner ^ place[1]
        value = grad_gains[vector : vector + 1, lane : lane + across]
        at = slice(QKV, QKV + across)
        keep[slot, row : row + 1, at] = jnp.where(same, value, 0.0).astype(BF)
        send[slot, row : row + 1, at] = jnp.where(same, 0.0, value).astype(BF)


def finish(place, grad_queries, own_unit, weights_t, gains, late, grads, units, size):
    rows = own_unit.shape[0]
    piece = (size, D // size // 2, QKV + LANES)
    return call(
        functools.partial(finish_kernel, size, len(grads)),
        (grad_queries, own_unit, weights_t, gains, late, *grads, *units),
        (sds(piece, BF), sds(piece, BF)),
        2 * rows * D * QKV * size,
        rows * D * 2 * size,
        place=(place,),
        scratch=[
            pltpu.VMEM((QKV, D + LANES), F32),
            pltpu.VMEM((D, QKV), F32),
            pltpu.VMEM((8, D), F32),
        ],
    )


def square_kernel(*refs):
    total = jnp.zeros((1, 1), F32)
    for ref in refs[:-1]:
        values = ref[...].astype(F32)
        rows = jnp.sum(values * values, axis=0, keepdims=True)
        total = total + jnp.sum(rows, axis=1, keepdims=True)
    refs[-1][...] = jnp.broadcast_to(total, refs[-1].shape)


def square_sum(*parts):
    size = sum(x.size for x in parts)
    return call(square_kernel, parts, sds((8, LANES), F32), 2 * size, 2 * size)


def group_sum_kernel(place, values, total, joined):
    total[...] = ordered_sum(place, values, joined)


def group_sum(place, values):
    return call(
        group_sum_kernel,
        (values,),
        sds(values.shape[1:], F32),
        values.size,
        4 * values.size,
        place=(place,),
        scratch=[pltpu.VMEM(values.shape, F32)],
    )


def bits(size):
    return [1 << k for k in range(size.bit_length() - 1)]


def masks(size):
    return sorted(range(1, size), key=lambda mask: (mask.bit_count(), mask))


def tie(*values):
    return lax.optimization_barrier(values)


def add_low(left, right):
    return (left.astype(F32) + right.astype(F32)).astype(BF)


def core_step(keep, send):
    return add_low(keep, swap(send, "seg", 1))


def scatter_step(total, size):
    received = [swap(total[mask], "wide", mask) for mask in range(1, size)]
    return functools.reduce(jnp.add, [x.astype(F32) for x in [total[0]] + received]).astype(BF)


def exchange(values, size):
    return jnp.stack([values] + [swap(values, "wide", mask) for mask in range(1, size)])


def segment_step(total):
    for mask in bits(lax.axis_size("seg"))[1:]:
        total = add_low(total, swap(total, "seg", mask))
    return total


def adam_update(weight, grad, moment, second, rate):
    moment = BETA_ONE * moment + (1 - BETA_ONE) * grad
    second = BETA_TWO * second + (1 - BETA_TWO) * grad * grad
    fixed_one = moment / (1 - BETA_ONE**ADAM_STEP)
    fixed_two = second / (1 - BETA_TWO**ADAM_STEP)
    weight = weight - rate * (fixed_one / (jnp.sqrt(fixed_two) + ADAM_EPS) + WEIGHT_DECAY * weight)
    return (weight, moment, second)


def adam_kernel(size, place, squares, early, early_other, late, late_other, *refs):
    masters, firsts, seconds = refs[0:3], refs[3:6], refs[6:9]
    news, new_firsts, new_seconds = refs[9:12], refs[12:15], refs[15:18]
    copies, norm = refs[18:21], refs[21]
    half = early.shape[0]
    same = place[0] == 0
    grad_norm = jnp.sqrt(squares[0:1, 0:1])
    norm[...] = jnp.broadcast_to(grad_norm, norm.shape)
    factor = jnp.minimum(1.0, CLIP_LIMIT / (grad_norm + 1e-06))

    def update(index, rows, lanes, grad, rate):
        at = (rows, lanes)
        found = adam_update(
            masters[index][at], grad * factor, firsts[index][at], seconds[index][at], rate
        )
        news[index][at], new_firsts[index][at], new_seconds[index][at] = found
        copies[index][at] = found[0].astype(BF)

    for side in range(2):
        use_own = same if side == 0 else jnp.logical_not(same)

        def pick(own, other, lanes):
            return jnp.where(use_own, own[:, lanes], other[:, lanes]).astype(F32)

        rows = slice(side * half, (side + 1) * half)
        update(0, rows, slice(0, QKV), pick(late, late_other, slice(0, QKV)), LEARN_RATE)
        update(0, rows, slice(QKV, QKV + REST), pick(early, early_other, slice(0, REST)),
               LEARN_RATE)
        for part in range(4):
            first = (4 * side + part) * half
            lanes = slice(REST + D * part, REST + D * (part + 1))
            update(1, slice(first, first + half), slice(0, D),
                   pick(early, early_other, lanes), LEARN_RATE)
    tall, across = gain_shape(size)
    lanes = slice(QKV, QKV + across)
    grad = jnp.where(same, late[:tall, lanes], late_other[:tall, lanes]).astype(F32)
    update(2, slice(0, tall), slice(0, across), grad, GAIN_RATE)


def adam(place, squares, grads, states, size):
    flat = gain_shape(size)
    states = [x.reshape(flat) if x.ndim == 1 else x for x in states]
    shapes = [x.shape for x in states[:3]]
    count = sum(x.size for x in states[:3])
    return call(
        functools.partial(adam_kernel, size),
        (squares, *grads, *states),
        tuple(sds(x, F32) for x in shapes) * 3
        + tuple(sds(x, BF) for x in shapes)
        + (sds((8, LANES), F32),),
        20 * count,
        28 * count,
        place=(place,),
    )


def adam_update(weight, grad, moment, second, rate):
    moment = BETA_ONE * moment + (1 - BETA_ONE) * grad
    second = BETA_TWO * second + (1 - BETA_TWO) * grad * grad
    fixed_one = moment / (1 - BETA_ONE**ADAM_STEP)
    fixed_two = second / (1 - BETA_TWO**ADAM_STEP)
    weight = weight - rate * (fixed_one / (jnp.sqrt(fixed_two) + ADAM_EPS) + WEIGHT_DECAY * weight)
    return (weight, moment, second)


def body(
    encoded,
    targets,
    present,
    wide_master,
    down_master,
    gain_master,
    wide_first,
    down_first,
    gain_first,
    wide_second,
    down_second,
    gain_second,
):
    size = lax.axis_size("wide") // 2
    position = lax.axis_index("wide") % size
    core = lax.axis_index("seg") % 2
    place = jnp.stack([core, position]).astype(jnp.int32)
    own = encoded[0]
    far = {0: swap(own, "wide", size)}
    first, rest = pack(place, wide_master, down_master, gain_master, size)

    high = size // 2
    first_mine = jnp.stack([first] + [swap(first, "wide", mask) for mask in range(1, size)])
    low_mine = [rest] + [swap(rest, "wide", mask) for mask in range(1, high)]
    far[0], first_mine, *low_mine = tie(far[0], first_mine, *low_mine)
    first_other = swap(first_mine, "seg", 1)
    queries_t, own_unit, weights_t, gains = start(place, own, first_mine, first_other, size)

    for mask in [high, *range(1, high)]:
        far[mask] = swap(far[0], "wide", mask)
    high_mine = [swap(x, "wide", high) for x in low_mine]
    low_other = [swap(x, "seg", 1) for x in low_mine]
    for mask in range(1, high):
        far[high + mask] = swap(far[high], "wide", mask)
    order = [high, *range(1, high), *range(high + 1, size)]
    groups = [[0]] + [order[k : k + 2] for k in range(0, size - 1, 2)]

    carry = None
    saved, units = [], []
    for group in groups:
        probs, keys_t, values_t, unit, tops, *carry = attend(
            [far[mask] for mask in group], queries_t, weights_t, gains, carry
        )
        saved.append((probs, keys_t, values_t, tops))
        units.append(unit)
    accum, top = carry
    accum, *high_mine = tie(accum, *high_mine)
    high_other = [swap(x, "seg", 1) for x in high_mine]
    rest_mine, rest_other = low_mine + high_mine, low_other + high_other

    rest_all, down_all = unpack(place, rest_mine + rest_other, size)
    (est_own, attended_t, inverse_total, branch_out, third, third_inverse, normed_two, slope,
     hidden, ffn_out, out_rows) = dense_forward(own, accum, rest_all, down_all, gains)

    errors, energy = error_energy(place, est_own, swap(est_own, "wide", size), targets[0])
    energy = exchange(energy, size)
    seg_count = lax.axis_size("seg")
    (grad_est, grad_ffn, grad_pre, grad_branch, grad_attended_t, delta, late_gains,
     loss) = dense_back(
        seg_count, place, present, energy, errors, rest_all, down_all, gains, attended_t, branch_out,
        third, third_inverse, slope, ffn_out,
    )
    keep, send = dense_weights(
        place, grad_est, grad_ffn, grad_pre, grad_branch, attended_t, normed_two, hidden,
        out_rows, size,
    )
    grad_attended_t, keep, send = tie(grad_attended_t, keep, send)

    early = core_step(keep, send)
    grad_queries, grads = None, []
    for k, item in enumerate(saved):
        grad_queries, grad_kv = attend_back(
            item, queries_t, delta, top, inverse_total, grad_attended_t, grad_queries
        )
        grads.append(grad_kv)
        if k == 0:
            grad_queries, early = tie(grad_queries, early)
            early = scatter_step(early, size)
    grad_queries, early = tie(grad_queries, early)
    early = segment_step(early)
    keep, send = finish(
        place, grad_queries, own_unit, weights_t, gains, late_gains, grads, units, size
    )
    late = core_step(keep, send)
    late, loss = tie(late, loss)
    for mask in bits(seg_count):
        loss = loss + swap(loss, "seg", mask)
    late = scatter_step(late, size)
    late, loss, early = tie(late, loss, early)
    early_other = swap(early, "seg", 1)
    late = segment_step(late)
    late_other = swap(late, "seg", 1)

    squares = square_sum(early, early_other, late, late_other)
    squares = group_sum(place, exchange(squares, size))
    squares = squares + swap(squares, "wide", size)
    *updated, grad_norm = adam(
        place,
        squares,
        (early, early_other, late, late_other),
        (wide_master, down_master, gain_master, wide_first, down_first, gain_first,
         wide_second, down_second, gain_second),
        size,
    )
    return (
        loss[0, 0],
        grad_norm[0, 0],
        *(x.reshape(-1) if k % 3 == 2 else x for k, x in enumerate(updated)),
    )


def solution(mesh):
    split, line = P("wide", None), P("wide")
    states = (split, split, line)
    return jax.shard_map(
        body,
        mesh=mesh,
        in_specs=(P("seg", "wide", None), P("seg", None, None), P("seg", None)) + states * 3,
        out_specs=(P(), P()) + states * 4,
        check_vma=False,
    )
```

```python
import functools
import math

import jax
import jax.numpy as jnp
from jax import lax
from jax.experimental import pallas as pl
from jax.experimental.pallas import tpu as pltpu
from jax.sharding import PartitionSpec as P

D = 384
HEADS = 8
HEAD = D // HEADS
FF = 1536
STEMS = 4
SAMPLES = 32
OUT = STEMS * SAMPLES
QKV = 3 * D
REST = D + FF + OUT
ADAM_STEP = 10
LANES = 128

NORM_EPS = 1e-05
ENERGY_EPS = 1e-05
BETA_ONE = 0.9
BETA_TWO = 0.999
ADAM_EPS = 1e-08
LEARN_RATE = 0.1
GAIN_RATE = 0.5
WEIGHT_DECAY = 0.01
CLIP_LIMIT = 0.001

BF = jnp.bfloat16
F32 = jnp.float32
SCALE = 1.0 / math.sqrt(HEAD)
LOG_TWO = math.log(2.0)
VMEM_LIMIT = 16 * 2**20


def swap(x, axis, mask):
    return lax.ppermute(x, axis, [(i, i ^ mask) for i in range(lax.axis_size(axis))])


def dot(left, right, left_dim=1, right_dim=0):
    return lax.dot_general(
        left,
        right,
        (((left_dim,), (right_dim,)), ((), ())),
        preferred_element_type=F32,
    )


def unit_rows(values):
    centred = values - jnp.mean(values, axis=-1, keepdims=True)
    spread = jnp.mean(centred * centred, axis=-1, keepdims=True)
    inverse = lax.rsqrt(spread + NORM_EPS)
    return centred * inverse, inverse


def call(kernel, operands, out_shape, flops, moved, place=(), scratch=(), in_specs=None,
         out_specs=None, aliases=None):
    here = pl.BlockSpec(memory_space=pltpu.VMEM)
    small = pl.BlockSpec(memory_space=pltpu.SMEM)
    return pl.pallas_call(
        kernel,
        out_shape=out_shape,
        in_specs=[small] * len(place) + (in_specs or [here] * len(operands)),
        out_specs=out_specs or jax.tree.map(lambda _: here, out_shape),
        scratch_shapes=scratch,
        input_output_aliases=aliases or {},
        compiler_params=pltpu.CompilerParams(vmem_limit_bytes=VMEM_LIMIT),
        cost_estimate=pl.CostEstimate(flops=flops, bytes_accessed=moved, transcendentals=0),
    )(*place, *operands)


def sds(shape, dtype):
    return jax.ShapeDtypeStruct(shape, dtype)


def gain_shape(size):
    count = 8 * D // size
    width = math.gcd(count, LANES)
    return count // width, width


def gain_places(size):
    tall, across = gain_shape(size)
    for owner in range(size):
        for row in range(tall):
            flat = (owner * tall + row) * across
            yield owner, row, flat // D, flat % D, across


def pack_kernel(size, place, wide, down, gains, first, rest):
    half = first.shape[0]
    same = place[0] == 0
    picked = jnp.where(same, wide[:half], wide[half:]).astype(BF)
    first[:, :QKV] = picked[:, :QKV]
    rest[:, :REST] = picked[:, QKV:]
    for part in range(4):
        row, other = half * part, half * (4 + part)
        piece = jnp.where(same, down[row : row + half], down[other : other + half])
        rest[:, REST + D * part : REST + D * (part + 1)] = piece.astype(BF)
    first[:, QKV:] = jnp.zeros((half, LANES), BF)
    tall, across = gain_shape(size)
    first[:tall, QKV : QKV + across] = jnp.where(same, gains[...], 0.0).astype(BF)


def pack(place, wide, down, gains, size):
    half = wide.shape[0] // 2
    return call(
        functools.partial(pack_kernel, size),
        (wide, down, gains.reshape(gain_shape(size))),
        (sds((half, QKV + LANES), BF), sds((half, REST + 4 * D), BF)),
        1000,
        4 * (wide.size + down.size),
        place=(place,),
    )


def start_kernel(size, place, own, mine, other, queries_t, own_unit, weights_t, gains, joined):
    core, position = place[0], place[1]
    half = mine.shape[1]
    for owner in range(size):
        slot = owner ^ position
        near, far = mine[slot], other[slot]
        row = 2 * owner * half
        joined[row : row + half] = jnp.where(core == 0, near, far)
        joined[row + half : row + 2 * half] = jnp.where(core == 0, far, near)
    for owner, row, vector, lane, across in gain_places(size):
        at = 2 * owner * half + row
        gains[vector : vector + 1, lane : lane + across] = joined[
            at : at + 1, QKV : QKV + across
        ].astype(F32)
    weights_t[...] = joined[:, :QKV].T
    hat, _ = unit_rows(own[...].astype(F32))
    own_unit[...] = hat.astype(BF)
    normed = (hat * gains[0:1] + gains[1:2]).astype(BF)
    found = dot(weights_t[:D], normed, 1, 1)
    queries_t[...] = (found * (SCALE / LOG_TWO)).astype(BF)


def start(place, own, mine, other, size):
    rows = own.shape[0]
    return call(
        functools.partial(start_kernel, size),
        (own, mine, other),
        (sds((D, rows), BF), sds((rows, D), BF), sds((QKV, D), BF), sds((8, D), F32)),
        2 * rows * D * D,
        rows * D * 8,
        place=(place,),
        scratch=[pltpu.VMEM((D, QKV + LANES), BF)],
    )


def heads_in_step(first, second, third):
    ahead, behind = first(0), None
    for h in range(HEADS):
        found = ahead
        if h + 1 < HEADS:
            ahead = first(h + 1)
        found = second(h, found)
        if behind is not None:
            third(h - 1, behind)
        behind = found
    third(HEADS - 1, behind)


def head_rows(h, offset=0, height=HEAD):
    return slice(offset + height * h, offset + height * (h + 1))


def over_blocks(count, visit):
    if count == 1:
        visit(0)
    else:
        lax.fori_loop(0, count, lambda block, carry: (visit(block), carry)[1], 0)


def attend_kernel(count, carried, *refs):
    queries_t, weights_t, gains = refs[:3]
    blocks = refs[3 : 3 + count]
    refs = refs[3 + count :]
    if carried:
        accum_in, top_in = refs[:2]
        refs = refs[2:]
    probs, keys_t, values_t, unit, tops, accum, top, joined = refs
    if carried:
        accum[...] = accum_in[...]
        top[...] = top_in[...]
    else:
        accum[...] = jnp.zeros_like(accum)
        top[...] = jnp.full_like(top, -1e30)
    for block in range(count):
        joined[block] = blocks[block][...]

    def visit(block):
        hat, _ = unit_rows(joined[block].astype(F32))
        unit[block] = hat.astype(BF)
        crossed = (hat * gains[2:3] + gains[3:4]).astype(BF)
        keys_t[block] = dot(weights_t[D : 2 * D], crossed, 1, 1).astype(BF)
        values_t[block] = dot(weights_t[2 * D :], crossed, 1, 1).astype(BF)
        ones = jnp.ones((16, crossed.shape[0]), BF)

        def score(h):
            return dot(keys_t[block, head_rows(h)], queries_t[head_rows(h)], 0, 0)

        def soften(h, scores):
            before = top[h : h + 1]
            newest = jnp.maximum(before, jnp.max(scores, axis=0, keepdims=True))
            top[h : h + 1] = newest
            weight = jnp.exp2(scores - newest).astype(BF)
            probs[block, h] = weight
            return weight, jnp.exp2(before - newest)

        def gather(h, found):
            weight, fade = found
            tall = head_rows(h, 0, 64)
            values = jnp.concatenate([values_t[block, head_rows(h)], ones], axis=0)
            accum[tall] = accum[tall] * fade + dot(values, weight)

        heads_in_step(score, soften, gather)
        tops[block] = top[...]

    over_blocks(count, visit)


def attend(blocks, queries_t, weights_t, gains, carry):
    count, rows = len(blocks), blocks[0].shape[0]
    tokens = queries_t.shape[1]
    return call(
        functools.partial(attend_kernel, count, carry is not None),
        (queries_t, weights_t, gains, *blocks, *(carry or ())),
        (
            sds((count, HEADS, rows, tokens), BF),
            sds((count, D, rows), BF),
            sds((count, D, rows), BF),
            sds((count, rows, D), BF),
            sds((count, HEADS, tokens), F32),
            sds((64 * HEADS, tokens), F32),
            sds((HEADS, tokens), F32),
        ),
        count * (4 * rows * tokens * D * 5 + 4 * rows * D * D),
        count * (HEADS * rows * tokens * 2),
        scratch=[pltpu.VMEM((count, rows, D), BF)],
    )


def unpack_kernel(size, place, *refs):
    high = size // 2
    rest, down, joined = refs[2 * high + 2 :]
    core, position = place[0], place[1]
    half = joined.shape[1]
    for side in range(2):
        pieces = refs[side * (high + 1) : (side + 1) * (high + 1)]
        for other in range(size):
            slot = 2 * (other ^ position) + (side ^ core)
            joined[slot] = pieces[other][...] if other < high else pieces[high][other - high]
    for owner in range(size):
        for side in range(2):
            slot = 2 * owner + side
            rest[slot * half : (slot + 1) * half] = joined[slot, :, :REST]
            for part in range(4):
                row = (4 * slot + part) * half
                down[row : row + half] = joined[
                    slot, :, REST + D * part : REST + D * (part + 1)
                ]


def unpack(place, pieces, size):
    half, across = pieces[0].shape
    return call(
        functools.partial(unpack_kernel, size),
        tuple(pieces),
        (sds((D, REST), BF), sds((FF, D), BF)),
        1000,
        4 * D * across,
        place=(place,),
        scratch=[pltpu.VMEM((2 * size, half, across), BF)],
    )


def row_part(part, rows):
    split = 3 * rows // 4
    return slice(split, rows) if part else slice(0, split)


def dense_kernel(part, inputs, accum, rest, down, gains, *refs):
    (attended_t, inverse_total, branch_out, third, third_inverse, normed_two, slope, hidden,
     ffn_out, out_rows, estimate) = refs[-11:]
    rows = row_part(part, inputs.shape[0])
    for h in range(HEADS):
        inverse = 1.0 / accum[64 * h + HEAD : 64 * h + HEAD + 1, rows]
        inverse_total[h : h + 1, rows] = inverse
        attended_t[HEAD * h : HEAD * (h + 1), rows] = (
            accum[64 * h : 64 * h + HEAD, rows] * inverse
        )
    branch = dot(attended_t[:, rows].astype(BF), rest[:, :D], 0, 0)
    branch_out[rows] = branch
    mid = inputs[rows].astype(F32) + gains[6:7] * branch
    hat, inverse = unit_rows(mid)
    third[rows] = hat
    third_inverse[rows] = inverse
    normed = (hat * gains[4:5] + gains[5:6]).astype(BF)
    normed_two[rows] = normed
    pre = dot(normed, rest[:, D : D + FF])
    gate = 0.5 * (1.0 + lax.erf(pre * math.sqrt(0.5)))
    hid = (pre * gate).astype(BF)
    hidden[rows] = hid
    bell = jnp.exp(-0.5 * pre * pre) * (1.0 / math.sqrt(2.0 * math.pi))
    slope[rows] = gate + pre * bell
    ffn = dot(hid, down[...])
    ffn_out[rows] = ffn
    out = (mid + gains[7:8] * ffn).astype(BF)
    out_rows[rows] = out
    estimate[...] = dot(out, rest[:, D + FF :]).astype(BF)


def dense_forward(part, inputs, accum, rest, down, gains, started):
    rows = inputs.shape[0]
    taken = row_part(part, rows)
    return call(
        functools.partial(dense_kernel, part),
        (inputs, accum, rest, down, gains, *started),
        (
            sds((D, rows), F32),
            sds((HEADS, rows), F32),
            sds((rows, D), F32),
            sds((rows, D), F32),
            sds((rows, 1), F32),
            sds((rows, D), BF),
            sds((rows, FF), F32),
            sds((rows, FF), BF),
            sds((rows, D), F32),
            sds((rows, D), BF),
            sds((taken.stop - taken.start, OUT), BF),
        ),
        rows * D * (D + 2 * FF + OUT),
        rows * FF * 4,
        aliases={5 + k: k for k in range(len(started))},
    )


def error_kernel(place, *refs):
    own, far, (targets, errors, energy) = refs[:2], refs[2:4], refs[4:]
    rows = errors.shape[0]
    row = lax.broadcasted_iota(jnp.int32, (8, OUT), 0)
    total = jnp.zeros((8, OUT), F32)
    for part in range(2):
        taken = row_part(part, rows)
        first = pl.multiple_of(place[1] * rows + taken.start, 8)
        wanted = targets[pl.ds(first, taken.stop - taken.start)]
        error = wanted - (own[part][...].astype(F32) + far[part][...].astype(F32))
        errors[taken] = error
        found = jnp.sum(error * error, axis=0, keepdims=True)
        clean = jnp.sum(wanted * wanted, axis=0, keepdims=True)
        total = total + jnp.where(row == 0, found, jnp.where(row == 1, clean, 0.0))
    energy[...] = total


def error_energy(place, own, far, targets):
    rows = own[0].shape[0] + own[1].shape[0]
    return call(
        error_kernel,
        (*own, *far, targets),
        (sds((rows, OUT), F32), sds((8, OUT), F32)),
        rows * OUT * 8,
        rows * OUT * 12,
        place=(place,),
    )


def ordered_sum(place, values, joined):
    size = joined.shape[0]
    for slot in range(size):
        joined[slot ^ place[1]] = values[slot]
    total = joined[0]
    for slot in range(1, size):
        total = total + joined[slot]
    return total


def stem_sums(values):
    stem = lax.broadcasted_iota(jnp.int32, values.shape, 1) // SAMPLES
    total = jnp.zeros_like(values)
    for k in range(STEMS):
        part = jnp.sum(jnp.where(stem == k, values, 0.0), axis=1, keepdims=True)
        total = jnp.where(stem == k, part, total)
    return total


def dense_back_kernel(segments, place, present, energies, errors, rest, down, gains, attended_t, branch_out,
                      third, third_inverse, slope, ffn_out, grad_est, grad_ffn, grad_pre,
                      grad_branch, grad_attended_t, delta, grad_gains, loss, joined):
    energy = ordered_sum(place, energies, joined)
    lane = lax.broadcasted_iota(jnp.int32, (1, OUT), 1)
    counted = jnp.zeros((1, OUT), F32)
    for k in range(STEMS):
        counted = jnp.where(lane // SAMPLES == k, present[0, k].astype(F32), counted)
    counted = counted * (10.0 / math.log(10.0) / (segments * STEMS))
    found = stem_sums(energy[0:1]) + ENERGY_EPS
    clean = stem_sums(energy[1:2]) + ENERGY_EPS
    terms = counted * (jnp.log(found) - jnp.log(clean))
    terms = jnp.where(lane % SAMPLES == 0, terms, 0.0)
    loss[...] = jnp.broadcast_to(jnp.sum(terms, axis=1, keepdims=True), loss.shape)
    low = (errors[...] * (-2.0 * counted / found)).astype(BF)
    grad_est[...] = low
    grad_out = dot(low, rest[:, D + FF :], 1, 1)
    grad_gains[3:4] = jnp.sum(grad_out * ffn_out[...], axis=0, keepdims=True)
    ffn = (grad_out * gains[7:8]).astype(BF)
    grad_ffn[...] = ffn
    hidden = dot(ffn, down[...], 1, 1).astype(BF)
    pre = (hidden.astype(F32) * slope[...]).astype(BF)
    grad_pre[...] = pre
    normed = dot(pre, rest[:, D : D + FF], 1, 1)
    hat = third[...]
    grad_gains[0:1] = jnp.sum(normed * hat, axis=0, keepdims=True)
    grad_gains[1:2] = jnp.sum(normed, axis=0, keepdims=True)
    scaled = normed * gains[4:5]
    grad_mid = grad_out + third_inverse[...] * (
        scaled
        - jnp.mean(scaled, axis=-1, keepdims=True)
        - hat * jnp.mean(scaled * hat, axis=-1, keepdims=True)
    )
    grad_gains[2:3] = jnp.sum(grad_mid * branch_out[...], axis=0, keepdims=True)
    branch = (grad_mid * gains[6:7]).astype(BF)
    grad_branch[...] = branch
    attended = dot(rest[:, :D], branch, 1, 1).astype(BF)
    grad_attended_t[...] = attended
    product = attended.astype(F32) * attended_t[...]
    for h in range(HEADS):
        delta[h : h + 1] = jnp.sum(product[head_rows(h)], axis=0, keepdims=True)


def dense_back(segments, place, present, energies, errors, rest, down, gains, attended_t, branch_out, third,
               third_inverse, slope, ffn_out):
    rows = errors.shape[0]
    return call(
        functools.partial(dense_back_kernel, segments),
        (energies, errors, rest, down, gains, attended_t, branch_out, third,
         third_inverse, slope, ffn_out),
        (
            sds((rows, OUT), BF),
            sds((rows, D), BF),
            sds((rows, FF), BF),
            sds((rows, D), BF),
            sds((D, rows), BF),
            sds((HEADS, rows), F32),
            sds((4, D), F32),
            sds((8, LANES), F32),
        ),
        2 * rows * D * (D + 2 * FF + OUT),
        rows * FF * 8,
        place=(place, present),
        scratch=[pltpu.VMEM(energies.shape, F32)],
    )


def deal(size, place, first, second, keep, send, owner, at):
    slot = owner ^ place[1]
    same = place[0] == 0
    keep[slot, :, at] = jnp.where(same, first, second).astype(BF)
    send[slot, :, at] = jnp.where(same, second, first).astype(BF)


def dense_weights_kernel(size, place, grad_est, grad_ffn, grad_pre, grad_branch, attended_t,
                         normed_two, hidden, out_rows, keep, send, wide, tall):
    half = keep.shape[1]
    wide[:, D + FF :] = dot(out_rows[...], grad_est[...], 0, 0)
    wide[:, D : D + FF] = dot(normed_two[...], grad_pre[...], 0, 0)
    wide[:, :D] = dot(attended_t[...].astype(BF), grad_branch[...])
    tall[...] = dot(hidden[...], grad_ffn[...], 0, 0)
    for owner in range(size):
        row = 2 * owner * half
        deal(
            size, place, wide[row : row + half], wide[row + half : row + 2 * half],
            keep, send, owner, slice(0, REST),
        )
        for part in range(4):
            first = (8 * owner + part) * half
            second = (8 * owner + 4 + part) * half
            deal(
                size, place, tall[first : first + half], tall[second : second + half],
                keep, send, owner, slice(REST + D * part, REST + D * (part + 1)),
            )


def dense_weights(place, grad_est, grad_ffn, grad_pre, grad_branch, attended_t, normed_two,
                  hidden, out_rows, size):
    rows = grad_est.shape[0]
    piece = (size, D // size // 2, REST + 4 * D)
    return call(
        functools.partial(dense_weights_kernel, size),
        (grad_est, grad_ffn, grad_pre, grad_branch, attended_t, normed_two, hidden, out_rows),
        (sds(piece, BF), sds(piece, BF)),
        2 * rows * D * (D + 2 * FF + OUT),
        rows * FF * 8,
        place=(place,),
        scratch=[pltpu.VMEM((D, REST), F32), pltpu.VMEM((FF, D), F32)],
    )


def attend_back_kernel(carried, probs, keys_t, values_t, tops, queries_t, delta, top,
                       inverse_total, grad_attended_t, *refs):
    if carried:
        refs[1][...] = refs[0][...]
    else:
        refs[0][...] = jnp.zeros_like(refs[0])
    grad_queries, grad_kv = refs[-2:]

    def visit(block):
        factor = jnp.exp2(tops[block] - top[...]) * inverse_total[...]
        shift = delta[...] * factor

        def begin(h):
            grad = grad_attended_t[head_rows(h)].astype(F32) * factor[h : h + 1]
            grad = grad.astype(BF)
            return grad, dot(values_t[block, head_rows(h)], grad, 0, 0)

        def turn(h, found):
            grad, grad_probs = found
            scores = probs[block, h].astype(F32) * (grad_probs - shift[h : h + 1])
            return grad, scores.astype(BF)

        def end(h, found):
            grad, scores = found
            at = head_rows(h)
            grad_queries[at] += dot(keys_t[block, at], scores)
            grad_kv[block, at] = (dot(queries_t[at], scores, 1, 1) * LOG_TWO).astype(BF)
            grad_kv[block, head_rows(h, D)] = dot(grad, probs[block, h], 1, 1).astype(BF)

        heads_in_step(begin, turn, end)

    over_blocks(probs.shape[0], visit)


def attend_back(saved, queries_t, delta, top, inverse_total, grad_attended_t, carry):
    probs, keys_t, values_t, tops = saved
    count, _, rows, tokens = probs.shape
    carry = () if carry is None else (carry,)
    return call(
        functools.partial(attend_back_kernel, len(carry)),
        (probs, keys_t, values_t, tops, queries_t, delta, top, inverse_total,
         grad_attended_t, *carry),
        (sds((D, tokens), F32), sds((count, 2 * D, rows), BF)),
        count * (8 * rows * tokens * D * 5),
        count * (HEADS * rows * tokens * 2),
    )


def finish_kernel(size, groups, place, grad_queries, own_unit, weights_t, gains, late,
                  *refs):
    grads, units = refs[:groups], refs[groups : 2 * groups]
    keep, send, moments, full, grad_gains = refs[2 * groups :]
    rows = own_unit.shape[0]
    ones = jnp.ones((rows, LANES), BF)
    query = (grad_queries[...] * SCALE).astype(BF)
    moments[:D] = dot(query, jnp.concatenate([own_unit[...], ones], axis=1))
    total = None
    for grad, unit in zip(grads, units):
        for block in range(grad.shape[0]):
            term = dot(grad[block], jnp.concatenate([unit[block], ones], axis=1))
            total = term if total is None else total + term
    moments[D:] = total
    for first, size_out, row in ((0, D, 0), (D, 2 * D, 2)):
        at = slice(first, first + size_out)
        moment = moments[at, :D]
        column = moments[at, D : D + 1]
        weight = weights_t[at].astype(F32)
        grad_gains[row : row + 1] = jnp.sum(weight * moment, axis=0, keepdims=True)
        grad_gains[row + 1 : row + 2] = jnp.sum(weight * column, axis=0, keepdims=True)
        product = moment * gains[row : row + 1] + column * gains[row + 1 : row + 2]
        full[:, at] = product.T
    grad_gains[4:8] = late[...]
    half = keep.shape[1]
    for owner in range(size):
        row = 2 * owner * half
        deal(
            size, place, full[row : row + half], full[row + half : row + 2 * half],
            keep, send, owner, slice(0, QKV),
        )
        slot = owner ^ place[1]
        keep[slot, :, QKV:] = jnp.zeros((half, LANES), BF)
        send[slot, :, QKV:] = jnp.zeros((half, LANES), BF)
    same = place[0] == 0
    for owner, row, vector, lane, across in gain_places(size):
        slot = owner ^ place[1]
        value = grad_gains[vector : vector + 1, lane : lane + across]
        at = slice(QKV, QKV + across)
        keep[slot, row : row + 1, at] = jnp.where(same, value, 0.0).astype(BF)
        send[slot, row : row + 1, at] = jnp.where(same, 0.0, value).astype(BF)


def finish(place, grad_queries, own_unit, weights_t, gains, late, grads, units, size):
    rows = own_unit.shape[0]
    piece = (size, D // size // 2, QKV + LANES)
    return call(
        functools.partial(finish_kernel, size, len(grads)),
        (grad_queries, own_unit, weights_t, gains, late, *grads, *units),
        (sds(piece, BF), sds(piece, BF)),
        2 * rows * D * QKV * size,
        rows * D * 2 * size,
        place=(place,),
        scratch=[
            pltpu.VMEM((QKV, D + LANES), F32),
            pltpu.VMEM((D, QKV), F32),
            pltpu.VMEM((8, D), F32),
        ],
    )


def square_kernel(*refs):
    total = jnp.zeros((1, 1), F32)
    for ref in refs[:-1]:
        values = ref[...].astype(F32)
        rows = jnp.sum(values * values, axis=0, keepdims=True)
        total = total + jnp.sum(rows, axis=1, keepdims=True)
    refs[-1][...] = jnp.broadcast_to(total, refs[-1].shape)


def square_sum(*parts):
    size = sum(x.size for x in parts)
    return call(square_kernel, parts, sds((8, LANES), F32), 2 * size, 2 * size)


def branch_sum_kernel(place, own, *refs):
    parts, total, joined = refs[:-2], refs[-2], refs[-1]
    for slot, part in enumerate(parts):
        value = part[...]
        if slot == 0:
            value = jnp.where(place[0] == 0, own[...], value)
        joined[slot ^ place[1]] = value
    found = joined[0]
    for slot in range(1, len(parts)):
        found = found + joined[slot]
    total[...] = found


def branch_sum(place, own, parts):
    return call(
        branch_sum_kernel,
        (own, *parts),
        sds(own.shape, F32),
        own.size,
        4 * own.size,
        place=(place,),
        scratch=[pltpu.VMEM((len(parts),) + own.shape, F32)],
    )


def bits(size):
    return [1 << k for k in range(size.bit_length() - 1)]


def masks(size):
    return sorted(range(1, size), key=lambda mask: (mask.bit_count(), mask))


def tie(*values):
    return lax.optimization_barrier(values)


def add_low(left, right):
    return (left.astype(F32) + right.astype(F32)).astype(BF)


def core_step(keep, send):
    return add_low(keep, swap(send, "seg", 1))


def branch_parts(values, size):
    segments, wide = lax.axis_size("seg"), 2 * size
    found = []
    for slot in range(size):
        pairs = []
        for seg in range(segments):
            mask = size + slot if seg % 2 else slot
            if mask:
                pairs += [(seg * wide + w, seg * wide + (w ^ mask)) for w in range(wide)]
        found.append(lax.ppermute(values, ("seg", "wide"), pairs))
    return found


def send_members(total, size):
    return [total[0]] + [swap(total[mask], "wide", mask) for mask in range(1, size)]


def sum_low(parts):
    return functools.reduce(jnp.add, [x.astype(F32) for x in parts]).astype(BF)


def exchange(values, size):
    return jnp.stack([values] + [swap(values, "wide", mask) for mask in range(1, size)])


def segment_step(total):
    for mask in bits(lax.axis_size("seg"))[1:]:
        total = add_low(total, swap(total, "seg", mask))
    return total


def adam_update(weight, grad, moment, second, rate):
    moment = BETA_ONE * moment + (1 - BETA_ONE) * grad
    second = BETA_TWO * second + (1 - BETA_TWO) * (grad * grad)
    fixed_one = moment * (rate / (1 - BETA_ONE**ADAM_STEP))
    fixed_two = second * (1 / (1 - BETA_TWO**ADAM_STEP))
    weight = weight * (1 - rate * WEIGHT_DECAY) - fixed_one / (jnp.sqrt(fixed_two) + ADAM_EPS)
    return (weight, moment, second)


def adam_chunks(size, half):
    tall, across = gain_shape(size)
    chunks = []
    for side in range(2):
        rows, ends = slice(4 * side * half, 4 * (side + 1) * half), slice(0, D)
        parts = [
            (slice((4 * side + k) * half, (4 * side + k + 1) * half), ends, 0,
             slice(REST + D * k, REST + D * (k + 1)))
            for k in range(4)
        ]
        chunks.append((1, side, rows, ends, parts))
        rows = slice(side * half, (side + 1) * half)
        parts = [
            (rows, slice(0, QKV), 1, slice(0, QKV)),
            (rows, slice(QKV, QKV + REST), 0, slice(0, REST)),
        ]
        chunks.append((0, side, rows, slice(0, QKV + REST), parts))
    rows, lanes = slice(0, tall), slice(0, across)
    chunks.append((2, 0, rows, lanes, [(rows, lanes, 1, slice(QKV, QKV + across))]))
    return chunks


def tiles(rows, lanes, source):
    high, across = rows.stop - rows.start, lanes.stop - lanes.start
    for row in range(0, high, 16):
        tall = min(16, high - row)
        for lane in range(0, across, D):
            part = min(D, across - lane)
            yield (
                (slice(rows.start + row, rows.start + row + tall),
                 slice(lanes.start + lane, lanes.start + lane + part)),
                (slice(row, row + tall),
                 slice(source.start + lane, source.start + lane + part)),
            )


def adam_kernel(size, place, squares, squares_other, early, early_other, late, late_other,
                *refs):
    states, outs, norm = [refs[k : k + 3] for k in (0, 3, 6)], refs[9:21], refs[21]
    held, sems = refs[22:34], refs[34]
    same = place[0] == 0
    grad_norm = jnp.sqrt(squares[0:1, 0:1] + squares_other[0:1, 0:1])
    norm[...] = grad_norm
    factor = jnp.minimum(1.0, CLIP_LIMIT / (grad_norm + 1e-06))
    copies, aligned = [], early.shape[0] % 16 == 0

    def send(source, target):
        copies.append(pltpu.make_async_copy(source, target, sems.at[len(copies)]))
        copies[-1].start()

    for index, side, rows, lanes, parts in adam_chunks(size, early.shape[0]):
        rate = GAIN_RATE if index == 2 else LEARN_RATE
        for part_rows, part_lanes, which, source in parts:
            own, other = (late, late_other) if which else (early, early_other)
            if side:
                own, other = other, own
            for here, there in tiles(part_rows, part_lanes, source):
                grad = jnp.where(same, own[there].astype(F32), other[there].astype(F32))
                weight, moment, second = (x[index][here] for x in states)
                found = adam_update(weight, grad * factor, moment, second, rate)
                for kind, value in enumerate((*found, found[0].astype(BF))):
                    held[3 * kind + index][here] = value
        if aligned:
            for slot in range(index, 12, 3):
                send(held[slot].at[rows, lanes], outs[slot].at[rows, lanes])
    if not aligned:
        for slot in range(12):
            send(held[slot], outs[slot])
    for copy in copies:
        copy.wait()


def adam(place, squares, grads, states, size):
    flat = gain_shape(size)
    states = [x.reshape(flat) if x.ndim == 1 else x for x in states]
    shapes = [x.shape for x in states[:3]]
    count = sum(x.size for x in states[:3])
    kinds = [(shape, F32) for shape in shapes] * 3 + [(shape, BF) for shape in shapes]
    outside = pl.BlockSpec(memory_space=pl.ANY)
    return call(
        functools.partial(adam_kernel, size),
        (*squares, *grads, *states),
        tuple(sds(*kind) for kind in kinds) + (sds((1, 1), F32),),
        20 * count,
        28 * count,
        place=(place,),
        out_specs=(outside,) * 12 + (pl.BlockSpec(memory_space=pltpu.VMEM),),
        scratch=[pltpu.VMEM(*kind) for kind in kinds]
        + [pltpu.SemaphoreType.DMA((4 * len(adam_chunks(size, grads[0].shape[0])),))],
    )


def body(
    encoded,
    targets,
    present,
    wide_master,
    down_master,
    gain_master,
    wide_first,
    down_first,
    gain_first,
    wide_second,
    down_second,
    gain_second,
):
    size = lax.axis_size("wide") // 2
    position = lax.axis_index("wide") % size
    core = lax.axis_index("seg") % 2
    place = jnp.stack([core, position]).astype(jnp.int32)
    own = encoded[0]
    far = {0: swap(own, "wide", size)}
    first, rest = pack(place, wide_master, down_master, gain_master, size)

    high = size // 2
    first_mine = jnp.stack([first] + [swap(first, "wide", mask) for mask in range(1, size)])
    low_mine = [rest] + [swap(rest, "wide", mask) for mask in range(1, high)]
    far[0], first_mine, *low_mine = tie(far[0], first_mine, *low_mine)
    first_other = swap(first_mine, "seg", 1)
    far[high] = swap(far[0], "wide", high)
    near, first_other = tie(far[0], first_other)
    for mask in range(1, high):
        far[mask] = swap(near, "wide", mask)
    queries_t, own_unit, weights_t, gains = start(place, own, first_mine, first_other, size)

    high_mine = swap(jnp.stack(low_mine), "wide", high)
    order = [high, *range(1, high), *range(high + 1, size)]
    groups = [[0]] + [order[k : k + 2] for k in range(0, size - 1, 2)]

    carry = None
    saved, units = [], []
    for group in groups:
        if len(saved) == 1:
            carry[0], far[high], *low_mine = tie(carry[0], far[high], *low_mine)
            low_other = [swap(x, "seg", 1) for x in low_mine]
            for mask in range(1, high):
                far[high + mask] = swap(far[high], "wide", mask)
        probs, keys_t, values_t, unit, tops, *carry = attend(
            [far[mask] for mask in group], queries_t, weights_t, gains, carry
        )
        saved.append((probs, keys_t, values_t, tops))
        if len(saved) == 2:
            carry[0], *low_other = tie(carry[0], *low_other)
        units.append(unit)
    accum, top = carry
    accum, high_mine = tie(accum, high_mine)
    high_other = swap(high_mine, "seg", 1)
    pieces = (*low_mine, high_mine, *low_other, high_other)

    rest_all, down_all = unpack(place, pieces, size)
    started, own_parts, far_parts = (), [], []
    for part in range(2):
        *started, estimate = dense_forward(
            part, own, accum, rest_all, down_all, gains, started
        )
        own_parts.append(estimate)
        far_parts.append(swap(estimate, "wide", size))
    (attended_t, inverse_total, branch_out, third, third_inverse, normed_two, slope, hidden,
     ffn_out, out_rows) = started

    errors, energy = error_energy(place, own_parts, far_parts, targets[0])
    energy = exchange(energy, size)
    seg_count = lax.axis_size("seg")
    (grad_est, grad_ffn, grad_pre, grad_branch, grad_attended_t, delta, late_gains,
     loss) = dense_back(
        seg_count, place, present, energy, errors, rest_all, down_all, gains, attended_t, branch_out,
        third, third_inverse, slope, ffn_out,
    )
    keep, send = dense_weights(
        place, grad_est, grad_ffn, grad_pre, grad_branch, attended_t, normed_two, hidden,
        out_rows, size,
    )
    grad_attended_t, keep, send = tie(grad_attended_t, keep, send)

    early = core_step(keep, send)
    grad_queries, grads = None, []
    for k, item in enumerate(saved):
        grad_queries, grad_kv = attend_back(
            item, queries_t, delta, top, inverse_total, grad_attended_t, grad_queries
        )
        grads.append(grad_kv)
        if k == 0:
            grad_queries, early = tie(grad_queries, early)
            early = send_members(early, size)
    keep, send = finish(
        place, grad_queries, own_unit, weights_t, gains, late_gains, grads, units, size
    )
    keep, send, *early = tie(keep, send, *early)
    late = core_step(keep, send)
    early = segment_step(sum_low(early))
    late, loss = tie(late, loss)
    for mask in bits(seg_count):
        loss = loss + swap(loss, "seg", mask)
    late = sum_low(send_members(late, size))
    late, loss, early = tie(late, loss, early)
    early_other = swap(early, "seg", 1)
    late = segment_step(late)
    late_other = swap(late, "seg", 1)

    squares = square_sum(early, early_other, late, late_other)
    squares = branch_sum(place, squares, branch_parts(squares, size))
    squares_other = swap(squares, "seg", 1)
    *updated, grad_norm = adam(
        place,
        (squares, squares_other),
        (early, early_other, late, late_other),
        (wide_master, down_master, gain_master, wide_first, down_first, gain_first,
         wide_second, down_second, gain_second),
        size,
    )
    return (
        loss[0, 0],
        grad_norm.reshape(()),
        *(x.reshape(-1) if k % 3 == 2 else x for k, x in enumerate(updated)),
    )


def solution(mesh):
    split, line = P("wide", None), P("wide")
    states = (split, split, line)
    return jax.shard_map(
        body,
        mesh=mesh,
        in_specs=(P("seg", "wide", None), P("seg", None, None), P("seg", None)) + states * 3,
        out_specs=(P(), P()) + states * 4,
        check_vma=False,
    )
```

```python
import functools
import math

import jax
import jax.numpy as jnp
from jax import lax
from jax.experimental import pallas as pl
from jax.experimental.pallas import tpu as pltpu
from jax.sharding import PartitionSpec as P

D = 384
HEADS = 8
HEAD = D // HEADS
FF = 1536
STEMS = 4
SAMPLES = 32
OUT = STEMS * SAMPLES
QKV = 3 * D
REST = D + FF + OUT
ADAM_STEP = 10
LANES = 128

NORM_EPS = 1e-05
ENERGY_EPS = 1e-05
BETA_ONE = 0.9
BETA_TWO = 0.999
ADAM_EPS = 1e-08
LEARN_RATE = 0.1
GAIN_RATE = 0.5
WEIGHT_DECAY = 0.01
CLIP_LIMIT = 0.001

BF = jnp.bfloat16
F32 = jnp.float32
SCALE = 1.0 / math.sqrt(HEAD)
LOG_TWO = math.log(2.0)
VMEM_LIMIT = 16 * 2**20


def swap(x, axis, mask):
    return lax.ppermute(x, axis, [(i, i ^ mask) for i in range(lax.axis_size(axis))])


def dot(left, right, left_dim=1, right_dim=0):
    return lax.dot_general(
        left,
        right,
        (((left_dim,), (right_dim,)), ((), ())),
        preferred_element_type=F32,
    )


def unit_rows(values):
    centred = values - jnp.mean(values, axis=-1, keepdims=True)
    spread = jnp.mean(centred * centred, axis=-1, keepdims=True)
    inverse = lax.rsqrt(spread + NORM_EPS)
    return centred * inverse, inverse


def call(kernel, operands, out_shape, flops, moved, place=(), scratch=(), in_specs=None,
         out_specs=None, aliases=None):
    here = pl.BlockSpec(memory_space=pltpu.VMEM)
    small = pl.BlockSpec(memory_space=pltpu.SMEM)
    return pl.pallas_call(
        kernel,
        out_shape=out_shape,
        in_specs=[small] * len(place) + (in_specs or [here] * len(operands)),
        out_specs=out_specs or jax.tree.map(lambda _: here, out_shape),
        scratch_shapes=scratch,
        input_output_aliases=aliases or {},
        compiler_params=pltpu.CompilerParams(vmem_limit_bytes=VMEM_LIMIT),
        cost_estimate=pl.CostEstimate(flops=flops, bytes_accessed=moved, transcendentals=0),
    )(*place, *operands)


def sds(shape, dtype):
    return jax.ShapeDtypeStruct(shape, dtype)


def gain_shape(size):
    count = 8 * D // size
    width = math.gcd(count, LANES)
    return count // width, width


def gain_places(size):
    tall, across = gain_shape(size)
    for owner in range(size):
        for row in range(tall):
            flat = (owner * tall + row) * across
            yield owner, row, flat // D, flat % D, across


def pack_kernel(size, place, wide, down, gains, first, rest):
    half = first.shape[0]
    same = place[0] == 0
    picked = jnp.where(same, wide[:half], wide[half:]).astype(BF)
    first[:, :QKV] = picked[:, :QKV]
    rest[:, :REST] = picked[:, QKV:]
    for part in range(4):
        row, other = half * part, half * (4 + part)
        piece = jnp.where(same, down[row : row + half], down[other : other + half])
        rest[:, REST + D * part : REST + D * (part + 1)] = piece.astype(BF)
    first[:, QKV:] = jnp.zeros((half, LANES), BF)
    tall, across = gain_shape(size)
    first[:tall, QKV : QKV + across] = jnp.where(same, gains[...], 0.0).astype(BF)


def pack(place, wide, down, gains, size):
    half = wide.shape[0] // 2
    return call(
        functools.partial(pack_kernel, size),
        (wide, down, gains.reshape(gain_shape(size))),
        (sds((half, QKV + LANES), BF), sds((half, REST + 4 * D), BF)),
        1000,
        4 * (wide.size + down.size),
        place=(place,),
    )


def start_kernel(size, place, own, mine, other, queries_t, own_unit, weights_t, gains, joined):
    core, position = place[0], place[1]
    half = mine.shape[1]
    for owner in range(size):
        slot = owner ^ position
        near, far = mine[slot], other[slot]
        row = 2 * owner * half
        joined[row : row + half] = jnp.where(core == 0, near, far)
        joined[row + half : row + 2 * half] = jnp.where(core == 0, far, near)
    for owner, row, vector, lane, across in gain_places(size):
        at = 2 * owner * half + row
        gains[vector : vector + 1, lane : lane + across] = joined[
            at : at + 1, QKV : QKV + across
        ].astype(F32)
    weights_t[...] = joined[:, :QKV].T
    hat, _ = unit_rows(own[...].astype(F32))
    own_unit[...] = hat.astype(BF)
    normed = (hat * gains[0:1] + gains[1:2]).astype(BF)
    found = dot(weights_t[:D], normed, 1, 1)
    queries_t[...] = (found * (SCALE / LOG_TWO)).astype(BF)


def start(place, own, mine, other, size):
    rows = own.shape[0]
    return call(
        functools.partial(start_kernel, size),
        (own, mine, other),
        (sds((D, rows), BF), sds((rows, D), BF), sds((QKV, D), BF), sds((8, D), F32)),
        2 * rows * D * D,
        rows * D * 8,
        place=(place,),
        scratch=[pltpu.VMEM((D, QKV + LANES), BF)],
    )


def heads_in_step(first, second, third):
    ahead, behind = first(0), None
    for h in range(HEADS):
        found = ahead
        if h + 1 < HEADS:
            ahead = first(h + 1)
        found = second(h, found)
        if behind is not None:
            third(h - 1, behind)
        behind = found
    third(HEADS - 1, behind)


def head_rows(h, offset=0, height=HEAD):
    return slice(offset + height * h, offset + height * (h + 1))


def over_blocks(count, visit):
    if count == 1:
        visit(0)
    else:
        lax.fori_loop(0, count, lambda block, carry: (visit(block), carry)[1], 0)


def attend_kernel(count, carried, *refs):
    queries_t, weights_t, gains = refs[:3]
    blocks = refs[3 : 3 + count]
    refs = refs[3 + count :]
    if carried:
        accum_in, top_in = refs[:2]
        refs = refs[2:]
    probs, keys_t, values_t, unit, tops, accum, top, joined = refs
    if carried:
        accum[...] = accum_in[...]
        top[...] = top_in[...]
    else:
        accum[...] = jnp.zeros_like(accum)
        top[...] = jnp.full_like(top, -1e30)
    for block in range(count):
        joined[block] = blocks[block][...]

    def visit(block):
        hat, _ = unit_rows(joined[block].astype(F32))
        unit[block] = hat.astype(BF)
        crossed = (hat * gains[2:3] + gains[3:4]).astype(BF)
        keys_t[block] = dot(weights_t[D : 2 * D], crossed, 1, 1).astype(BF)
        values_t[block] = dot(weights_t[2 * D :], crossed, 1, 1).astype(BF)
        ones = jnp.ones((16, crossed.shape[0]), BF)

        def score(h):
            return dot(keys_t[block, head_rows(h)], queries_t[head_rows(h)], 0, 0)

        def soften(h, scores):
            before = top[h : h + 1]
            newest = jnp.maximum(before, jnp.max(scores, axis=0, keepdims=True))
            top[h : h + 1] = newest
            weight = jnp.exp2(scores - newest).astype(BF)
            probs[block, h] = weight
            return weight, jnp.exp2(before - newest)

        def gather(h, found):
            weight, fade = found
            tall = head_rows(h, 0, 64)
            values = jnp.concatenate([values_t[block, head_rows(h)], ones], axis=0)
            accum[tall] = accum[tall] * fade + dot(values, weight)

        heads_in_step(score, soften, gather)
        tops[block] = top[...]

    over_blocks(count, visit)


def attend(blocks, queries_t, weights_t, gains, carry):
    count, rows = len(blocks), blocks[0].shape[0]
    tokens = queries_t.shape[1]
    return call(
        functools.partial(attend_kernel, count, carry is not None),
        (queries_t, weights_t, gains, *blocks, *(carry or ())),
        (
            sds((count, HEADS, rows, tokens), BF),
            sds((count, D, rows), BF),
            sds((count, D, rows), BF),
            sds((count, rows, D), BF),
            sds((count, HEADS, tokens), F32),
            sds((64 * HEADS, tokens), F32),
            sds((HEADS, tokens), F32),
        ),
        count * rows * tokens * D,
        count * rows * tokens,
        scratch=[pltpu.VMEM((count, rows, D), BF)],
    )


def unpack_kernel(size, place, *refs):
    high = size // 2
    rest, down, joined = refs[2 * high + 2 :]
    core, position = place[0], place[1]
    half = joined.shape[1]
    for side in range(2):
        pieces = refs[side * (high + 1) : (side + 1) * (high + 1)]
        for other in range(size):
            slot = 2 * (other ^ position) + (side ^ core)
            joined[slot] = pieces[other][...] if other < high else pieces[high][other - high]
    for owner in range(size):
        for side in range(2):
            slot = 2 * owner + side
            rest[slot * half : (slot + 1) * half] = joined[slot, :, :REST]
            for part in range(4):
                row = (4 * slot + part) * half
                down[row : row + half] = joined[
                    slot, :, REST + D * part : REST + D * (part + 1)
                ]


def unpack(place, pieces, size):
    half, across = pieces[0].shape
    return call(
        functools.partial(unpack_kernel, size),
        tuple(pieces),
        (sds((D, REST), BF), sds((FF, D), BF)),
        1000,
        4 * D * across,
        place=(place,),
        scratch=[pltpu.VMEM((2 * size, half, across), BF)],
    )


def row_part(part, rows):
    split = 3 * rows // 4
    return slice(split, rows) if part else slice(0, split)


def dense_kernel(part, inputs, accum, rest, down, gains, *refs):
    (attended_t, inverse_total, branch_out, third, third_inverse, normed_two, slope, hidden,
     ffn_out, out_rows, estimate) = refs[-11:]
    rows = row_part(part, inputs.shape[0])
    for h in range(HEADS):
        inverse = 1.0 / accum[64 * h + HEAD : 64 * h + HEAD + 1, rows]
        inverse_total[h : h + 1, rows] = inverse
        attended_t[HEAD * h : HEAD * (h + 1), rows] = (
            accum[64 * h : 64 * h + HEAD, rows] * inverse
        )
    branch = dot(attended_t[:, rows].astype(BF), rest[:, :D], 0, 0)
    branch_out[rows] = branch
    mid = inputs[rows].astype(F32) + gains[6:7] * branch
    hat, inverse = unit_rows(mid)
    third[rows] = hat
    third_inverse[rows] = inverse
    normed = (hat * gains[4:5] + gains[5:6]).astype(BF)
    normed_two[rows] = normed
    pre = dot(normed, rest[:, D : D + FF])
    gate = 0.5 * (1.0 + lax.erf(pre * math.sqrt(0.5)))
    hid = (pre * gate).astype(BF)
    hidden[rows] = hid
    bell = jnp.exp(-0.5 * pre * pre) * (1.0 / math.sqrt(2.0 * math.pi))
    slope[rows] = gate + pre * bell
    ffn = dot(hid, down[...])
    ffn_out[rows] = ffn
    out = (mid + gains[7:8] * ffn).astype(BF)
    out_rows[rows] = out
    estimate[...] = dot(out, rest[:, D + FF :]).astype(BF)


def dense_forward(part, inputs, accum, rest, down, gains, started):
    rows = inputs.shape[0]
    taken = row_part(part, rows)
    return call(
        functools.partial(dense_kernel, part),
        (inputs, accum, rest, down, gains, *started),
        (
            sds((D, rows), F32),
            sds((HEADS, rows), F32),
            sds((rows, D), F32),
            sds((rows, D), F32),
            sds((rows, 1), F32),
            sds((rows, D), BF),
            sds((rows, FF), F32),
            sds((rows, FF), BF),
            sds((rows, D), F32),
            sds((rows, D), BF),
            sds((taken.stop - taken.start, OUT), BF),
        ),
        rows * D * (D + 2 * FF + OUT),
        rows * FF * 4,
        aliases={5 + k: k for k in range(len(started))},
    )


def error_kernel(place, *refs):
    own, far, (targets, errors, energy) = refs[:2], refs[2:4], refs[4:]
    rows = errors.shape[0]
    row = lax.broadcasted_iota(jnp.int32, (8, OUT), 0)
    total = jnp.zeros((8, OUT), F32)
    for part in range(2):
        taken = row_part(part, rows)
        first = pl.multiple_of(place[1] * rows + taken.start, 8)
        wanted = targets[pl.ds(first, taken.stop - taken.start)]
        error = wanted - (own[part][...].astype(F32) + far[part][...].astype(F32))
        errors[taken] = error
        found = jnp.sum(error * error, axis=0, keepdims=True)
        clean = jnp.sum(wanted * wanted, axis=0, keepdims=True)
        total = total + jnp.where(row == 0, found, jnp.where(row == 1, clean, 0.0))
    energy[...] = total


def error_energy(place, own, far, targets):
    rows = own[0].shape[0] + own[1].shape[0]
    return call(
        error_kernel,
        (*own, *far, targets),
        (sds((rows, OUT), F32), sds((8, OUT), F32)),
        rows * OUT * 8,
        rows * OUT * 12,
        place=(place,),
    )


def ordered_sum(place, values, joined):
    size = joined.shape[0]
    for slot in range(size):
        joined[slot ^ place[1]] = values[slot]
    total = joined[0]
    for slot in range(1, size):
        total = total + joined[slot]
    return total


def stem_sums(values):
    stem = lax.broadcasted_iota(jnp.int32, values.shape, 1) // SAMPLES
    total = jnp.zeros_like(values)
    for k in range(STEMS):
        part = jnp.sum(jnp.where(stem == k, values, 0.0), axis=1, keepdims=True)
        total = jnp.where(stem == k, part, total)
    return total


def dense_back_kernel(segments, place, present, energies, errors, rest, down, gains, attended_t, branch_out,
                      third, third_inverse, slope, ffn_out, grad_est, grad_ffn, grad_pre,
                      grad_branch, grad_attended_t, delta, grad_gains, loss, joined):
    energy = ordered_sum(place, energies, joined)
    lane = lax.broadcasted_iota(jnp.int32, (1, OUT), 1)
    counted = jnp.zeros((1, OUT), F32)
    for k in range(STEMS):
        counted = jnp.where(lane // SAMPLES == k, present[0, k].astype(F32), counted)
    counted = counted * (10.0 / math.log(10.0) / (segments * STEMS))
    found = stem_sums(energy[0:1]) + ENERGY_EPS
    clean = stem_sums(energy[1:2]) + ENERGY_EPS
    terms = counted * (jnp.log(found) - jnp.log(clean))
    terms = jnp.where(lane % SAMPLES == 0, terms, 0.0)
    loss[...] = jnp.broadcast_to(jnp.sum(terms, axis=1, keepdims=True), loss.shape)
    low = (errors[...] * (-2.0 * counted / found)).astype(BF)
    grad_est[...] = low
    grad_out = dot(low, rest[:, D + FF :], 1, 1)
    grad_gains[3:4] = jnp.sum(grad_out * ffn_out[...], axis=0, keepdims=True)
    ffn = (grad_out * gains[7:8]).astype(BF)
    grad_ffn[...] = ffn
    hidden = dot(ffn, down[...], 1, 1).astype(BF)
    pre = (hidden.astype(F32) * slope[...]).astype(BF)
    grad_pre[...] = pre
    normed = dot(pre, rest[:, D : D + FF], 1, 1)
    hat = third[...]
    grad_gains[0:1] = jnp.sum(normed * hat, axis=0, keepdims=True)
    grad_gains[1:2] = jnp.sum(normed, axis=0, keepdims=True)
    scaled = normed * gains[4:5]
    grad_mid = grad_out + third_inverse[...] * (
        scaled
        - jnp.mean(scaled, axis=-1, keepdims=True)
        - hat * jnp.mean(scaled * hat, axis=-1, keepdims=True)
    )
    grad_gains[2:3] = jnp.sum(grad_mid * branch_out[...], axis=0, keepdims=True)
    branch = (grad_mid * gains[6:7]).astype(BF)
    grad_branch[...] = branch
    attended = dot(rest[:, :D], branch, 1, 1).astype(BF)
    grad_attended_t[...] = attended
    product = attended.astype(F32) * attended_t[...]
    for h in range(HEADS):
        delta[h : h + 1] = jnp.sum(product[head_rows(h)], axis=0, keepdims=True)


def dense_back(segments, place, present, energies, errors, rest, down, gains, attended_t, branch_out, third,
               third_inverse, slope, ffn_out):
    rows = errors.shape[0]
    return call(
        functools.partial(dense_back_kernel, segments),
        (energies, errors, rest, down, gains, attended_t, branch_out, third,
         third_inverse, slope, ffn_out),
        (
            sds((rows, OUT), BF),
            sds((rows, D), BF),
            sds((rows, FF), BF),
            sds((rows, D), BF),
            sds((D, rows), BF),
            sds((HEADS, rows), F32),
            sds((4, D), F32),
            sds((8, LANES), F32),
        ),
        2 * rows * D * (D + 2 * FF + OUT),
        rows * FF * 8,
        place=(place, present),
        scratch=[pltpu.VMEM(energies.shape, F32)],
    )


def deal(size, place, first, second, keep, send, owner, at):
    slot = owner ^ place[1]
    same = place[0] == 0
    keep[slot, :, at] = jnp.where(same, first, second).astype(BF)
    send[slot, :, at] = jnp.where(same, second, first).astype(BF)


def dense_weights_kernel(size, place, grad_est, grad_ffn, grad_pre, grad_branch, attended_t,
                         normed_two, hidden, out_rows, keep, send, wide, tall):
    half = keep.shape[1]
    wide[:, D + FF :] = dot(out_rows[...], grad_est[...], 0, 0)
    wide[:, D : D + FF] = dot(normed_two[...], grad_pre[...], 0, 0)
    wide[:, :D] = dot(attended_t[...].astype(BF), grad_branch[...])
    tall[...] = dot(hidden[...], grad_ffn[...], 0, 0)
    for owner in range(size):
        row = 2 * owner * half
        deal(
            size, place, wide[row : row + half], wide[row + half : row + 2 * half],
            keep, send, owner, slice(0, REST),
        )
        for part in range(4):
            first = (8 * owner + part) * half
            second = (8 * owner + 4 + part) * half
            deal(
                size, place, tall[first : first + half], tall[second : second + half],
                keep, send, owner, slice(REST + D * part, REST + D * (part + 1)),
            )


def dense_weights(place, grad_est, grad_ffn, grad_pre, grad_branch, attended_t, normed_two,
                  hidden, out_rows, size):
    rows = grad_est.shape[0]
    piece = (size, D // size // 2, REST + 4 * D)
    return call(
        functools.partial(dense_weights_kernel, size),
        (grad_est, grad_ffn, grad_pre, grad_branch, attended_t, normed_two, hidden, out_rows),
        (sds(piece, BF), sds(piece, BF)),
        2 * rows * D * (D + 2 * FF + OUT),
        rows * FF * 8,
        place=(place,),
        scratch=[pltpu.VMEM((D, REST), F32), pltpu.VMEM((FF, D), F32)],
    )


def attend_back_kernel(carried, probs, keys_t, values_t, tops, queries_t, delta, top,
                       inverse_total, grad_attended_t, *refs):
    if carried:
        refs[1][...] = refs[0][...]
    else:
        refs[0][...] = jnp.zeros_like(refs[0])
    grad_queries, grad_kv = refs[-2:]

    def visit(block):
        factor = jnp.exp2(tops[block] - top[...]) * inverse_total[...]
        shift = delta[...] * factor

        def begin(h):
            grad = grad_attended_t[head_rows(h)].astype(F32) * factor[h : h + 1]
            grad = grad.astype(BF)
            return grad, dot(values_t[block, head_rows(h)], grad, 0, 0)

        def turn(h, found):
            grad, grad_probs = found
            scores = probs[block, h].astype(F32) * (grad_probs - shift[h : h + 1])
            return grad, scores.astype(BF)

        def end(h, found):
            grad, scores = found
            at = head_rows(h)
            grad_queries[at] += dot(keys_t[block, at], scores)
            grad_kv[block, at] = (dot(queries_t[at], scores, 1, 1) * LOG_TWO).astype(BF)
            grad_kv[block, head_rows(h, D)] = dot(grad, probs[block, h], 1, 1).astype(BF)

        heads_in_step(begin, turn, end)

    over_blocks(probs.shape[0], visit)


def attend_back(saved, queries_t, delta, top, inverse_total, grad_attended_t, carry):
    probs, keys_t, values_t, tops = saved
    count, _, rows, tokens = probs.shape
    carry = () if carry is None else (carry,)
    return call(
        functools.partial(attend_back_kernel, len(carry)),
        (probs, keys_t, values_t, tops, queries_t, delta, top, inverse_total,
         grad_attended_t, *carry),
        (sds((D, tokens), F32), sds((count, 2 * D, rows), BF)),
        count * (8 * rows * tokens * D * 5),
        count * (HEADS * rows * tokens * 2),
    )


def finish_kernel(size, groups, place, grad_queries, own_unit, weights_t, gains, late,
                  *refs):
    grads, units = refs[:groups], refs[groups : 2 * groups]
    keep, send, moments, full, grad_gains = refs[2 * groups :]
    rows = own_unit.shape[0]
    ones = jnp.ones((rows, LANES), BF)
    query = (grad_queries[...] * SCALE).astype(BF)
    moments[:D] = dot(query, jnp.concatenate([own_unit[...], ones], axis=1))
    total = None
    for grad, unit in zip(grads, units):
        for block in range(grad.shape[0]):
            term = dot(grad[block], jnp.concatenate([unit[block], ones], axis=1))
            total = term if total is None else total + term
    moments[D:] = total
    for first, size_out, row in ((0, D, 0), (D, 2 * D, 2)):
        at = slice(first, first + size_out)
        moment = moments[at, :D]
        column = moments[at, D : D + 1]
        weight = weights_t[at].astype(F32)
        grad_gains[row : row + 1] = jnp.sum(weight * moment, axis=0, keepdims=True)
        grad_gains[row + 1 : row + 2] = jnp.sum(weight * column, axis=0, keepdims=True)
        product = moment * gains[row : row + 1] + column * gains[row + 1 : row + 2]
        full[:, at] = product.T
    grad_gains[4:8] = late[...]
    half = keep.shape[1]
    for owner in range(size):
        row = 2 * owner * half
        deal(
            size, place, full[row : row + half], full[row + half : row + 2 * half],
            keep, send, owner, slice(0, QKV),
        )
        slot = owner ^ place[1]
        keep[slot, :, QKV:] = jnp.zeros((half, LANES), BF)
        send[slot, :, QKV:] = jnp.zeros((half, LANES), BF)
    same = place[0] == 0
    for owner, row, vector, lane, across in gain_places(size):
        slot = owner ^ place[1]
        value = grad_gains[vector : vector + 1, lane : lane + across]
        at = slice(QKV, QKV + across)
        keep[slot, row : row + 1, at] = jnp.where(same, value, 0.0).astype(BF)
        send[slot, row : row + 1, at] = jnp.where(same, 0.0, value).astype(BF)


def finish(place, grad_queries, own_unit, weights_t, gains, late, grads, units, size):
    rows = own_unit.shape[0]
    piece = (size, D // size // 2, QKV + LANES)
    return call(
        functools.partial(finish_kernel, size, len(grads)),
        (grad_queries, own_unit, weights_t, gains, late, *grads, *units),
        (sds(piece, BF), sds(piece, BF)),
        2 * rows * D * QKV * size,
        rows * D * 2 * size,
        place=(place,),
        scratch=[
            pltpu.VMEM((QKV, D + LANES), F32),
            pltpu.VMEM((D, QKV), F32),
            pltpu.VMEM((8, D), F32),
        ],
    )


def square_kernel(*refs):
    total = jnp.zeros((1, 1), F32)
    for ref in refs[:-1]:
        values = ref[...].astype(F32)
        rows = jnp.sum(values * values, axis=0, keepdims=True)
        total = total + jnp.sum(rows, axis=1, keepdims=True)
    refs[-1][...] = jnp.broadcast_to(total, refs[-1].shape)


def square_sum(*parts):
    size = sum(x.size for x in parts)
    return call(square_kernel, parts, sds((8, LANES), F32), 2 * size, 2 * size)


def branch_sum_kernel(place, own, *refs):
    parts, total, joined = refs[:-2], refs[-2], refs[-1]
    for slot, part in enumerate(parts):
        value = part[...]
        if slot == 0:
            value = jnp.where(place[0] == 0, own[...], value)
        joined[slot ^ place[1]] = value
    found = joined[0]
    for slot in range(1, len(parts)):
        found = found + joined[slot]
    total[...] = found


def branch_sum(place, own, parts):
    return call(
        branch_sum_kernel,
        (own, *parts),
        sds(own.shape, F32),
        own.size,
        4 * own.size,
        place=(place,),
        scratch=[pltpu.VMEM((len(parts),) + own.shape, F32)],
    )


def bits(size):
    return [1 << k for k in range(size.bit_length() - 1)]


def masks(size):
    return sorted(range(1, size), key=lambda mask: (mask.bit_count(), mask))


def tie(*values):
    return lax.optimization_barrier(values)


def add_low(left, right):
    return (left.astype(F32) + right.astype(F32)).astype(BF)


def core_step(keep, send):
    return add_low(keep, swap(send, "seg", 1))


def branch_parts(values, size):
    segments, wide = lax.axis_size("seg"), 2 * size
    found = []
    for slot in range(size):
        pairs = []
        for seg in range(segments):
            mask = size + slot if seg % 2 else slot
            if mask:
                pairs += [(seg * wide + w, seg * wide + (w ^ mask)) for w in range(wide)]
        found.append(lax.ppermute(values, ("seg", "wide"), pairs))
    return found


def send_members(total, size):
    return [total[0]] + [swap(total[mask], "wide", mask) for mask in range(1, size)]


def sum_low(parts):
    return functools.reduce(jnp.add, [x.astype(F32) for x in parts]).astype(BF)


def exchange(values, size):
    return jnp.stack([values] + [swap(values, "wide", mask) for mask in range(1, size)])


def segment_step(total):
    for mask in bits(lax.axis_size("seg"))[1:]:
        total = add_low(total, swap(total, "seg", mask))
    return total


def adam_update(weight, grad, moment, second, rate):
    moment = BETA_ONE * moment + (1 - BETA_ONE) * grad
    second = BETA_TWO * second + (1 - BETA_TWO) * (grad * grad)
    fixed_one = moment * (rate / (1 - BETA_ONE**ADAM_STEP))
    fixed_two = second * (1 / (1 - BETA_TWO**ADAM_STEP))
    weight = weight * (1 - rate * WEIGHT_DECAY) - fixed_one / (jnp.sqrt(fixed_two) + ADAM_EPS)
    return (weight, moment, second)


def adam_chunks(size, half):
    tall, across = gain_shape(size)
    chunks = []
    for side in range(2):
        rows, ends = slice(4 * side * half, 4 * (side + 1) * half), slice(0, D)
        parts = [
            (slice((4 * side + k) * half, (4 * side + k + 1) * half), ends, 0,
             slice(REST + D * k, REST + D * (k + 1)))
            for k in range(4)
        ]
        chunks.append((1, side, rows, ends, parts))
        rows = slice(side * half, (side + 1) * half)
        parts = [
            (rows, slice(0, QKV), 1, slice(0, QKV)),
            (rows, slice(QKV, QKV + REST), 0, slice(0, REST)),
        ]
        chunks.append((0, side, rows, slice(0, QKV + REST), parts))
    rows, lanes = slice(0, tall), slice(0, across)
    chunks.append((2, 0, rows, lanes, [(rows, lanes, 1, slice(QKV, QKV + across))]))
    return chunks


def tiles(rows, lanes, source):
    high, across = rows.stop - rows.start, lanes.stop - lanes.start
    for row in range(0, high, 16):
        tall = min(16, high - row)
        for lane in range(0, across, D):
            part = min(D, across - lane)
            yield (
                (slice(rows.start + row, rows.start + row + tall),
                 slice(lanes.start + lane, lanes.start + lane + part)),
                (slice(row, row + tall),
                 slice(source.start + lane, source.start + lane + part)),
            )


def adam_kernel(size, place, squares, squares_other, early, early_other, late, late_other,
                *refs):
    states, outs, norm = [refs[k : k + 3] for k in (0, 3, 6)], refs[9:21], refs[21]
    held, sems = refs[22:34], refs[34]
    same = place[0] == 0
    grad_norm = jnp.sqrt(squares[0:1, 0:1] + squares_other[0:1, 0:1])
    norm[...] = grad_norm
    factor = jnp.minimum(1.0, CLIP_LIMIT / (grad_norm + 1e-06))
    copies, aligned = [], early.shape[0] % 16 == 0

    def send(source, target):
        copies.append(pltpu.make_async_copy(source, target, sems.at[len(copies)]))
        copies[-1].start()

    for index, side, rows, lanes, parts in adam_chunks(size, early.shape[0]):
        rate = GAIN_RATE if index == 2 else LEARN_RATE
        for part_rows, part_lanes, which, source in parts:
            own, other = (late, late_other) if which else (early, early_other)
            if side:
                own, other = other, own
            for here, there in tiles(part_rows, part_lanes, source):
                grad = jnp.where(same, own[there].astype(F32), other[there].astype(F32))
                weight, moment, second = (x[index][here] for x in states)
                found = adam_update(weight, grad * factor, moment, second, rate)
                for kind, value in enumerate((*found, found[0].astype(BF))):
                    held[3 * kind + index][here] = value
        if aligned:
            for slot in range(index, 12, 3):
                send(held[slot].at[rows, lanes], outs[slot].at[rows, lanes])
    if not aligned:
        for slot in range(12):
            send(held[slot], outs[slot])
    for copy in copies:
        copy.wait()


def adam(place, squares, grads, states, size):
    flat = gain_shape(size)
    states = [x.reshape(flat) if x.ndim == 1 else x for x in states]
    shapes = [x.shape for x in states[:3]]
    count = sum(x.size for x in states[:3])
    kinds = [(shape, F32) for shape in shapes] * 3 + [(shape, BF) for shape in shapes]
    outside = pl.BlockSpec(memory_space=pl.ANY)
    return call(
        functools.partial(adam_kernel, size),
        (*squares, *grads, *states),
        tuple(sds(*kind) for kind in kinds) + (sds((1, 1), F32),),
        20 * count,
        28 * count,
        place=(place,),
        out_specs=(outside,) * 12 + (pl.BlockSpec(memory_space=pltpu.VMEM),),
        scratch=[pltpu.VMEM(*kind) for kind in kinds]
        + [pltpu.SemaphoreType.DMA((4 * len(adam_chunks(size, grads[0].shape[0])),))],
    )


def body(
    encoded,
    targets,
    present,
    wide_master,
    down_master,
    gain_master,
    wide_first,
    down_first,
    gain_first,
    wide_second,
    down_second,
    gain_second,
):
    size = lax.axis_size("wide") // 2
    position = lax.axis_index("wide") % size
    core = lax.axis_index("seg") % 2
    place = jnp.stack([core, position]).astype(jnp.int32)
    own = encoded[0]
    far = {0: swap(own, "wide", size)}
    first, rest = pack(place, wide_master, down_master, gain_master, size)

    high = size // 2
    first_mine = jnp.stack([first] + [swap(first, "wide", mask) for mask in range(1, size)])
    low_mine = [rest] + [swap(rest, "wide", mask) for mask in range(1, high)]
    far[0], first_mine, *low_mine = tie(far[0], first_mine, *low_mine)
    first_other = swap(first_mine, "seg", 1)
    far[high] = swap(far[0], "wide", high)
    for mask in range(1, high):
        far[mask] = swap(far[0], "wide", mask)
    queries_t, own_unit, weights_t, gains = start(place, own, first_mine, first_other, size)

    high_mine = swap(jnp.stack(low_mine), "wide", high)
    order = [high, *range(1, high), *range(high + 1, size)]
    groups = [[0]] + [order[k : k + 2] for k in range(0, size - 1, 2)]

    carry = None
    saved, units = [], []
    for group in groups:
        if len(saved) == 1:
            near = [far[mask] for mask in range(1, high)]
            carry[0], far[high], near, *low_mine = tie(carry[0], far[high], near, *low_mine)
            far.update(zip(range(1, high), near))
            low_other = [swap(x, "seg", 1) for x in low_mine]
            for mask in range(1, high):
                far[high + mask] = swap(far[high], "wide", mask)
        probs, keys_t, values_t, unit, tops, *carry = attend(
            [far[mask] for mask in group], queries_t, weights_t, gains, carry
        )
        saved.append((probs, keys_t, values_t, tops))
        if len(saved) == 2:
            carry[0], *low_other = tie(carry[0], *low_other)
        units.append(unit)
    accum, top = carry
    accum, high_mine = tie(accum, high_mine)
    high_other = swap(high_mine, "seg", 1)
    pieces = (*low_mine, high_mine, *low_other, high_other)

    rest_all, down_all = unpack(place, pieces, size)
    started, own_parts, far_parts = (), [], []
    for part in range(2):
        *started, estimate = dense_forward(
            part, own, accum, rest_all, down_all, gains, started
        )
        own_parts.append(estimate)
        far_parts.append(swap(estimate, "wide", size))
    (attended_t, inverse_total, branch_out, third, third_inverse, normed_two, slope, hidden,
     ffn_out, out_rows) = started

    errors, energy = error_energy(place, own_parts, far_parts, targets[0])
    energy = exchange(energy, size)
    seg_count = lax.axis_size("seg")
    (grad_est, grad_ffn, grad_pre, grad_branch, grad_attended_t, delta, late_gains,
     loss) = dense_back(
        seg_count, place, present, energy, errors, rest_all, down_all, gains, attended_t, branch_out,
        third, third_inverse, slope, ffn_out,
    )
    keep, send = dense_weights(
        place, grad_est, grad_ffn, grad_pre, grad_branch, attended_t, normed_two, hidden,
        out_rows, size,
    )
    grad_attended_t, keep, send = tie(grad_attended_t, keep, send)

    early = core_step(keep, send)
    grad_queries, grads = None, []
    for k, item in enumerate(saved):
        grad_queries, grad_kv = attend_back(
            item, queries_t, delta, top, inverse_total, grad_attended_t, grad_queries
        )
        grads.append(grad_kv)
        if k == 0:
            grad_queries, early = tie(grad_queries, early)
            early = send_members(early, size)
    keep, send = finish(
        place, grad_queries, own_unit, weights_t, gains, late_gains, grads, units, size
    )
    keep, send, *early = tie(keep, send, *early)
    late = core_step(keep, send)
    early = segment_step(sum_low(early))
    late, loss = tie(late, loss)
    for mask in bits(seg_count):
        loss = loss + swap(loss, "seg", mask)
    late = sum_low(send_members(late, size))
    late, loss, early = tie(late, loss, early)
    early_other = swap(early, "seg", 1)
    late = segment_step(late)
    late_other = swap(late, "seg", 1)

    squares = square_sum(early, early_other, late, late_other)
    squares = branch_sum(place, squares, branch_parts(squares, size))
    squares_other = swap(squares, "seg", 1)
    *updated, grad_norm = adam(
        place,
        (squares, squares_other),
        (early, early_other, late, late_other),
        (wide_master, down_master, gain_master, wide_first, down_first, gain_first,
         wide_second, down_second, gain_second),
        size,
    )
    return (
        loss[0, 0],
        grad_norm.reshape(()),
        *(x.reshape(-1) if k % 3 == 2 else x for k, x in enumerate(updated)),
    )


def solution(mesh):
    split, line = P("wide", None), P("wide")
    states = (split, split, line)
    return jax.shard_map(
        body,
        mesh=mesh,
        in_specs=(P("seg", "wide", None), P("seg", None, None), P("seg", None)) + states * 3,
        out_specs=(P(), P()) + states * 4,
        check_vma=False,
    )
```

```python
import functools
import math

import jax
import jax.numpy as jnp
from jax import lax
from jax.experimental import pallas as pl
from jax.experimental.pallas import tpu as pltpu
from jax.sharding import PartitionSpec as P

D = 384
HEADS = 8
HEAD = D // HEADS
FF = 1536
STEMS = 4
SAMPLES = 32
OUT = STEMS * SAMPLES
QKV = 3 * D
REST = D + FF + OUT
ADAM_STEP = 10
LANES = 128

NORM_EPS = 1e-05
ENERGY_EPS = 1e-05
BETA_ONE = 0.9
BETA_TWO = 0.999
ADAM_EPS = 1e-08
LEARN_RATE = 0.1
GAIN_RATE = 0.5
WEIGHT_DECAY = 0.01
CLIP_LIMIT = 0.001

BF = jnp.bfloat16
F32 = jnp.float32
SCALE = 1.0 / math.sqrt(HEAD)
LOG_TWO = math.log(2.0)
VMEM_LIMIT = 16 * 2**20


def swap(x, axis, mask):
    return lax.ppermute(x, axis, [(i, i ^ mask) for i in range(lax.axis_size(axis))])


def dot(left, right, left_dim=1, right_dim=0):
    return lax.dot_general(
        left,
        right,
        (((left_dim,), (right_dim,)), ((), ())),
        preferred_element_type=F32,
    )


def unit_rows(values):
    centred = values - jnp.mean(values, axis=-1, keepdims=True)
    spread = jnp.mean(centred * centred, axis=-1, keepdims=True)
    inverse = lax.rsqrt(spread + NORM_EPS)
    return centred * inverse, inverse


def call(kernel, operands, out_shape, flops, moved, place=(), scratch=(), in_specs=None,
         out_specs=None, aliases=None):
    here = pl.BlockSpec(memory_space=pltpu.VMEM)
    small = pl.BlockSpec(memory_space=pltpu.SMEM)
    return pl.pallas_call(
        kernel,
        out_shape=out_shape,
        in_specs=[small] * len(place) + (in_specs or [here] * len(operands)),
        out_specs=out_specs or jax.tree.map(lambda _: here, out_shape),
        scratch_shapes=scratch,
        input_output_aliases=aliases or {},
        compiler_params=pltpu.CompilerParams(vmem_limit_bytes=VMEM_LIMIT),
        cost_estimate=pl.CostEstimate(flops=flops, bytes_accessed=moved, transcendentals=0),
    )(*place, *operands)


def sds(shape, dtype):
    return jax.ShapeDtypeStruct(shape, dtype)


def gain_shape(size):
    count = 8 * D // size
    width = math.gcd(count, LANES)
    return count // width, width


def gain_places(size):
    tall, across = gain_shape(size)
    for owner in range(size):
        for row in range(tall):
            flat = (owner * tall + row) * across
            yield owner, row, flat // D, flat % D, across


def pack_kernel(size, place, wide, down, gains, first, rest):
    half = first.shape[0]
    same = place[0] == 0
    picked = jnp.where(same, wide[:half], wide[half:]).astype(BF)
    first[:, :QKV] = picked[:, :QKV]
    rest[:, :REST] = picked[:, QKV:]
    for part in range(4):
        row, other = half * part, half * (4 + part)
        piece = jnp.where(same, down[row : row + half], down[other : other + half])
        rest[:, REST + D * part : REST + D * (part + 1)] = piece.astype(BF)
    first[:, QKV:] = jnp.zeros((half, LANES), BF)
    tall, across = gain_shape(size)
    first[:tall, QKV : QKV + across] = jnp.where(same, gains[...], 0.0).astype(BF)


def pack(place, wide, down, gains, size):
    half = wide.shape[0] // 2
    return call(
        functools.partial(pack_kernel, size),
        (wide, down, gains.reshape(gain_shape(size))),
        (sds((half, QKV + LANES), BF), sds((half, REST + 4 * D), BF)),
        1000,
        4 * (wide.size + down.size),
        place=(place,),
    )


def start_kernel(size, place, own, mine, other, queries_t, own_unit, weights_t, gains, joined):
    core, position = place[0], place[1]
    half = mine.shape[1]
    for owner in range(size):
        slot = owner ^ position
        near, far = mine[slot], other[slot]
        row = 2 * owner * half
        joined[row : row + half] = jnp.where(core == 0, near, far)
        joined[row + half : row + 2 * half] = jnp.where(core == 0, far, near)
    for owner, row, vector, lane, across in gain_places(size):
        at = 2 * owner * half + row
        gains[vector : vector + 1, lane : lane + across] = joined[
            at : at + 1, QKV : QKV + across
        ].astype(F32)
    weights_t[...] = joined[:, :QKV].T
    hat, _ = unit_rows(own[...].astype(F32))
    own_unit[...] = hat.astype(BF)
    normed = (hat * gains[0:1] + gains[1:2]).astype(BF)
    found = dot(weights_t[:D], normed, 1, 1)
    queries_t[...] = (found * (SCALE / LOG_TWO)).astype(BF)


def start(place, own, mine, other, size):
    rows = own.shape[0]
    return call(
        functools.partial(start_kernel, size),
        (own, mine, other),
        (sds((D, rows), BF), sds((rows, D), BF), sds((QKV, D), BF), sds((8, D), F32)),
        2 * rows * D * D,
        rows * D * 8,
        place=(place,),
        scratch=[pltpu.VMEM((D, QKV + LANES), BF)],
    )


def heads_in_step(first, second, third):
    ahead, behind = first(0), None
    for h in range(HEADS):
        found = ahead
        if h + 1 < HEADS:
            ahead = first(h + 1)
        found = second(h, found)
        if behind is not None:
            third(h - 1, behind)
        behind = found
    third(HEADS - 1, behind)


def head_rows(h, offset=0, height=HEAD):
    return slice(offset + height * h, offset + height * (h + 1))


def over_blocks(count, visit):
    if count == 1:
        visit(0)
    else:
        lax.fori_loop(0, count, lambda block, carry: (visit(block), carry)[1], 0)


def attend_kernel(count, carried, *refs):
    queries_t, weights_t, gains = refs[:3]
    blocks = refs[3 : 3 + count]
    refs = refs[3 + count :]
    if carried:
        accum_in, top_in = refs[:2]
        refs = refs[2:]
    probs, keys_t, values_t, unit, tops, accum, top, joined = refs
    if carried:
        accum[...] = accum_in[...]
        top[...] = top_in[...]
    else:
        accum[...] = jnp.zeros_like(accum)
        top[...] = jnp.full_like(top, -1e30)
    for block in range(count):
        joined[block] = blocks[block][...]

    def visit(block):
        hat, _ = unit_rows(joined[block].astype(F32))
        unit[block] = hat.astype(BF)
        crossed = (hat * gains[2:3] + gains[3:4]).astype(BF)
        keys_t[block] = dot(weights_t[D : 2 * D], crossed, 1, 1).astype(BF)
        values_t[block] = dot(weights_t[2 * D :], crossed, 1, 1).astype(BF)
        ones = jnp.ones((16, crossed.shape[0]), BF)

        def score(h):
            return dot(keys_t[block, head_rows(h)], queries_t[head_rows(h)], 0, 0)

        def soften(h, scores):
            before = top[h : h + 1]
            newest = jnp.maximum(before, jnp.max(scores, axis=0, keepdims=True))
            top[h : h + 1] = newest
            weight = jnp.exp2(scores - newest).astype(BF)
            probs[block, h] = weight
            return weight, jnp.exp2(before - newest)

        def gather(h, found):
            weight, fade = found
            tall = head_rows(h, 0, 64)
            values = jnp.concatenate([values_t[block, head_rows(h)], ones], axis=0)
            accum[tall] = accum[tall] * fade + dot(values, weight)

        heads_in_step(score, soften, gather)
        tops[block] = top[...]

    over_blocks(count, visit)


def attend(blocks, queries_t, weights_t, gains, carry):
    count, rows = len(blocks), blocks[0].shape[0]
    tokens = queries_t.shape[1]
    return call(
        functools.partial(attend_kernel, count, carry is not None),
        (queries_t, weights_t, gains, *blocks, *(carry or ())),
        (
            sds((count, HEADS, rows, tokens), BF),
            sds((count, D, rows), BF),
            sds((count, D, rows), BF),
            sds((count, rows, D), BF),
            sds((count, HEADS, tokens), F32),
            sds((64 * HEADS, tokens), F32),
            sds((HEADS, tokens), F32),
        ),
        count * rows * tokens * D,
        count * rows * tokens,
        scratch=[pltpu.VMEM((count, rows, D), BF)],
    )


def unpack_kernel(size, place, *refs):
    high = size // 2
    rest, down, joined = refs[2 * high + 2 :]
    core, position = place[0], place[1]
    half = joined.shape[1]
    for side in range(2):
        pieces = refs[side * (high + 1) : (side + 1) * (high + 1)]
        for other in range(size):
            slot = 2 * (other ^ position) + (side ^ core)
            joined[slot] = pieces[other][...] if other < high else pieces[high][other - high]
    for owner in range(size):
        for side in range(2):
            slot = 2 * owner + side
            rest[slot * half : (slot + 1) * half] = joined[slot, :, :REST]
            for part in range(4):
                row = (4 * slot + part) * half
                down[row : row + half] = joined[
                    slot, :, REST + D * part : REST + D * (part + 1)
                ]


def unpack(place, pieces, size):
    half, across = pieces[0].shape
    return call(
        functools.partial(unpack_kernel, size),
        tuple(pieces),
        (sds((D, REST), BF), sds((FF, D), BF)),
        1000,
        4 * D * across,
        place=(place,),
        scratch=[pltpu.VMEM((2 * size, half, across), BF)],
    )


def row_part(part, rows):
    split = 3 * rows // 4
    return slice(split, rows) if part else slice(0, split)


def dense_kernel(part, inputs, accum, rest, down, gains, *refs):
    (attended_t, inverse_total, branch_out, third, third_inverse, normed_two, slope, hidden,
     ffn_out, out_rows, estimate) = refs[-11:]
    rows = row_part(part, inputs.shape[0])
    for h in range(HEADS):
        inverse = 1.0 / accum[64 * h + HEAD : 64 * h + HEAD + 1, rows]
        inverse_total[h : h + 1, rows] = inverse
        attended_t[HEAD * h : HEAD * (h + 1), rows] = (
            accum[64 * h : 64 * h + HEAD, rows] * inverse
        )
    branch = dot(attended_t[:, rows].astype(BF), rest[:, :D], 0, 0)
    branch_out[rows] = branch
    mid = inputs[rows].astype(F32) + gains[6:7] * branch
    hat, inverse = unit_rows(mid)
    third[rows] = hat
    third_inverse[rows] = inverse
    normed = (hat * gains[4:5] + gains[5:6]).astype(BF)
    normed_two[rows] = normed
    pre = dot(normed, rest[:, D : D + FF])
    gate = 0.5 * (1.0 + lax.erf(pre * math.sqrt(0.5)))
    hid = (pre * gate).astype(BF)
    hidden[rows] = hid
    bell = jnp.exp(-0.5 * pre * pre) * (1.0 / math.sqrt(2.0 * math.pi))
    slope[rows] = gate + pre * bell
    ffn = dot(hid, down[...])
    ffn_out[rows] = ffn
    out = (mid + gains[7:8] * ffn).astype(BF)
    out_rows[rows] = out
    estimate[...] = dot(out, rest[:, D + FF :]).astype(BF)


def dense_forward(part, inputs, accum, rest, down, gains, started):
    rows = inputs.shape[0]
    taken = row_part(part, rows)
    return call(
        functools.partial(dense_kernel, part),
        (inputs, accum, rest, down, gains, *started),
        (
            sds((D, rows), F32),
            sds((HEADS, rows), F32),
            sds((rows, D), F32),
            sds((rows, D), F32),
            sds((rows, 1), F32),
            sds((rows, D), BF),
            sds((rows, FF), F32),
            sds((rows, FF), BF),
            sds((rows, D), F32),
            sds((rows, D), BF),
            sds((taken.stop - taken.start, OUT), BF),
        ),
        rows * D * (D + 2 * FF + OUT),
        rows * FF * 4,
        aliases={5 + k: k for k in range(len(started))},
    )


def error_kernel(place, *refs):
    own, far, (targets, errors, energy) = refs[:2], refs[2:4], refs[4:]
    rows = errors.shape[0]
    row = lax.broadcasted_iota(jnp.int32, (8, OUT), 0)
    total = jnp.zeros((8, OUT), F32)
    for part in range(2):
        taken = row_part(part, rows)
        first = pl.multiple_of(place[1] * rows + taken.start, 8)
        wanted = targets[pl.ds(first, taken.stop - taken.start)]
        error = wanted - (own[part][...].astype(F32) + far[part][...].astype(F32))
        errors[taken] = error
        found = jnp.sum(error * error, axis=0, keepdims=True)
        clean = jnp.sum(wanted * wanted, axis=0, keepdims=True)
        total = total + jnp.where(row == 0, found, jnp.where(row == 1, clean, 0.0))
    energy[...] = total


def error_energy(place, own, far, targets):
    rows = own[0].shape[0] + own[1].shape[0]
    return call(
        error_kernel,
        (*own, *far, targets),
        (sds((rows, OUT), F32), sds((8, OUT), F32)),
        rows * OUT * 8,
        rows * OUT * 12,
        place=(place,),
    )


def ordered_sum(place, values, joined):
    size = joined.shape[0]
    for slot in range(size):
        joined[slot ^ place[1]] = values[slot]
    total = joined[0]
    for slot in range(1, size):
        total = total + joined[slot]
    return total


def stem_sums(values):
    stem = lax.broadcasted_iota(jnp.int32, values.shape, 1) // SAMPLES
    total = jnp.zeros_like(values)
    for k in range(STEMS):
        part = jnp.sum(jnp.where(stem == k, values, 0.0), axis=1, keepdims=True)
        total = jnp.where(stem == k, part, total)
    return total


def dense_back_kernel(segments, place, present, energies, errors, rest, down, gains, attended_t, branch_out,
                      third, third_inverse, slope, ffn_out, grad_est, grad_ffn, grad_pre,
                      grad_branch, grad_attended_t, delta, grad_gains, loss, joined):
    energy = ordered_sum(place, energies, joined)
    lane = lax.broadcasted_iota(jnp.int32, (1, OUT), 1)
    counted = jnp.zeros((1, OUT), F32)
    for k in range(STEMS):
        counted = jnp.where(lane // SAMPLES == k, present[0, k].astype(F32), counted)
    counted = counted * (10.0 / math.log(10.0) / (segments * STEMS))
    found = stem_sums(energy[0:1]) + ENERGY_EPS
    clean = stem_sums(energy[1:2]) + ENERGY_EPS
    terms = counted * (jnp.log(found) - jnp.log(clean))
    terms = jnp.where(lane % SAMPLES == 0, terms, 0.0)
    loss[...] = jnp.broadcast_to(jnp.sum(terms, axis=1, keepdims=True), loss.shape)
    low = (errors[...] * (-2.0 * counted / found)).astype(BF)
    grad_est[...] = low
    grad_out = dot(low, rest[:, D + FF :], 1, 1)
    grad_gains[3:4] = jnp.sum(grad_out * ffn_out[...], axis=0, keepdims=True)
    ffn = (grad_out * gains[7:8]).astype(BF)
    grad_ffn[...] = ffn
    hidden = dot(ffn, down[...], 1, 1).astype(BF)
    pre = (hidden.astype(F32) * slope[...]).astype(BF)
    grad_pre[...] = pre
    normed = dot(pre, rest[:, D : D + FF], 1, 1)
    hat = third[...]
    grad_gains[0:1] = jnp.sum(normed * hat, axis=0, keepdims=True)
    grad_gains[1:2] = jnp.sum(normed, axis=0, keepdims=True)
    scaled = normed * gains[4:5]
    grad_mid = grad_out + third_inverse[...] * (
        scaled
        - jnp.mean(scaled, axis=-1, keepdims=True)
        - hat * jnp.mean(scaled * hat, axis=-1, keepdims=True)
    )
    grad_gains[2:3] = jnp.sum(grad_mid * branch_out[...], axis=0, keepdims=True)
    branch = (grad_mid * gains[6:7]).astype(BF)
    grad_branch[...] = branch
    attended = dot(rest[:, :D], branch, 1, 1).astype(BF)
    grad_attended_t[...] = attended
    product = attended.astype(F32) * attended_t[...]
    for h in range(HEADS):
        delta[h : h + 1] = jnp.sum(product[head_rows(h)], axis=0, keepdims=True)


def dense_back(segments, place, present, energies, errors, rest, down, gains, attended_t, branch_out, third,
               third_inverse, slope, ffn_out):
    rows = errors.shape[0]
    return call(
        functools.partial(dense_back_kernel, segments),
        (energies, errors, rest, down, gains, attended_t, branch_out, third,
         third_inverse, slope, ffn_out),
        (
            sds((rows, OUT), BF),
            sds((rows, D), BF),
            sds((rows, FF), BF),
            sds((rows, D), BF),
            sds((D, rows), BF),
            sds((HEADS, rows), F32),
            sds((4, D), F32),
            sds((8, LANES), F32),
        ),
        2 * rows * D * (D + 2 * FF + OUT),
        rows * FF * 8,
        place=(place, present),
        scratch=[pltpu.VMEM(energies.shape, F32)],
    )


def deal(size, place, first, second, keep, send, owner, at):
    slot = owner ^ place[1]
    same = place[0] == 0
    keep[slot, :, at] = jnp.where(same, first, second).astype(BF)
    send[slot, :, at] = jnp.where(same, second, first).astype(BF)


def dense_weights_kernel(size, place, grad_est, grad_ffn, grad_pre, grad_branch, attended_t,
                         normed_two, hidden, out_rows, keep, send, wide, tall):
    half = keep.shape[1]
    wide[:, D + FF :] = dot(out_rows[...], grad_est[...], 0, 0)
    wide[:, D : D + FF] = dot(normed_two[...], grad_pre[...], 0, 0)
    wide[:, :D] = dot(attended_t[...].astype(BF), grad_branch[...])
    tall[...] = dot(hidden[...], grad_ffn[...], 0, 0)
    for owner in range(size):
        row = 2 * owner * half
        deal(
            size, place, wide[row : row + half], wide[row + half : row + 2 * half],
            keep, send, owner, slice(0, REST),
        )
        for part in range(4):
            first = (8 * owner + part) * half
            second = (8 * owner + 4 + part) * half
            deal(
                size, place, tall[first : first + half], tall[second : second + half],
                keep, send, owner, slice(REST + D * part, REST + D * (part + 1)),
            )


def dense_weights(place, grad_est, grad_ffn, grad_pre, grad_branch, attended_t, normed_two,
                  hidden, out_rows, size):
    rows = grad_est.shape[0]
    piece = (size, D // size // 2, REST + 4 * D)
    return call(
        functools.partial(dense_weights_kernel, size),
        (grad_est, grad_ffn, grad_pre, grad_branch, attended_t, normed_two, hidden, out_rows),
        (sds(piece, BF), sds(piece, BF)),
        2 * rows * D * (D + 2 * FF + OUT),
        rows * FF * 8,
        place=(place,),
        scratch=[pltpu.VMEM((D, REST), F32), pltpu.VMEM((FF, D), F32)],
    )


def attend_back_kernel(carried, probs, keys_t, values_t, tops, queries_t, delta, top,
                       inverse_total, grad_attended_t, *refs):
    if carried:
        refs[1][...] = refs[0][...]
    else:
        refs[0][...] = jnp.zeros_like(refs[0])
    grad_queries, grad_kv = refs[-2:]

    def visit(block):
        factor = jnp.exp2(tops[block] - top[...]) * inverse_total[...]
        shift = delta[...] * factor

        def begin(h):
            grad = grad_attended_t[head_rows(h)].astype(F32) * factor[h : h + 1]
            grad = grad.astype(BF)
            return grad, dot(values_t[block, head_rows(h)], grad, 0, 0)

        def turn(h, found):
            grad, grad_probs = found
            scores = probs[block, h].astype(F32) * (grad_probs - shift[h : h + 1])
            return grad, scores.astype(BF)

        def end(h, found):
            grad, scores = found
            at = head_rows(h)
            grad_queries[at] += dot(keys_t[block, at], scores)
            grad_kv[block, at] = (dot(queries_t[at], scores, 1, 1) * LOG_TWO).astype(BF)
            grad_kv[block, head_rows(h, D)] = dot(grad, probs[block, h], 1, 1).astype(BF)

        heads_in_step(begin, turn, end)

    over_blocks(probs.shape[0], visit)


def attend_back(saved, queries_t, delta, top, inverse_total, grad_attended_t, carry):
    probs, keys_t, values_t, tops = saved
    count, _, rows, tokens = probs.shape
    carry = () if carry is None else (carry,)
    return call(
        functools.partial(attend_back_kernel, len(carry)),
        (probs, keys_t, values_t, tops, queries_t, delta, top, inverse_total,
         grad_attended_t, *carry),
        (sds((D, tokens), F32), sds((count, 2 * D, rows), BF)),
        count * (8 * rows * tokens * D * 5),
        count * (HEADS * rows * tokens * 2),
    )


def finish_kernel(size, groups, place, grad_queries, own_unit, weights_t, gains, late,
                  *refs):
    grads, units = refs[:groups], refs[groups : 2 * groups]
    keep, send, moments, full, grad_gains = refs[2 * groups :]
    rows = own_unit.shape[0]
    ones = jnp.ones((rows, LANES), BF)
    query = (grad_queries[...] * SCALE).astype(BF)
    moments[:D] = dot(query, jnp.concatenate([own_unit[...], ones], axis=1))
    total = None
    for grad, unit in zip(grads, units):
        for block in range(grad.shape[0]):
            term = dot(grad[block], jnp.concatenate([unit[block], ones], axis=1))
            total = term if total is None else total + term
    moments[D:] = total
    for first, size_out, row in ((0, D, 0), (D, 2 * D, 2)):
        at = slice(first, first + size_out)
        moment = moments[at, :D]
        column = moments[at, D : D + 1]
        weight = weights_t[at].astype(F32)
        grad_gains[row : row + 1] = jnp.sum(weight * moment, axis=0, keepdims=True)
        grad_gains[row + 1 : row + 2] = jnp.sum(weight * column, axis=0, keepdims=True)
        product = moment * gains[row : row + 1] + column * gains[row + 1 : row + 2]
        full[:, at] = product.T
    grad_gains[4:8] = late[...]
    half = keep.shape[1]
    for owner in range(size):
        row = 2 * owner * half
        deal(
            size, place, full[row : row + half], full[row + half : row + 2 * half],
            keep, send, owner, slice(0, QKV),
        )
        slot = owner ^ place[1]
        keep[slot, :, QKV:] = jnp.zeros((half, LANES), BF)
        send[slot, :, QKV:] = jnp.zeros((half, LANES), BF)
    same = place[0] == 0
    for owner, row, vector, lane, across in gain_places(size):
        slot = owner ^ place[1]
        value = grad_gains[vector : vector + 1, lane : lane + across]
        at = slice(QKV, QKV + across)
        keep[slot, row : row + 1, at] = jnp.where(same, value, 0.0).astype(BF)
        send[slot, row : row + 1, at] = jnp.where(same, 0.0, value).astype(BF)


def finish(place, grad_queries, own_unit, weights_t, gains, late, grads, units, size):
    rows = own_unit.shape[0]
    piece = (size, D // size // 2, QKV + LANES)
    return call(
        functools.partial(finish_kernel, size, len(grads)),
        (grad_queries, own_unit, weights_t, gains, late, *grads, *units),
        (sds(piece, BF), sds(piece, BF)),
        2 * rows * D * QKV * size,
        rows * D * 2 * size,
        place=(place,),
        scratch=[
            pltpu.VMEM((QKV, D + LANES), F32),
            pltpu.VMEM((D, QKV), F32),
            pltpu.VMEM((8, D), F32),
        ],
    )


def square_kernel(*refs):
    total = jnp.zeros((1, 1), F32)
    for ref in refs[:-1]:
        values = ref[...].astype(F32)
        rows = jnp.sum(values * values, axis=0, keepdims=True)
        total = total + jnp.sum(rows, axis=1, keepdims=True)
    refs[-1][...] = jnp.broadcast_to(total, refs[-1].shape)


def square_sum(*parts):
    size = sum(x.size for x in parts)
    return call(square_kernel, parts, sds((8, LANES), F32), 2 * size, 2 * size)


def branch_sum_kernel(place, own, *refs):
    parts, total, joined = refs[:-2], refs[-2], refs[-1]
    for slot, part in enumerate(parts):
        value = part[...]
        if slot == 0:
            value = jnp.where(place[0] == 0, own[...], value)
        joined[slot ^ place[1]] = value
    found = joined[0]
    for slot in range(1, len(parts)):
        found = found + joined[slot]
    total[...] = found


def branch_sum(place, own, parts):
    return call(
        branch_sum_kernel,
        (own, *parts),
        sds(own.shape, F32),
        own.size,
        4 * own.size,
        place=(place,),
        scratch=[pltpu.VMEM((len(parts),) + own.shape, F32)],
    )


def bits(size):
    return [1 << k for k in range(size.bit_length() - 1)]


def masks(size):
    return sorted(range(1, size), key=lambda mask: (mask.bit_count(), mask))


def tie(*values):
    return lax.optimization_barrier(values)


def add_low(left, right):
    return (left.astype(F32) + right.astype(F32)).astype(BF)


def core_step(keep, send):
    return add_low(keep, swap(send, "seg", 1))


def branch_parts(values, size):
    segments, wide = lax.axis_size("seg"), 2 * size
    found = []
    for slot in range(size):
        pairs = []
        for seg in range(segments):
            mask = size + slot if seg % 2 else slot
            if mask:
                pairs += [(seg * wide + w, seg * wide + (w ^ mask)) for w in range(wide)]
        found.append(lax.ppermute(values, ("seg", "wide"), pairs))
    return found


def send_members(total, size):
    return [total[0]] + [swap(total[mask], "wide", mask) for mask in [2, 3, 1]]


def sum_low(parts):
    return functools.reduce(jnp.add, [x.astype(F32) for x in parts]).astype(BF)


def exchange(values, size):
    return jnp.stack([values] + [swap(values, "wide", mask) for mask in range(1, size)])


def segment_step(total):
    for mask in bits(lax.axis_size("seg"))[1:]:
        total = add_low(total, swap(total, "seg", mask))
    return total


def adam_update(weight, grad, moment, second, rate):
    moment = BETA_ONE * moment + (1 - BETA_ONE) * grad
    second = BETA_TWO * second + (1 - BETA_TWO) * (grad * grad)
    fixed_one = moment * (rate / (1 - BETA_ONE**ADAM_STEP))
    fixed_two = second * (1 / (1 - BETA_TWO**ADAM_STEP))
    weight = weight * (1 - rate * WEIGHT_DECAY) - fixed_one / (jnp.sqrt(fixed_two) + ADAM_EPS)
    return (weight, moment, second)


def adam_chunks(size, half):
    tall, across = gain_shape(size)
    chunks = []
    for side in range(2):
        rows, ends = slice(4 * side * half, 4 * (side + 1) * half), slice(0, D)
        parts = [
            (slice((4 * side + k) * half, (4 * side + k + 1) * half), ends, 0,
             slice(REST + D * k, REST + D * (k + 1)))
            for k in range(4)
        ]
        chunks.append((1, side, rows, ends, parts))
        rows = slice(side * half, (side + 1) * half)
        parts = [
            (rows, slice(0, QKV), 1, slice(0, QKV)),
            (rows, slice(QKV, QKV + REST), 0, slice(0, REST)),
        ]
        chunks.append((0, side, rows, slice(0, QKV + REST), parts))
    rows, lanes = slice(0, tall), slice(0, across)
    chunks.append((2, 0, rows, lanes, [(rows, lanes, 1, slice(QKV, QKV + across))]))
    return chunks


def tiles(rows, lanes, source):
    high, across = rows.stop - rows.start, lanes.stop - lanes.start
    for row in range(0, high, 16):
        tall = min(16, high - row)
        for lane in range(0, across, D):
            part = min(D, across - lane)
            yield (
                (slice(rows.start + row, rows.start + row + tall),
                 slice(lanes.start + lane, lanes.start + lane + part)),
                (slice(row, row + tall),
                 slice(source.start + lane, source.start + lane + part)),
            )


def adam_kernel(size, place, squares, squares_other, early, early_other, late, late_other,
                *refs):
    states, outs, norm = [refs[k : k + 3] for k in (0, 3, 6)], refs[9:21], refs[21]
    held, sems = refs[22:34], refs[34]
    same = place[0] == 0
    grad_norm = jnp.sqrt(squares[0:1, 0:1] + squares_other[0:1, 0:1])
    norm[...] = grad_norm
    factor = jnp.minimum(1.0, CLIP_LIMIT / (grad_norm + 1e-06))
    copies, aligned = [], early.shape[0] % 16 == 0

    def send(source, target):
        copies.append(pltpu.make_async_copy(source, target, sems.at[len(copies)]))
        copies[-1].start()

    for index, side, rows, lanes, parts in adam_chunks(size, early.shape[0]):
        rate = GAIN_RATE if index == 2 else LEARN_RATE
        for part_rows, part_lanes, which, source in parts:
            own, other = (late, late_other) if which else (early, early_other)
            if side:
                own, other = other, own
            for here, there in tiles(part_rows, part_lanes, source):
                grad = jnp.where(same, own[there].astype(F32), other[there].astype(F32))
                weight, moment, second = (x[index][here] for x in states)
                found = adam_update(weight, grad * factor, moment, second, rate)
                for kind, value in enumerate((*found, found[0].astype(BF))):
                    held[3 * kind + index][here] = value
        if aligned:
            for slot in range(index, 12, 3):
                send(held[slot].at[rows, lanes], outs[slot].at[rows, lanes])
    if not aligned:
        for slot in range(12):
            send(held[slot], outs[slot])
    for copy in copies:
        copy.wait()


def adam(place, squares, grads, states, size):
    flat = gain_shape(size)
    states = [x.reshape(flat) if x.ndim == 1 else x for x in states]
    shapes = [x.shape for x in states[:3]]
    count = sum(x.size for x in states[:3])
    kinds = [(shape, F32) for shape in shapes] * 3 + [(shape, BF) for shape in shapes]
    outside = pl.BlockSpec(memory_space=pl.ANY)
    return call(
        functools.partial(adam_kernel, size),
        (*squares, *grads, *states),
        tuple(sds(*kind) for kind in kinds) + (sds((1, 1), F32),),
        20 * count,
        28 * count,
        place=(place,),
        out_specs=(outside,) * 12 + (pl.BlockSpec(memory_space=pltpu.VMEM),),
        scratch=[pltpu.VMEM(*kind) for kind in kinds]
        + [pltpu.SemaphoreType.DMA((4 * len(adam_chunks(size, grads[0].shape[0])),))],
    )


def body(
    encoded,
    targets,
    present,
    wide_master,
    down_master,
    gain_master,
    wide_first,
    down_first,
    gain_first,
    wide_second,
    down_second,
    gain_second,
):
    size = lax.axis_size("wide") // 2
    position = lax.axis_index("wide") % size
    core = lax.axis_index("seg") % 2
    place = jnp.stack([core, position]).astype(jnp.int32)
    own = encoded[0]
    far = {0: swap(own, "wide", size)}
    first, rest = pack(place, wide_master, down_master, gain_master, size)

    high = size // 2
    first_mine = jnp.stack([first] + [swap(first, "wide", mask) for mask in range(1, size)])
    low_mine = [rest] + [swap(rest, "wide", mask) for mask in range(1, high)]
    far[0], first_mine, *low_mine = tie(far[0], first_mine, *low_mine)
    first_other = swap(first_mine, "seg", 1)
    far[high] = swap(far[0], "wide", high)
    for mask in range(1, high):
        far[mask] = swap(far[0], "wide", mask)
    queries_t, own_unit, weights_t, gains = start(place, own, first_mine, first_other, size)

    high_mine = swap(jnp.stack(low_mine), "wide", high)
    order = [high, *range(1, high), *range(high + 1, size)]
    groups = [[0]] + [order[k : k + 2] for k in range(0, size - 1, 2)]

    carry = None
    saved, units = [], []
    for group in groups:
        if len(saved) == 1:
            near = [far[mask] for mask in range(1, high)]
            near, far[high], carry[0], *low_mine = tie(near, far[high], carry[0], *low_mine)
            far.update(zip(range(1, high), near))
            low_other = [swap(x, "seg", 1) for x in low_mine]
            for mask in range(1, high):
                far[high + mask] = swap(far[high], "wide", mask)
        probs, keys_t, values_t, unit, tops, *carry = attend(
            [far[mask] for mask in group], queries_t, weights_t, gains, carry
        )
        saved.append((probs, keys_t, values_t, tops))
        if len(saved) == 2:
            carry[0], *low_other = tie(carry[0], *low_other)
        units.append(unit)
    accum, top = carry
    accum, high_mine = tie(accum, high_mine)
    high_other = swap(high_mine, "seg", 1)
    pieces = (*low_mine, high_mine, *low_other, high_other)

    rest_all, down_all = unpack(place, pieces, size)
    started, own_parts, far_parts = (), [], []
    for part in range(2):
        *started, estimate = dense_forward(
            part, own, accum, rest_all, down_all, gains, started
        )
        own_parts.append(estimate)
        far_parts.append(swap(estimate, "wide", size))
    (attended_t, inverse_total, branch_out, third, third_inverse, normed_two, slope, hidden,
     ffn_out, out_rows) = started

    errors, energy = error_energy(place, own_parts, far_parts, targets[0])
    energy = exchange(energy, size)
    seg_count = lax.axis_size("seg")
    (grad_est, grad_ffn, grad_pre, grad_branch, grad_attended_t, delta, late_gains,
     loss) = dense_back(
        seg_count, place, present, energy, errors, rest_all, down_all, gains, attended_t, branch_out,
        third, third_inverse, slope, ffn_out,
    )
    keep, send = dense_weights(
        place, grad_est, grad_ffn, grad_pre, grad_branch, attended_t, normed_two, hidden,
        out_rows, size,
    )
    grad_attended_t, keep, send = tie(grad_attended_t, keep, send)

    early = core_step(keep, send)
    grad_queries, grads = None, []
    for k, item in enumerate(saved):
        grad_queries, grad_kv = attend_back(
            item, queries_t, delta, top, inverse_total, grad_attended_t, grad_queries
        )
        grads.append(grad_kv)
        if k == 0:
            grad_queries, early = tie(grad_queries, early)
            early = send_members(early, size)
    keep, send = finish(
        place, grad_queries, own_unit, weights_t, gains, late_gains, grads, units, size
    )
    keep, send, *early = tie(keep, send, *early)
    late = core_step(keep, send)
    early = segment_step(sum_low(early))
    late, loss = tie(late, loss)
    for mask in bits(seg_count):
        loss = loss + swap(loss, "seg", mask)
    late = sum_low(send_members(late, size))
    late, loss, early = tie(late, loss, early)
    early_other = swap(early, "seg", 1)
    late = segment_step(late)
    late_other = swap(late, "seg", 1)

    squares = square_sum(early, early_other, late, late_other)
    squares = branch_sum(place, squares, branch_parts(squares, size))
    squares_other = swap(squares, "seg", 1)
    *updated, grad_norm = adam(
        place,
        (squares, squares_other),
        (early, early_other, late, late_other),
        (wide_master, down_master, gain_master, wide_first, down_first, gain_first,
         wide_second, down_second, gain_second),
        size,
    )
    return (
        loss[0, 0],
        grad_norm.reshape(()),
        *(x.reshape(-1) if k % 3 == 2 else x for k, x in enumerate(updated)),
    )


def solution(mesh):
    split, line = P("wide", None), P("wide")
    states = (split, split, line)
    return jax.shard_map(
        body,
        mesh=mesh,
        in_specs=(P("seg", "wide", None), P("seg", None, None), P("seg", None)) + states * 3,
        out_specs=(P(), P()) + states * 4,
        check_vma=False,
    )
```

```python
import functools
import math

import jax
import jax.numpy as jnp
from jax import lax
from jax.experimental import pallas as pl
from jax.experimental.pallas import tpu as pltpu
from jax.sharding import PartitionSpec as P

D = 384
HEADS = 8
HEAD = D // HEADS
FF = 1536
STEMS = 4
SAMPLES = 32
OUT = STEMS * SAMPLES
QKV = 3 * D
REST = D + FF + OUT
ADAM_STEP = 10
LANES = 128

NORM_EPS = 1e-05
ENERGY_EPS = 1e-05
BETA_ONE = 0.9
BETA_TWO = 0.999
ADAM_EPS = 1e-08
LEARN_RATE = 0.1
GAIN_RATE = 0.5
WEIGHT_DECAY = 0.01
CLIP_LIMIT = 0.001

BF = jnp.bfloat16
F32 = jnp.float32
SCALE = 1.0 / math.sqrt(HEAD)
LOG_TWO = math.log(2.0)
VMEM_LIMIT = 16 * 2**20


def swap(x, axis, mask):
    return lax.ppermute(x, axis, [(i, i ^ mask) for i in range(lax.axis_size(axis))])


def dot(left, right, left_dim=1, right_dim=0):
    return lax.dot_general(
        left,
        right,
        (((left_dim,), (right_dim,)), ((), ())),
        preferred_element_type=F32,
    )


def unit_rows(values):
    centred = values - jnp.mean(values, axis=-1, keepdims=True)
    spread = jnp.mean(centred * centred, axis=-1, keepdims=True)
    inverse = lax.rsqrt(spread + NORM_EPS)
    return centred * inverse, inverse


def call(kernel, operands, out_shape, flops, moved, place=(), scratch=(), in_specs=None,
         out_specs=None, aliases=None):
    here = pl.BlockSpec(memory_space=pltpu.VMEM)
    small = pl.BlockSpec(memory_space=pltpu.SMEM)
    return pl.pallas_call(
        kernel,
        out_shape=out_shape,
        in_specs=[small] * len(place) + (in_specs or [here] * len(operands)),
        out_specs=out_specs or jax.tree.map(lambda _: here, out_shape),
        scratch_shapes=scratch,
        input_output_aliases=aliases or {},
        compiler_params=pltpu.CompilerParams(vmem_limit_bytes=VMEM_LIMIT),
        cost_estimate=pl.CostEstimate(flops=flops, bytes_accessed=moved, transcendentals=0),
    )(*place, *operands)


def sds(shape, dtype):
    return jax.ShapeDtypeStruct(shape, dtype)


def gain_shape(size):
    count = 8 * D // size
    width = math.gcd(count, LANES)
    return count // width, width


def gain_places(size):
    tall, across = gain_shape(size)
    for owner in range(size):
        for row in range(tall):
            flat = (owner * tall + row) * across
            yield owner, row, flat // D, flat % D, across


def pack_kernel(size, place, wide, down, gains, first, rest):
    half = first.shape[0]
    same = place[0] == 0
    picked = jnp.where(same, wide[:half], wide[half:]).astype(BF)
    first[:, :QKV] = picked[:, :QKV]
    rest[:, :REST] = picked[:, QKV:]
    for part in range(4):
        row, other = half * part, half * (4 + part)
        piece = jnp.where(same, down[row : row + half], down[other : other + half])
        rest[:, REST + D * part : REST + D * (part + 1)] = piece.astype(BF)
    first[:, QKV:] = jnp.zeros((half, LANES), BF)
    tall, across = gain_shape(size)
    first[:tall, QKV : QKV + across] = jnp.where(same, gains[...], 0.0).astype(BF)


def pack(place, wide, down, gains, size):
    half = wide.shape[0] // 2
    return call(
        functools.partial(pack_kernel, size),
        (wide, down, gains.reshape(gain_shape(size))),
        (sds((half, QKV + LANES), BF), sds((half, REST + 4 * D), BF)),
        1000,
        4 * (wide.size + down.size),
        place=(place,),
    )


def start_kernel(size, place, own, mine, other, queries_t, own_unit_t, weights_t, gains,
                 joined):
    core, position = place[0], place[1]
    half = mine.shape[1]
    for owner in range(size):
        slot = owner ^ position
        near, far = mine[slot], other[slot]
        row = 2 * owner * half
        joined[row : row + half] = jnp.where(core == 0, near, far)
        joined[row + half : row + 2 * half] = jnp.where(core == 0, far, near)
    for owner, row, vector, lane, across in gain_places(size):
        at = 2 * owner * half + row
        gains[vector : vector + 1, lane : lane + across] = joined[
            at : at + 1, QKV : QKV + across
        ].astype(F32)
    weights_t[...] = joined[:, :QKV].T
    hat, _ = unit_rows(own[...].astype(F32))
    own_unit_t[...] = hat.astype(BF).T
    normed = (hat * gains[0:1] + gains[1:2]).astype(BF)
    found = dot(weights_t[:D], normed, 1, 1)
    queries_t[...] = (found * (SCALE / LOG_TWO)).astype(BF)


def start(place, own, mine, other, size):
    rows = own.shape[0]
    return call(
        functools.partial(start_kernel, size),
        (own, mine, other),
        (
            sds((D, rows), BF),
            sds((D, rows), BF),
            sds((QKV, D), BF),
            sds((8, D), F32),
            sds((D, QKV + LANES), BF),
        ),
        2 * rows * D * D,
        rows * D * 8,
        place=(place,),
    )


def heads_in_step(first, second, third):
    ahead, behind = first(0), None
    for h in range(HEADS):
        found = ahead
        if h + 1 < HEADS:
            ahead = first(h + 1)
        found = second(h, found)
        if behind is not None:
            third(h - 1, behind)
        behind = found
    third(HEADS - 1, behind)


def head_rows(h, offset=0, height=HEAD):
    return slice(offset + height * h, offset + height * (h + 1))


def over_blocks(count, visit):
    if count == 1:
        visit(0)
    else:
        lax.fori_loop(0, count, lambda block, carry: (visit(block), carry)[1], 0)


def attend_kernel(count, carried, *refs):
    queries_t, weights_t, gains = refs[:3]
    blocks = refs[3 : 3 + count]
    refs = refs[3 + count :]
    if carried:
        accum_in, top_in = refs[:2]
        refs = refs[2:]
    probs, keys_t, values_t, unit_t, tops, accum, top, joined = refs
    if carried:
        accum[...] = accum_in[...]
        top[...] = top_in[...]
    else:
        accum[...] = jnp.zeros_like(accum)
        top[...] = jnp.full_like(top, -1e30)
    for block in range(count):
        joined[block] = blocks[block][...]

    def visit(block):
        hat, _ = unit_rows(joined[block].astype(F32))
        unit_t[block] = hat.astype(BF).T
        crossed = (hat * gains[2:3] + gains[3:4]).astype(BF)
        keys_t[block] = dot(weights_t[D : 2 * D], crossed, 1, 1).astype(BF)
        values_t[block] = dot(weights_t[2 * D :], crossed, 1, 1).astype(BF)
        ones = jnp.ones((16, crossed.shape[0]), BF)

        def score(h):
            return dot(keys_t[block, head_rows(h)], queries_t[head_rows(h)], 0, 0)

        def soften(h, scores):
            before = top[h : h + 1]
            newest = jnp.maximum(before, jnp.max(scores, axis=0, keepdims=True))
            top[h : h + 1] = newest
            weight = jnp.exp2(scores - newest).astype(BF)
            probs[block, h] = weight
            return weight, jnp.exp2(before - newest)

        def gather(h, found):
            weight, fade = found
            tall = head_rows(h, 0, 64)
            values = jnp.concatenate([values_t[block, head_rows(h)], ones], axis=0)
            accum[tall] = accum[tall] * fade + dot(values, weight)

        heads_in_step(score, soften, gather)
        tops[block] = top[...]

    over_blocks(count, visit)


def attend(blocks, queries_t, weights_t, gains, carry):
    count, rows = len(blocks), blocks[0].shape[0]
    tokens = queries_t.shape[1]
    return call(
        functools.partial(attend_kernel, count, carry is not None),
        (queries_t, weights_t, gains, *blocks, *(carry or ())),
        (
            sds((count, HEADS, rows, tokens), BF),
            sds((count, D, rows), BF),
            sds((count, D, rows), BF),
            sds((count, D, rows), BF),
            sds((count, HEADS, tokens), F32),
            sds((64 * HEADS, tokens), F32),
            sds((HEADS, tokens), F32),
        ),
        count * rows * tokens * D,
        count * rows * tokens,
        scratch=[pltpu.VMEM((count, rows, D), BF)],
    )


def unpack_kernel(size, place, *refs):
    high = size // 2
    rest, down, joined = refs[2 * high + 2 :]
    core, position = place[0], place[1]
    half = joined.shape[1]
    for side in range(2):
        pieces = refs[side * (high + 1) : (side + 1) * (high + 1)]
        for other in range(size):
            slot = 2 * (other ^ position) + (side ^ core)
            joined[slot] = pieces[other][...] if other < high else pieces[high][other - high]
    for owner in range(size):
        for side in range(2):
            slot = 2 * owner + side
            rest[slot * half : (slot + 1) * half] = joined[slot, :, :REST]
            for part in range(4):
                row = (4 * slot + part) * half
                down[row : row + half] = joined[
                    slot, :, REST + D * part : REST + D * (part + 1)
                ]


def unpack(place, pieces, size):
    half, across = pieces[0].shape
    return call(
        functools.partial(unpack_kernel, size),
        tuple(pieces),
        (sds((D, REST), BF), sds((FF, D), BF)),
        1000,
        4 * D * across,
        place=(place,),
        scratch=[pltpu.VMEM((2 * size, half, across), BF)],
    )


def row_part(part, rows):
    split = 3 * rows // 4
    return slice(split, rows) if part else slice(0, split)


def dense_kernel(part, inputs, accum, rest, down, gains, *refs):
    (attended_t, inverse_total, branch_out, third, third_inverse, normed_two, slope, hidden,
     ffn_out, out_rows, estimate) = refs[-11:]
    rows = row_part(part, inputs.shape[0])
    for h in range(HEADS):
        inverse = 1.0 / accum[64 * h + HEAD : 64 * h + HEAD + 1, rows]
        inverse_total[h : h + 1, rows] = inverse
        attended_t[HEAD * h : HEAD * (h + 1), rows] = (
            accum[64 * h : 64 * h + HEAD, rows] * inverse
        )
    branch = dot(attended_t[:, rows].astype(BF), rest[:, :D], 0, 0)
    branch_out[rows] = branch
    mid = inputs[rows].astype(F32) + gains[6:7] * branch
    hat, inverse = unit_rows(mid)
    third[rows] = hat
    third_inverse[rows] = inverse
    normed = (hat * gains[4:5] + gains[5:6]).astype(BF)
    normed_two[rows] = normed
    pre = dot(normed, rest[:, D : D + FF])
    gate = 0.5 * (1.0 + lax.erf(pre * math.sqrt(0.5)))
    hid = (pre * gate).astype(BF)
    hidden[rows] = hid
    bell = jnp.exp(-0.5 * pre * pre) * (1.0 / math.sqrt(2.0 * math.pi))
    slope[rows] = gate + pre * bell
    ffn = dot(hid, down[...])
    ffn_out[rows] = ffn
    out = (mid + gains[7:8] * ffn).astype(BF)
    out_rows[rows] = out
    estimate[...] = dot(out, rest[:, D + FF :]).astype(BF)


def dense_forward(part, inputs, accum, rest, down, gains, started):
    rows = inputs.shape[0]
    taken = row_part(part, rows)
    return call(
        functools.partial(dense_kernel, part),
        (inputs, accum, rest, down, gains, *started),
        (
            sds((D, rows), F32),
            sds((HEADS, rows), F32),
            sds((rows, D), F32),
            sds((rows, D), F32),
            sds((rows, 1), F32),
            sds((rows, D), BF),
            sds((rows, FF), F32),
            sds((rows, FF), BF),
            sds((rows, D), F32),
            sds((rows, D), BF),
            sds((taken.stop - taken.start, OUT), BF),
        ),
        rows * D * (D + 2 * FF + OUT),
        rows * FF * 4,
        aliases={5 + k: k for k in range(len(started))},
    )


def error_kernel(place, *refs):
    own, far, (targets, errors, energy) = refs[:2], refs[2:4], refs[4:]
    rows = errors.shape[0]
    row = lax.broadcasted_iota(jnp.int32, (8, OUT), 0)
    total = jnp.zeros((8, OUT), F32)
    for part in range(2):
        taken = row_part(part, rows)
        first = pl.multiple_of(place[1] * rows + taken.start, 8)
        wanted = targets[pl.ds(first, taken.stop - taken.start)]
        error = wanted - (own[part][...].astype(F32) + far[part][...].astype(F32))
        errors[taken] = error
        found = jnp.sum(error * error, axis=0, keepdims=True)
        clean = jnp.sum(wanted * wanted, axis=0, keepdims=True)
        total = total + jnp.where(row == 0, found, jnp.where(row == 1, clean, 0.0))
    energy[...] = total


def error_energy(place, own, far, targets):
    rows = own[0].shape[0] + own[1].shape[0]
    return call(
        error_kernel,
        (*own, *far, targets),
        (sds((rows, OUT), F32), sds((8, OUT), F32)),
        rows * OUT * 8,
        rows * OUT * 12,
        place=(place,),
    )


def ordered_sum(place, values, joined):
    size = joined.shape[0]
    for slot in range(size):
        joined[slot ^ place[1]] = values[slot]
    total = joined[0]
    for slot in range(1, size):
        total = total + joined[slot]
    return total


def stem_sums(values):
    stem = lax.broadcasted_iota(jnp.int32, values.shape, 1) // SAMPLES
    total = jnp.zeros_like(values)
    for k in range(STEMS):
        part = jnp.sum(jnp.where(stem == k, values, 0.0), axis=1, keepdims=True)
        total = jnp.where(stem == k, part, total)
    return total


def dense_back_kernel(segments, place, present, energies, errors, rest, down, gains, attended_t, branch_out,
                      third, third_inverse, slope, ffn_out, grad_est, grad_ffn, grad_pre,
                      grad_branch, grad_attended_t, delta, grad_gains, loss, joined):
    energy = ordered_sum(place, energies, joined)
    lane = lax.broadcasted_iota(jnp.int32, (1, OUT), 1)
    counted = jnp.zeros((1, OUT), F32)
    for k in range(STEMS):
        counted = jnp.where(lane // SAMPLES == k, present[0, k].astype(F32), counted)
    counted = counted * (10.0 / math.log(10.0) / (segments * STEMS))
    found = stem_sums(energy[0:1]) + ENERGY_EPS
    clean = stem_sums(energy[1:2]) + ENERGY_EPS
    terms = counted * (jnp.log(found) - jnp.log(clean))
    terms = jnp.where(lane % SAMPLES == 0, terms, 0.0)
    loss[...] = jnp.broadcast_to(jnp.sum(terms, axis=1, keepdims=True), loss.shape)
    low = (errors[...] * (-2.0 * counted / found)).astype(BF)
    grad_est[...] = low
    grad_out = dot(low, rest[:, D + FF :], 1, 1)
    grad_gains[3:4] = jnp.sum(grad_out * ffn_out[...], axis=0, keepdims=True)
    ffn = (grad_out * gains[7:8]).astype(BF)
    grad_ffn[...] = ffn
    hidden = dot(ffn, down[...], 1, 1).astype(BF)
    pre = (hidden.astype(F32) * slope[...]).astype(BF)
    grad_pre[...] = pre
    normed = dot(pre, rest[:, D : D + FF], 1, 1)
    hat = third[...]
    grad_gains[0:1] = jnp.sum(normed * hat, axis=0, keepdims=True)
    grad_gains[1:2] = jnp.sum(normed, axis=0, keepdims=True)
    scaled = normed * gains[4:5]
    grad_mid = grad_out + third_inverse[...] * (
        scaled
        - jnp.mean(scaled, axis=-1, keepdims=True)
        - hat * jnp.mean(scaled * hat, axis=-1, keepdims=True)
    )
    grad_gains[2:3] = jnp.sum(grad_mid * branch_out[...], axis=0, keepdims=True)
    branch = (grad_mid * gains[6:7]).astype(BF)
    grad_branch[...] = branch
    attended = dot(rest[:, :D], branch, 1, 1).astype(BF)
    grad_attended_t[...] = attended
    product = attended.astype(F32) * attended_t[...]
    for h in range(HEADS):
        delta[h : h + 1] = jnp.sum(product[head_rows(h)], axis=0, keepdims=True)


def dense_back(segments, place, present, energies, errors, rest, down, gains, attended_t, branch_out, third,
               third_inverse, slope, ffn_out):
    rows = errors.shape[0]
    return call(
        functools.partial(dense_back_kernel, segments),
        (energies, errors, rest, down, gains, attended_t, branch_out, third,
         third_inverse, slope, ffn_out),
        (
            sds((rows, OUT), BF),
            sds((rows, D), BF),
            sds((rows, FF), BF),
            sds((rows, D), BF),
            sds((D, rows), BF),
            sds((HEADS, rows), F32),
            sds((4, D), F32),
            sds((8, LANES), F32),
        ),
        2 * rows * D * (D + 2 * FF + OUT),
        rows * FF * 8,
        place=(place, present),
        scratch=[pltpu.VMEM(energies.shape, F32)],
    )


def deal(size, place, first, second, keep, send, owner, at):
    slot = owner ^ place[1]
    same = place[0] == 0
    keep[slot, :, at] = jnp.where(same, first, second).astype(BF)
    send[slot, :, at] = jnp.where(same, second, first).astype(BF)


def dense_weights_kernel(size, place, grad_est, grad_ffn, grad_pre, grad_branch, attended_t,
                         normed_two, hidden, out_rows, keep, send, wide, tall):
    half = keep.shape[1]
    wide[:, D + FF :] = dot(out_rows[...], grad_est[...], 0, 0)
    wide[:, D : D + FF] = dot(normed_two[...], grad_pre[...], 0, 0)
    wide[:, :D] = dot(attended_t[...].astype(BF), grad_branch[...])
    tall[...] = dot(hidden[...], grad_ffn[...], 0, 0)
    for owner in range(size):
        row = 2 * owner * half
        deal(
            size, place, wide[row : row + half], wide[row + half : row + 2 * half],
            keep, send, owner, slice(0, REST),
        )
        for part in range(4):
            first = (8 * owner + part) * half
            second = (8 * owner + 4 + part) * half
            deal(
                size, place, tall[first : first + half], tall[second : second + half],
                keep, send, owner, slice(REST + D * part, REST + D * (part + 1)),
            )


def dense_weights(place, grad_est, grad_ffn, grad_pre, grad_branch, attended_t, normed_two,
                  hidden, out_rows, size):
    rows = grad_est.shape[0]
    piece = (size, D // size // 2, REST + 4 * D)
    return call(
        functools.partial(dense_weights_kernel, size),
        (grad_est, grad_ffn, grad_pre, grad_branch, attended_t, normed_two, hidden, out_rows),
        (sds(piece, BF), sds(piece, BF)),
        2 * rows * D * (D + 2 * FF + OUT),
        rows * FF * 8,
        place=(place,),
        scratch=[pltpu.VMEM((D, REST), F32), pltpu.VMEM((FF, D), F32)],
    )


def attend_back_kernel(carried, probs, keys_t, values_t, tops, queries_t, delta, top,
                       inverse_total, grad_attended_t, *refs):
    if carried:
        refs[1][...] = refs[0][...]
    else:
        refs[0][...] = jnp.zeros_like(refs[0])
    grad_queries, grad_kv = refs[-2:]

    def visit(block):
        factor = jnp.exp2(tops[block] - top[...]) * inverse_total[...]
        shift = delta[...] * factor

        def begin(h):
            grad = grad_attended_t[head_rows(h)].astype(F32) * factor[h : h + 1]
            grad = grad.astype(BF)
            return grad, dot(values_t[block, head_rows(h)], grad, 0, 0)

        def turn(h, found):
            grad, grad_probs = found
            scores = probs[block, h].astype(F32) * (grad_probs - shift[h : h + 1])
            return grad, scores.astype(BF)

        def end(h, found):
            grad, scores = found
            at = head_rows(h)
            grad_queries[at] += dot(keys_t[block, at], scores)
            grad_kv[block, at] = (dot(queries_t[at], scores, 1, 1) * LOG_TWO).astype(BF)
            grad_kv[block, head_rows(h, D)] = dot(grad, probs[block, h], 1, 1).astype(BF)

        heads_in_step(begin, turn, end)

    over_blocks(probs.shape[0], visit)


def attend_back(saved, queries_t, delta, top, inverse_total, grad_attended_t, carry):
    probs, keys_t, values_t, tops = saved
    count, _, rows, tokens = probs.shape
    carry = () if carry is None else (carry,)
    return call(
        functools.partial(attend_back_kernel, len(carry)),
        (probs, keys_t, values_t, tops, queries_t, delta, top, inverse_total,
         grad_attended_t, *carry),
        (sds((D, tokens), F32), sds((count, 2 * D, rows), BF)),
        count * (8 * rows * tokens * D * 5),
        count * (HEADS * rows * tokens * 2),
    )


def unit_products(units, grads):
    total = None
    for k in range(0, len(units), 4):
        left = jnp.concatenate(units[k : k + 4], axis=1)
        left = jnp.concatenate([left, jnp.ones((16, left.shape[1]), BF)], axis=0)
        term = dot(left, jnp.concatenate(grads[k : k + 4], axis=1), 1, 1)
        total = term if total is None else total + term
    return total


def finish_kernel(size, groups, place, grad_queries, own_unit_t, weights, gains, late, *refs):
    grads, units = refs[:groups], refs[groups : 2 * groups]
    keep, send, full, grad_gains = refs[2 * groups :]
    query = (grad_queries[...] * SCALE).astype(BF)
    blocks = [(g, block) for g, grad in enumerate(grads) for block in range(grad.shape[0])]
    found = (
        unit_products([own_unit_t[...]], [query]),
        unit_products([units[g][b] for g, b in blocks], [grads[g][b] for g, b in blocks]),
    )
    columns = gains[...].T
    lane = lax.broadcasted_iota(jnp.int32, (D, LANES), 1)
    small = jnp.zeros((D, LANES), F32)
    for product, first, row in zip(found, (0, D), (0, 2)):
        at = slice(first, first + product.shape[1])
        moment, total = product[:D], product[D : D + 1]
        weight = weights[:, at].astype(F32)
        for k, terms in enumerate((weight * moment, weight * total)):
            small = jnp.where(lane == row + k, jnp.sum(terms, axis=1, keepdims=True), small)
        value = moment * columns[:, row : row + 1] + total * columns[:, row + 1 : row + 2]
        full[:, at] = value.astype(BF)
    grad_gains[:4] = small.T[:4]
    grad_gains[4:8] = late[...]
    half = keep.shape[1]
    for owner in range(size):
        row = 2 * owner * half
        deal(
            size, place, full[row : row + half], full[row + half : row + 2 * half],
            keep, send, owner, slice(0, QKV),
        )
    same = place[0] == 0
    tall, across = gain_shape(size)
    for owner in range(size):
        rows = [
            grad_gains[vector : vector + 1, lane : lane + across]
            for where, _, vector, lane, _ in gain_places(size)
            if where == owner
        ]
        block = jnp.concatenate(rows + [jnp.zeros((half - tall, across), F32)], axis=0)
        if across < LANES:
            block = jnp.concatenate([block, jnp.zeros((half, LANES - across), F32)], axis=1)
        slot = owner ^ place[1]
        keep[slot, :, QKV:] = jnp.where(same, block, 0.0).astype(BF)
        send[slot, :, QKV:] = jnp.where(same, 0.0, block).astype(BF)


def finish(place, grad_queries, own_unit_t, weights, gains, late, grads, units, size):
    rows = own_unit_t.shape[1]
    piece = (size, D // size // 2, QKV + LANES)
    return call(
        functools.partial(finish_kernel, size, len(grads)),
        (grad_queries, own_unit_t, weights, gains, late, *grads, *units),
        (sds(piece, BF), sds(piece, BF)),
        2 * rows * D * QKV * size,
        rows * D * 2 * size,
        place=(place,),
        scratch=[
            pltpu.VMEM((D, QKV), BF),
            pltpu.VMEM((8, D), F32),
        ],
    )


def square_kernel(*refs):
    total = jnp.zeros((1, 1), F32)
    for ref in refs[:-1]:
        values = ref[...].astype(F32)
        rows = jnp.sum(values * values, axis=0, keepdims=True)
        total = total + jnp.sum(rows, axis=1, keepdims=True)
    refs[-1][...] = jnp.broadcast_to(total, refs[-1].shape)


def square_sum(*parts):
    size = sum(x.size for x in parts)
    return call(square_kernel, parts, sds((8, LANES), F32), 2 * size, 2 * size)


def branch_sum_kernel(place, own, *refs):
    parts, total, joined = refs[:-2], refs[-2], refs[-1]
    for slot, part in enumerate(parts):
        value = part[...]
        if slot == 0:
            value = jnp.where(place[0] == 0, own[...], value)
        joined[slot ^ place[1]] = value
    found = joined[0]
    for slot in range(1, len(parts)):
        found = found + joined[slot]
    total[...] = found


def branch_sum(place, own, parts):
    return call(
        branch_sum_kernel,
        (own, *parts),
        sds(own.shape, F32),
        own.size,
        4 * own.size,
        place=(place,),
        scratch=[pltpu.VMEM((len(parts),) + own.shape, F32)],
    )


def bits(size):
    return [1 << k for k in range(size.bit_length() - 1)]


def masks(size):
    return sorted(range(1, size), key=lambda mask: (mask.bit_count(), mask))


def tie(*values):
    return lax.optimization_barrier(values)


def add_low(left, right):
    return (left.astype(F32) + right.astype(F32)).astype(BF)


def core_step(keep, send):
    return add_low(keep, swap(send, "seg", 1))


def branch_parts(values, size):
    segments, wide = lax.axis_size("seg"), 2 * size
    found = []
    for slot in range(size):
        pairs = []
        for seg in range(segments):
            mask = size + slot if seg % 2 else slot
            if mask:
                pairs += [(seg * wide + w, seg * wide + (w ^ mask)) for w in range(wide)]
        found.append(lax.ppermute(values, ("seg", "wide"), pairs))
    return found


def send_members(total, size):
    return [total[0]] + [swap(total[mask], "wide", mask) for mask in [2, 3, 1]]


def sum_low(parts):
    return functools.reduce(jnp.add, [x.astype(F32) for x in parts]).astype(BF)


def exchange(values, size):
    return jnp.stack([values] + [swap(values, "wide", mask) for mask in range(1, size)])


def segment_step(total):
    for mask in bits(lax.axis_size("seg"))[1:]:
        total = add_low(total, swap(total, "seg", mask))
    return total


def adam_update(weight, grad, moment, second, rate):
    moment = BETA_ONE * moment + (1 - BETA_ONE) * grad
    second = BETA_TWO * second + (1 - BETA_TWO) * (grad * grad)
    fixed_one = moment * (rate / (1 - BETA_ONE**ADAM_STEP))
    fixed_two = second * (1 / (1 - BETA_TWO**ADAM_STEP))
    weight = weight * (1 - rate * WEIGHT_DECAY) - fixed_one / (jnp.sqrt(fixed_two) + ADAM_EPS)
    return (weight, moment, second)


def adam_chunks(size, half):
    tall, across = gain_shape(size)
    chunks = []
    for side in range(2):
        rows, ends = slice(4 * side * half, 4 * (side + 1) * half), slice(0, D)
        parts = [
            (slice((4 * side + k) * half, (4 * side + k + 1) * half), ends, 0,
             slice(REST + D * k, REST + D * (k + 1)))
            for k in range(4)
        ]
        chunks.append((1, side, rows, ends, parts))
        rows = slice(side * half, (side + 1) * half)
        parts = [
            (rows, slice(0, QKV), 1, slice(0, QKV)),
            (rows, slice(QKV, QKV + REST), 0, slice(0, REST)),
        ]
        chunks.append((0, side, rows, slice(0, QKV + REST), parts))
    rows, lanes = slice(0, tall), slice(0, across)
    chunks.append((2, 0, rows, lanes, [(rows, lanes, 1, slice(QKV, QKV + across))]))
    return chunks


def tiles(rows, lanes, source):
    high, across = rows.stop - rows.start, lanes.stop - lanes.start
    for row in range(0, high, 16):
        tall = min(16, high - row)
        for lane in range(0, across, D):
            part = min(D, across - lane)
            yield (
                (slice(rows.start + row, rows.start + row + tall),
                 slice(lanes.start + lane, lanes.start + lane + part)),
                (slice(row, row + tall),
                 slice(source.start + lane, source.start + lane + part)),
            )


def adam_kernel(size, place, squares, squares_other, early, early_other, late, late_other,
                *refs):
    states, outs, norm = [refs[k : k + 3] for k in (0, 3, 6)], refs[9:21], refs[21]
    held, sems = refs[22:34], refs[34]
    same = place[0] == 0
    grad_norm = jnp.sqrt(squares[0:1, 0:1] + squares_other[0:1, 0:1])
    norm[...] = grad_norm
    factor = jnp.minimum(1.0, CLIP_LIMIT / (grad_norm + 1e-06))
    copies, aligned = [], early.shape[0] % 16 == 0

    def send(source, target):
        copies.append(pltpu.make_async_copy(source, target, sems.at[len(copies)]))
        copies[-1].start()

    for index, side, rows, lanes, parts in adam_chunks(size, early.shape[0]):
        rate = GAIN_RATE if index == 2 else LEARN_RATE
        for part_rows, part_lanes, which, source in parts:
            own, other = (late, late_other) if which else (early, early_other)
            if side:
                own, other = other, own
            for here, there in tiles(part_rows, part_lanes, source):
                grad = jnp.where(same, own[there].astype(F32), other[there].astype(F32))
                weight, moment, second = (x[index][here] for x in states)
                found = adam_update(weight, grad * factor, moment, second, rate)
                for kind, value in enumerate((*found, found[0].astype(BF))):
                    held[3 * kind + index][here] = value
        if aligned:
            for slot in range(index, 12, 3):
                send(held[slot].at[rows, lanes], outs[slot].at[rows, lanes])
    if not aligned:
        for slot in range(12):
            send(held[slot], outs[slot])
    for copy in copies:
        copy.wait()


def adam(place, squares, grads, states, size):
    flat = gain_shape(size)
    states = [x.reshape(flat) if x.ndim == 1 else x for x in states]
    shapes = [x.shape for x in states[:3]]
    count = sum(x.size for x in states[:3])
    kinds = [(shape, F32) for shape in shapes] * 3 + [(shape, BF) for shape in shapes]
    outside = pl.BlockSpec(memory_space=pl.ANY)
    return call(
        functools.partial(adam_kernel, size),
        (*squares, *grads, *states),
        tuple(sds(*kind) for kind in kinds) + (sds((1, 1), F32),),
        20 * count,
        28 * count,
        place=(place,),
        out_specs=(outside,) * 12 + (pl.BlockSpec(memory_space=pltpu.VMEM),),
        scratch=[pltpu.VMEM(*kind) for kind in kinds]
        + [pltpu.SemaphoreType.DMA((4 * len(adam_chunks(size, grads[0].shape[0])),))],
    )


def body(
    encoded,
    targets,
    present,
    wide_master,
    down_master,
    gain_master,
    wide_first,
    down_first,
    gain_first,
    wide_second,
    down_second,
    gain_second,
):
    size = lax.axis_size("wide") // 2
    position = lax.axis_index("wide") % size
    core = lax.axis_index("seg") % 2
    place = jnp.stack([core, position]).astype(jnp.int32)
    own = encoded[0]
    far = {0: swap(own, "wide", size)}
    first, rest = pack(place, wide_master, down_master, gain_master, size)

    high = size // 2
    first_mine = jnp.stack([first] + [swap(first, "wide", mask) for mask in range(1, size)])
    low_mine = [rest] + [swap(rest, "wide", mask) for mask in range(1, high)]
    far[0], first_mine, *low_mine = tie(far[0], first_mine, *low_mine)
    first_other = swap(first_mine, "seg", 1)
    far[high] = swap(far[0], "wide", high)
    for mask in range(1, high):
        far[mask] = swap(far[0], "wide", mask)
    queries_t, own_unit_t, weights_t, gains, first_all = start(place, own, first_mine, first_other, size)

    high_mine = swap(jnp.stack(low_mine), "wide", high)
    order = [high, *range(1, high), *range(high + 1, size)]
    groups = [[0]] + [order[k : k + 2] for k in range(0, size - 1, 2)]

    carry = None
    saved, units = [], []
    for group in groups:
        if len(saved) == 1:
            near = [far[mask] for mask in range(1, high)]
            near, far[high], carry[0], *low_mine = tie(near, far[high], carry[0], *low_mine)
            far.update(zip(range(1, high), near))
            low_other = [swap(x, "seg", 1) for x in low_mine]
            for mask in range(1, high):
                far[high + mask] = swap(far[high], "wide", mask)
        probs, keys_t, values_t, unit, tops, *carry = attend(
            [far[mask] for mask in group], queries_t, weights_t, gains, carry
        )
        saved.append((probs, keys_t, values_t, tops))
        if len(saved) == 2:
            carry[0], *low_other = tie(carry[0], *low_other)
        units.append(unit)
    accum, top = carry
    accum, high_mine = tie(accum, high_mine)
    high_other = swap(high_mine, "seg", 1)
    pieces = (*low_mine, high_mine, *low_other, high_other)

    rest_all, down_all = unpack(place, pieces, size)
    started, own_parts, far_parts = (), [], []
    for part in range(2):
        *started, estimate = dense_forward(
            part, own, accum, rest_all, down_all, gains, started
        )
        own_parts.append(estimate)
        far_parts.append(swap(estimate, "wide", size))
    (attended_t, inverse_total, branch_out, third, third_inverse, normed_two, slope, hidden,
     ffn_out, out_rows) = started

    errors, energy = error_energy(place, own_parts, far_parts, targets[0])
    energy = exchange(energy, size)
    seg_count = lax.axis_size("seg")
    (grad_est, grad_ffn, grad_pre, grad_branch, grad_attended_t, delta, late_gains,
     loss) = dense_back(
        seg_count, place, present, energy, errors, rest_all, down_all, gains, attended_t, branch_out,
        third, third_inverse, slope, ffn_out,
    )
    keep, send = dense_weights(
        place, grad_est, grad_ffn, grad_pre, grad_branch, attended_t, normed_two, hidden,
        out_rows, size,
    )
    grad_attended_t, keep, send = tie(grad_attended_t, keep, send)

    early = core_step(keep, send)
    grad_queries, grads = None, []
    for k, item in enumerate(saved):
        grad_queries, grad_kv = attend_back(
            item, queries_t, delta, top, inverse_total, grad_attended_t, grad_queries
        )
        grads.append(grad_kv)
        if k == 0:
            grad_queries, early = tie(grad_queries, early)
            early = send_members(early, size)
    keep, send = finish(
        place, grad_queries, own_unit_t, first_all, gains, late_gains, grads, units, size
    )
    keep, send, *early = tie(keep, send, *early)
    late = core_step(keep, send)
    early = segment_step(sum_low(early))
    late, loss = tie(late, loss)
    for mask in bits(seg_count):
        loss = loss + swap(loss, "seg", mask)
    late = sum_low(send_members(late, size))
    late, loss, early = tie(late, loss, early)
    early_other = swap(early, "seg", 1)
    late = segment_step(late)
    late_other = swap(late, "seg", 1)

    squares = square_sum(early, early_other, late, late_other)
    squares = branch_sum(place, squares, branch_parts(squares, size))
    squares_other = swap(squares, "seg", 1)
    *updated, grad_norm = adam(
        place,
        (squares, squares_other),
        (early, early_other, late, late_other),
        (wide_master, down_master, gain_master, wide_first, down_first, gain_first,
         wide_second, down_second, gain_second),
        size,
    )
    return (
        loss[0, 0],
        grad_norm.reshape(()),
        *(x.reshape(-1) if k % 3 == 2 else x for k, x in enumerate(updated)),
    )


def solution(mesh):
    split, line = P("wide", None), P("wide")
    states = (split, split, line)
    return jax.shard_map(
        body,
        mesh=mesh,
        in_specs=(P("seg", "wide", None), P("seg", None, None), P("seg", None)) + states * 3,
        out_specs=(P(), P()) + states * 4,
        check_vma=False,
    )
```

```python
import functools
import math

import jax
import jax.numpy as jnp
from jax import lax
from jax.experimental import pallas as pl
from jax.experimental.pallas import tpu as pltpu
from jax.sharding import PartitionSpec as P

D = 384
HEADS = 8
HEAD = D // HEADS
FF = 1536
STEMS = 4
SAMPLES = 32
OUT = STEMS * SAMPLES
QKV = 3 * D
REST = D + FF + OUT
ADAM_STEP = 10
LANES = 128

NORM_EPS = 1e-05
ENERGY_EPS = 1e-05
BETA_ONE = 0.9
BETA_TWO = 0.999
ADAM_EPS = 1e-08
LEARN_RATE = 0.1
GAIN_RATE = 0.5
WEIGHT_DECAY = 0.01
CLIP_LIMIT = 0.001

BF = jnp.bfloat16
F32 = jnp.float32
SCALE = 1.0 / math.sqrt(HEAD)
LOG_TWO = math.log(2.0)
VMEM_LIMIT = 16 * 2**20


def swap(x, axis, mask):
    return lax.ppermute(x, axis, [(i, i ^ mask) for i in range(lax.axis_size(axis))])


def dot(left, right, left_dim=1, right_dim=0):
    return lax.dot_general(
        left,
        right,
        (((left_dim,), (right_dim,)), ((), ())),
        preferred_element_type=F32,
    )


def unit_rows(values):
    centred = values - jnp.mean(values, axis=-1, keepdims=True)
    spread = jnp.mean(centred * centred, axis=-1, keepdims=True)
    inverse = lax.rsqrt(spread + NORM_EPS)
    return centred * inverse, inverse


def call(kernel, operands, out_shape, flops, moved, placed=False, scratch=(), out_specs=None,
         aliases=None):
    here = pl.BlockSpec(memory_space=pltpu.VMEM)
    size = lax.axis_size("wide") // 2

    def body_of(*refs):
        if placed:
            place = lax.axis_index("seg") % 2, lax.axis_index("wide") % size
            kernel(place, *refs)
        else:
            kernel(*refs)

    return pl.pallas_call(
        body_of,
        out_shape=out_shape,
        in_specs=[here] * len(operands),
        out_specs=out_specs or jax.tree.map(lambda _: here, out_shape),
        scratch_shapes=scratch,
        input_output_aliases=aliases or {},
        compiler_params=pltpu.CompilerParams(vmem_limit_bytes=VMEM_LIMIT),
        cost_estimate=pl.CostEstimate(flops=flops, bytes_accessed=moved, transcendentals=0),
    )(*operands)


def sds(shape, dtype):
    return jax.ShapeDtypeStruct(shape, dtype)


def gain_shape(size):
    count = 8 * D // size
    width = math.gcd(count, LANES)
    return count // width, width


def gain_places(size):
    tall, across = gain_shape(size)
    for owner in range(size):
        for row in range(tall):
            flat = (owner * tall + row) * across
            yield owner, row, flat // D, flat % D, across


def pack_kernel(size, place, wide, down, gains, first, rest):
    half = first.shape[0]
    same = place[0] == 0
    picked = jnp.where(same, wide[:half], wide[half:]).astype(BF)
    first[:, :QKV] = picked[:, :QKV]
    rest[:, :REST] = picked[:, QKV:]
    for part in range(4):
        row, other = half * part, half * (4 + part)
        piece = jnp.where(same, down[row : row + half], down[other : other + half])
        rest[:, REST + D * part : REST + D * (part + 1)] = piece.astype(BF)
    first[:, QKV:] = jnp.zeros((half, LANES), BF)
    tall, across = gain_shape(size)
    first[:tall, QKV : QKV + across] = jnp.where(same, gains[...], 0.0).astype(BF)


def pack(wide, down, gains, size):
    half = wide.shape[0] // 2
    return call(
        functools.partial(pack_kernel, size),
        (wide, down, gains.reshape(gain_shape(size))),
        (sds((half, QKV + LANES), BF), sds((half, REST + 4 * D), BF)),
        1000,
        4 * (wide.size + down.size),
        placed=True,
    )


def start_kernel(size, place, own, mine, other, queries_t, own_unit_t, weights_t, gains,
                 joined):
    core, position = place[0], place[1]
    half = mine.shape[1]
    for owner in range(size):
        slot = owner ^ position
        near, far = mine[slot], other[slot]
        row = 2 * owner * half
        joined[row : row + half] = jnp.where(core == 0, near, far)
        joined[row + half : row + 2 * half] = jnp.where(core == 0, far, near)
    for owner, row, vector, lane, across in gain_places(size):
        at = 2 * owner * half + row
        gains[vector : vector + 1, lane : lane + across] = joined[
            at : at + 1, QKV : QKV + across
        ].astype(F32)
    weights_t[...] = joined[:, :QKV].T
    hat, _ = unit_rows(own[...].astype(F32))
    own_unit_t[...] = hat.astype(BF).T
    normed = (hat * gains[0:1] + gains[1:2]).astype(BF)
    found = dot(weights_t[:D], normed, 1, 1)
    queries_t[...] = (found * (SCALE / LOG_TWO)).astype(BF)


def start(own, mine, other, size):
    rows = own.shape[0]
    return call(
        functools.partial(start_kernel, size),
        (own, mine, other),
        (
            sds((D, rows), BF),
            sds((D, rows), BF),
            sds((QKV, D), BF),
            sds((8, D), F32),
            sds((D, QKV + LANES), BF),
        ),
        2 * rows * D * D,
        rows * D * 8,
        placed=True,
    )


def heads_in_step(first, second, third):
    ahead, behind = first(0), None
    for h in range(HEADS):
        found = ahead
        if h + 1 < HEADS:
            ahead = first(h + 1)
        found = second(h, found)
        if behind is not None:
            third(h - 1, behind)
        behind = found
    third(HEADS - 1, behind)


def head_rows(h, offset=0, height=HEAD):
    return slice(offset + height * h, offset + height * (h + 1))


def over_blocks(count, visit):
    if count == 1:
        visit(0)
    else:
        lax.fori_loop(0, count, lambda block, carry: (visit(block), carry)[1], 0)


def attend_kernel(count, carried, *refs):
    queries_t, weights_t, gains = refs[:3]
    blocks = refs[3 : 3 + count]
    refs = refs[3 + count :]
    if carried:
        accum_in, top_in = refs[:2]
        refs = refs[2:]
    probs, keys_t, values_t, unit_t, tops, accum, top, joined = refs
    if carried:
        accum[...] = accum_in[...]
        top[...] = top_in[...]
    else:
        accum[...] = jnp.zeros_like(accum)
        top[...] = jnp.full_like(top, -1e30)
    for block in range(count):
        joined[block] = blocks[block][...]

    def visit(block):
        hat, _ = unit_rows(joined[block].astype(F32))
        unit_t[block] = hat.astype(BF).T
        crossed = (hat * gains[2:3] + gains[3:4]).astype(BF)
        keys_t[block] = dot(weights_t[D : 2 * D], crossed, 1, 1).astype(BF)
        values_t[block] = dot(weights_t[2 * D :], crossed, 1, 1).astype(BF)
        ones = jnp.ones((16, crossed.shape[0]), BF)

        def score(h):
            return dot(keys_t[block, head_rows(h)], queries_t[head_rows(h)], 0, 0)

        def soften(h, scores):
            before = top[h : h + 1]
            newest = jnp.maximum(before, jnp.max(scores, axis=0, keepdims=True))
            top[h : h + 1] = newest
            weight = jnp.exp2(scores - newest).astype(BF)
            probs[block, h] = weight
            return weight, jnp.exp2(before - newest)

        def gather(h, found):
            weight, fade = found
            tall = head_rows(h, 0, 64)
            values = jnp.concatenate([values_t[block, head_rows(h)], ones], axis=0)
            accum[tall] = accum[tall] * fade + dot(values, weight)

        heads_in_step(score, soften, gather)
        tops[block] = top[...]

    over_blocks(count, visit)


def attend(blocks, queries_t, weights_t, gains, carry):
    count, rows = len(blocks), blocks[0].shape[0]
    tokens = queries_t.shape[1]
    return call(
        functools.partial(attend_kernel, count, carry is not None),
        (queries_t, weights_t, gains, *blocks, *(carry or ())),
        (
            sds((count, HEADS, rows, tokens), BF),
            sds((count, D, rows), BF),
            sds((count, D, rows), BF),
            sds((count, D, rows), BF),
            sds((count, HEADS, tokens), F32),
            sds((64 * HEADS, tokens), F32),
            sds((HEADS, tokens), F32),
        ),
        count * rows * tokens * D,
        count * rows * tokens,
        scratch=[pltpu.VMEM((count, rows, D), BF)],
    )


def unpack_kernel(size, place, *refs):
    high = size // 2
    rest, down, joined = refs[2 * high + 2 :]
    core, position = place[0], place[1]
    half = joined.shape[1]
    for side in range(2):
        pieces = refs[side * (high + 1) : (side + 1) * (high + 1)]
        for other in range(size):
            slot = 2 * (other ^ position) + (side ^ core)
            joined[slot] = pieces[other][...] if other < high else pieces[high][other - high]
    for owner in range(size):
        for side in range(2):
            slot = 2 * owner + side
            rest[slot * half : (slot + 1) * half] = joined[slot, :, :REST]
            for part in range(4):
                row = (4 * slot + part) * half
                down[row : row + half] = joined[
                    slot, :, REST + D * part : REST + D * (part + 1)
                ]


def unpack(pieces, size):
    half, across = pieces[0].shape
    return call(
        functools.partial(unpack_kernel, size),
        tuple(pieces),
        (sds((D, REST), BF), sds((FF, D), BF)),
        1000,
        4 * D * across,
        placed=True,
        scratch=[pltpu.VMEM((2 * size, half, across), BF)],
    )


def row_part(part, rows):
    split = 3 * rows // 4
    return slice(split, rows) if part else slice(0, split)


def dense_kernel(part, inputs, accum, rest, down, gains, *refs):
    (attended_t, inverse_total, branch_out, third, third_inverse, normed_two, slope, hidden,
     ffn_out, out_rows, estimate) = refs[-11:]
    rows = row_part(part, inputs.shape[0])
    for h in range(HEADS):
        inverse = 1.0 / accum[64 * h + HEAD : 64 * h + HEAD + 1, rows]
        inverse_total[h : h + 1, rows] = inverse
        attended_t[HEAD * h : HEAD * (h + 1), rows] = (
            accum[64 * h : 64 * h + HEAD, rows] * inverse
        )
    branch = dot(attended_t[:, rows].astype(BF), rest[:, :D], 0, 0)
    branch_out[rows] = branch
    mid = inputs[rows].astype(F32) + gains[6:7] * branch
    hat, inverse = unit_rows(mid)
    third[rows] = hat
    third_inverse[rows] = inverse
    normed = (hat * gains[4:5] + gains[5:6]).astype(BF)
    normed_two[rows] = normed
    pre = dot(normed, rest[:, D : D + FF])
    gate = 0.5 * (1.0 + lax.erf(pre * math.sqrt(0.5)))
    hid = (pre * gate).astype(BF)
    hidden[rows] = hid
    bell = jnp.exp(-0.5 * pre * pre) * (1.0 / math.sqrt(2.0 * math.pi))
    slope[rows] = gate + pre * bell
    ffn = dot(hid, down[...])
    ffn_out[rows] = ffn
    out = (mid + gains[7:8] * ffn).astype(BF)
    out_rows[rows] = out
    estimate[...] = dot(out, rest[:, D + FF :]).astype(BF)


def dense_forward(part, inputs, accum, rest, down, gains, started):
    rows = inputs.shape[0]
    taken = row_part(part, rows)
    return call(
        functools.partial(dense_kernel, part),
        (inputs, accum, rest, down, gains, *started),
        (
            sds((D, rows), F32),
            sds((HEADS, rows), F32),
            sds((rows, D), F32),
            sds((rows, D), F32),
            sds((rows, 1), F32),
            sds((rows, D), BF),
            sds((rows, FF), F32),
            sds((rows, FF), BF),
            sds((rows, D), F32),
            sds((rows, D), BF),
            sds((taken.stop - taken.start, OUT), BF),
        ),
        rows * D * (D + 2 * FF + OUT),
        rows * FF * 4,
        aliases={5 + k: k for k in range(len(started))},
    )


def error_kernel(place, *refs):
    own, far, (targets, errors, energy) = refs[:2], refs[2:4], refs[4:]
    rows = errors.shape[0]
    row = lax.broadcasted_iota(jnp.int32, (8, OUT), 0)
    total = jnp.zeros((8, OUT), F32)
    for part in range(2):
        taken = row_part(part, rows)
        first = pl.multiple_of(place[1] * rows + taken.start, 8)
        wanted = targets[pl.ds(first, taken.stop - taken.start)]
        error = wanted - (own[part][...].astype(F32) + far[part][...].astype(F32))
        errors[taken] = error
        found = jnp.sum(error * error, axis=0, keepdims=True)
        clean = jnp.sum(wanted * wanted, axis=0, keepdims=True)
        total = total + jnp.where(row == 0, found, jnp.where(row == 1, clean, 0.0))
    energy[...] = total


def error_energy(own, far, targets):
    rows = own[0].shape[0] + own[1].shape[0]
    return call(
        error_kernel,
        (*own, *far, targets),
        (sds((rows, OUT), F32), sds((8, OUT), F32)),
        rows * OUT * 8,
        rows * OUT * 12,
        placed=True,
    )


def even_sum(parts):
    while len(parts) > 1:
        parts = [first + second for first, second in zip(parts[0::2], parts[1::2])]
    return parts[0]


def stem_sums(values):
    stem = lax.broadcasted_iota(jnp.int32, values.shape, 1) // SAMPLES
    total = jnp.zeros_like(values)
    for k in range(STEMS):
        part = jnp.sum(jnp.where(stem == k, values, 0.0), axis=1, keepdims=True)
        total = jnp.where(stem == k, part, total)
    return total


def dense_back_kernel(segments, present, energies, errors, rest, down, gains, attended_t, branch_out,
                      third, third_inverse, slope, ffn_out, grad_est, grad_ffn, grad_pre,
                      grad_branch, grad_attended_t, delta, grad_gains, loss):
    energy = even_sum([energies[slot] for slot in range(energies.shape[0])])
    lane = lax.broadcasted_iota(jnp.int32, (1, OUT), 1)
    counted = jnp.zeros((1, OUT), F32)
    for k in range(STEMS):
        counted = jnp.where(lane // SAMPLES == k, present[:, k : k + 1].astype(F32), counted)
    counted = counted * (10.0 / math.log(10.0) / (segments * STEMS))
    found = stem_sums(energy[0:1]) + ENERGY_EPS
    clean = stem_sums(energy[1:2]) + ENERGY_EPS
    terms = counted * (jnp.log(found) - jnp.log(clean))
    terms = jnp.where(lane % SAMPLES == 0, terms, 0.0)
    loss[...] = jnp.broadcast_to(jnp.sum(terms, axis=1, keepdims=True), loss.shape)
    low = (errors[...] * (-2.0 * counted / found)).astype(BF)
    grad_est[...] = low
    grad_out = dot(low, rest[:, D + FF :], 1, 1)
    grad_gains[3:4] = jnp.sum(grad_out * ffn_out[...], axis=0, keepdims=True)
    ffn = (grad_out * gains[7:8]).astype(BF)
    grad_ffn[...] = ffn
    hidden = dot(ffn, down[...], 1, 1).astype(BF)
    pre = (hidden.astype(F32) * slope[...]).astype(BF)
    grad_pre[...] = pre
    normed = dot(pre, rest[:, D : D + FF], 1, 1)
    hat = third[...]
    grad_gains[0:1] = jnp.sum(normed * hat, axis=0, keepdims=True)
    grad_gains[1:2] = jnp.sum(normed, axis=0, keepdims=True)
    scaled = normed * gains[4:5]
    grad_mid = grad_out + third_inverse[...] * (
        scaled
        - jnp.mean(scaled, axis=-1, keepdims=True)
        - hat * jnp.mean(scaled * hat, axis=-1, keepdims=True)
    )
    grad_gains[2:3] = jnp.sum(grad_mid * branch_out[...], axis=0, keepdims=True)
    branch = (grad_mid * gains[6:7]).astype(BF)
    grad_branch[...] = branch
    attended = dot(rest[:, :D], branch, 1, 1).astype(BF)
    grad_attended_t[...] = attended
    product = attended.astype(F32) * attended_t[...]
    for h in range(HEADS):
        delta[h : h + 1] = jnp.sum(product[head_rows(h)], axis=0, keepdims=True)


def dense_back(segments, present, energies, errors, rest, down, gains, attended_t, branch_out, third,
               third_inverse, slope, ffn_out):
    rows = errors.shape[0]
    return call(
        functools.partial(dense_back_kernel, segments),
        (present, energies, errors, rest, down, gains, attended_t, branch_out, third,
         third_inverse, slope, ffn_out),
        (
            sds((rows, OUT), BF),
            sds((rows, D), BF),
            sds((rows, FF), BF),
            sds((rows, D), BF),
            sds((D, rows), BF),
            sds((HEADS, rows), F32),
            sds((4, D), F32),
            sds((8, LANES), F32),
        ),
        2 * rows * D * (D + 2 * FF + OUT),
        rows * FF * 8,
    )


def deal(size, place, first, second, keep, send, owner, at):
    slot = owner ^ place[1]
    same = place[0] == 0
    keep[slot, :, at] = jnp.where(same, first, second).astype(BF)
    send[slot, :, at] = jnp.where(same, second, first).astype(BF)


def dense_weights_kernel(size, place, grad_est, grad_ffn, grad_pre, grad_branch, attended_t,
                         normed_two, hidden, out_rows, keep, send, wide, tall):
    half = keep.shape[1]
    wide[:, D + FF :] = dot(out_rows[...], grad_est[...], 0, 0)
    wide[:, D : D + FF] = dot(normed_two[...], grad_pre[...], 0, 0)
    wide[:, :D] = dot(attended_t[...].astype(BF), grad_branch[...])
    tall[...] = dot(hidden[...], grad_ffn[...], 0, 0)
    for owner in range(size):
        row = 2 * owner * half
        deal(
            size, place, wide[row : row + half], wide[row + half : row + 2 * half],
            keep, send, owner, slice(0, REST),
        )
        for part in range(4):
            first = (8 * owner + part) * half
            second = (8 * owner + 4 + part) * half
            deal(
                size, place, tall[first : first + half], tall[second : second + half],
                keep, send, owner, slice(REST + D * part, REST + D * (part + 1)),
            )


def dense_weights(grad_est, grad_ffn, grad_pre, grad_branch, attended_t, normed_two,
                  hidden, out_rows, size):
    rows = grad_est.shape[0]
    piece = (size, D // size // 2, REST + 4 * D)
    return call(
        functools.partial(dense_weights_kernel, size),
        (grad_est, grad_ffn, grad_pre, grad_branch, attended_t, normed_two, hidden, out_rows),
        (sds(piece, BF), sds(piece, BF)),
        2 * rows * D * (D + 2 * FF + OUT),
        rows * FF * 8,
        placed=True,
        scratch=[pltpu.VMEM((D, REST), F32), pltpu.VMEM((FF, D), F32)],
    )


def attend_back_kernel(carried, probs, keys_t, values_t, tops, queries_t, delta, top,
                       inverse_total, grad_attended_t, *refs):
    if carried:
        refs[1][...] = refs[0][...]
    else:
        refs[0][...] = jnp.zeros_like(refs[0])
    grad_queries, grad_kv = refs[-2:]

    def visit(block):
        factor = jnp.exp2(tops[block] - top[...]) * inverse_total[...]
        shift = delta[...] * factor

        def begin(h):
            grad = grad_attended_t[head_rows(h)].astype(F32) * factor[h : h + 1]
            grad = grad.astype(BF)
            return grad, dot(values_t[block, head_rows(h)], grad, 0, 0)

        def turn(h, found):
            grad, grad_probs = found
            scores = probs[block, h].astype(F32) * (grad_probs - shift[h : h + 1])
            return grad, scores.astype(BF)

        def end(h, found):
            grad, scores = found
            at = head_rows(h)
            grad_queries[at] += dot(keys_t[block, at], scores)
            grad_kv[block, at] = (dot(queries_t[at], scores, 1, 1) * LOG_TWO).astype(BF)
            grad_kv[block, head_rows(h, D)] = dot(grad, probs[block, h], 1, 1).astype(BF)

        heads_in_step(begin, turn, end)

    over_blocks(probs.shape[0], visit)


def attend_back(saved, queries_t, delta, top, inverse_total, grad_attended_t, carry):
    probs, keys_t, values_t, tops = saved
    count, _, rows, tokens = probs.shape
    carry = () if carry is None else (carry,)
    return call(
        functools.partial(attend_back_kernel, len(carry)),
        (probs, keys_t, values_t, tops, queries_t, delta, top, inverse_total,
         grad_attended_t, *carry),
        (sds((D, tokens), F32), sds((count, 2 * D, rows), BF)),
        count * (8 * rows * tokens * D * 5),
        count * (HEADS * rows * tokens * 2),
    )


def unit_products(units, grads):
    total = None
    for k in range(0, len(units), 4):
        left = jnp.concatenate(units[k : k + 4], axis=1)
        left = jnp.concatenate([left, jnp.ones((16, left.shape[1]), BF)], axis=0)
        term = dot(left, jnp.concatenate(grads[k : k + 4], axis=1), 1, 1)
        total = term if total is None else total + term
    return total


def finish_kernel(size, groups, place, grad_queries, own_unit_t, weights, gains, late, *refs):
    grads, units = refs[:groups], refs[groups : 2 * groups]
    keep, send, full, grad_gains = refs[2 * groups :]
    query = (grad_queries[...] * SCALE).astype(BF)
    blocks = [(g, block) for g, grad in enumerate(grads) for block in range(grad.shape[0])]
    found = (
        unit_products([own_unit_t[...]], [query]),
        unit_products([units[g][b] for g, b in blocks], [grads[g][b] for g, b in blocks]),
    )
    columns = gains[...].T
    lane = lax.broadcasted_iota(jnp.int32, (D, LANES), 1)
    small = jnp.zeros((D, LANES), F32)
    for product, first, row in zip(found, (0, D), (0, 2)):
        at = slice(first, first + product.shape[1])
        moment, total = product[:D], product[D : D + 1]
        weight = weights[:, at].astype(F32)
        for k, terms in enumerate((weight * moment, weight * total)):
            small = jnp.where(lane == row + k, jnp.sum(terms, axis=1, keepdims=True), small)
        value = moment * columns[:, row : row + 1] + total * columns[:, row + 1 : row + 2]
        full[:, at] = value.astype(BF)
    grad_gains[:4] = small.T[:4]
    grad_gains[4:8] = late[...]
    half = keep.shape[1]
    for owner in range(size):
        row = 2 * owner * half
        deal(
            size, place, full[row : row + half], full[row + half : row + 2 * half],
            keep, send, owner, slice(0, QKV),
        )
    same = place[0] == 0
    tall, across = gain_shape(size)
    for owner in range(size):
        rows = [
            grad_gains[vector : vector + 1, lane : lane + across]
            for where, _, vector, lane, _ in gain_places(size)
            if where == owner
        ]
        block = jnp.concatenate(rows + [jnp.zeros((half - tall, across), F32)], axis=0)
        if across < LANES:
            block = jnp.concatenate([block, jnp.zeros((half, LANES - across), F32)], axis=1)
        slot = owner ^ place[1]
        keep[slot, :, QKV:] = jnp.where(same, block, 0.0).astype(BF)
        send[slot, :, QKV:] = jnp.where(same, 0.0, block).astype(BF)


def finish(grad_queries, own_unit_t, weights, gains, late, grads, units, size):
    rows = own_unit_t.shape[1]
    piece = (size, D // size // 2, QKV + LANES)
    return call(
        functools.partial(finish_kernel, size, len(grads)),
        (grad_queries, own_unit_t, weights, gains, late, *grads, *units),
        (sds(piece, BF), sds(piece, BF)),
        2 * rows * D * QKV * size,
        rows * D * 2 * size,
        placed=True,
        scratch=[
            pltpu.VMEM((D, QKV), BF),
            pltpu.VMEM((8, D), F32),
        ],
    )


def square_kernel(place, *refs):
    found = []
    for ref in refs[:4]:
        values = ref[...].astype(F32)
        rows = jnp.sum(values * values, axis=0, keepdims=True)
        found.append(jnp.sum(rows, axis=1, keepdims=True))
    total = jnp.broadcast_to(even_sum(found), refs[4].shape)
    refs[4][...] = total
    refs[5][...] = jnp.where(place[0] == 0, total, 0.0)


def square_sum(*parts):
    size = sum(x.size for x in parts)
    shape = sds((8, LANES), F32)
    return call(square_kernel, parts, (shape, shape), 2 * size, 2 * size, placed=True)


def bits(size):
    return [1 << k for k in range(size.bit_length() - 1)]


def masks(size):
    return sorted(range(1, size), key=lambda mask: (mask.bit_count(), mask))


def tie(*values):
    return lax.optimization_barrier(values)


def add_low(left, right):
    return (left.astype(F32) + right.astype(F32)).astype(BF)


def core_step(keep, send):
    return add_low(keep, swap(send, "seg", 1))


def branch_parts(values, size):
    segments, wide = lax.axis_size("seg"), 2 * size
    found = []
    for slot in range(size):
        pairs = []
        for seg in range(segments):
            mask = size + slot if seg % 2 else slot
            if mask:
                pairs += [(seg * wide + w, seg * wide + (w ^ mask)) for w in range(wide)]
        found.append(lax.ppermute(values, ("seg", "wide"), pairs))
    return found


def send_members(total, size):
    return [total[0]] + [swap(total[mask], "wide", mask) for mask in [2, 3, 1]]


def sum_low(parts):
    return functools.reduce(jnp.add, [x.astype(F32) for x in parts]).astype(BF)


def exchange(values, size):
    return jnp.stack([values] + [swap(values, "wide", mask) for mask in range(1, size)])


def segment_step(total):
    for mask in bits(lax.axis_size("seg"))[1:]:
        total = add_low(total, swap(total, "seg", mask))
    return total


def adam_update(weight, grad, moment, second, rate):
    moment = BETA_ONE * moment + (1 - BETA_ONE) * grad
    second = BETA_TWO * second + (1 - BETA_TWO) * (grad * grad)
    fixed_one = moment * (rate / (1 - BETA_ONE**ADAM_STEP))
    fixed_two = second * (1 / (1 - BETA_TWO**ADAM_STEP))
    weight = weight * (1 - rate * WEIGHT_DECAY) - fixed_one / (jnp.sqrt(fixed_two) + ADAM_EPS)
    return (weight, moment, second)


def adam_chunks(size, half):
    tall, across = gain_shape(size)
    chunks = []
    for side in range(2):
        rows, ends = slice(4 * side * half, 4 * (side + 1) * half), slice(0, D)
        parts = [
            (slice((4 * side + k) * half, (4 * side + k + 1) * half), ends, 0,
             slice(REST + D * k, REST + D * (k + 1)))
            for k in range(4)
        ]
        chunks.append((1, side, rows, ends, parts))
        rows = slice(side * half, (side + 1) * half)
        parts = [
            (rows, slice(0, QKV), 1, slice(0, QKV)),
            (rows, slice(QKV, QKV + REST), 0, slice(0, REST)),
        ]
        chunks.append((0, side, rows, slice(0, QKV + REST), parts))
    rows, lanes = slice(0, tall), slice(0, across)
    chunks.append((2, 0, rows, lanes, [(rows, lanes, 1, slice(QKV, QKV + across))]))
    return chunks


def tiles(rows, lanes, source):
    high, across = rows.stop - rows.start, lanes.stop - lanes.start
    for row in range(0, high, 16):
        tall = min(16, high - row)
        for lane in range(0, across, D):
            part = min(D, across - lane)
            yield (
                (slice(rows.start + row, rows.start + row + tall),
                 slice(lanes.start + lane, lanes.start + lane + part)),
                (slice(row, row + tall),
                 slice(source.start + lane, source.start + lane + part)),
            )


def adam_kernel(size, place, squares, squares_other, early, early_other, late, late_other,
                *refs):
    states, outs, norm = [refs[k : k + 3] for k in (0, 3, 6)], refs[9:21], refs[21]
    held, sems = refs[22:34], refs[34]
    same = place[0] == 0
    grad_norm = jnp.sqrt(squares[0:1, 0:1] + squares_other[0:1, 0:1])
    norm[...] = grad_norm
    factor = jnp.minimum(1.0, CLIP_LIMIT / (grad_norm + 1e-06))
    copies, aligned = [], early.shape[0] % 16 == 0

    def send(source, target):
        copies.append(pltpu.make_async_copy(source, target, sems.at[len(copies)]))
        copies[-1].start()

    for index, side, rows, lanes, parts in adam_chunks(size, early.shape[0]):
        rate = GAIN_RATE if index == 2 else LEARN_RATE
        for part_rows, part_lanes, which, source in parts:
            own, other = (late, late_other) if which else (early, early_other)
            if side:
                own, other = other, own
            for here, there in tiles(part_rows, part_lanes, source):
                grad = jnp.where(same, own[there].astype(F32), other[there].astype(F32))
                weight, moment, second = (x[index][here] for x in states)
                found = adam_update(weight, grad * factor, moment, second, rate)
                for kind, value in enumerate((*found, found[0].astype(BF))):
                    held[3 * kind + index][here] = value
        if aligned:
            for slot in range(index, 12, 3):
                send(held[slot].at[rows, lanes], outs[slot].at[rows, lanes])
    if not aligned:
        for slot in range(12):
            send(held[slot], outs[slot])
    for copy in copies:
        copy.wait()


def adam(squares, grads, states, size):
    flat = gain_shape(size)
    states = [x.reshape(flat) if x.ndim == 1 else x for x in states]
    shapes = [x.shape for x in states[:3]]
    count = sum(x.size for x in states[:3])
    kinds = [(shape, F32) for shape in shapes] * 3 + [(shape, BF) for shape in shapes]
    outside = pl.BlockSpec(memory_space=pl.ANY)
    return call(
        functools.partial(adam_kernel, size),
        (*squares, *grads, *states),
        tuple(sds(*kind) for kind in kinds) + (sds((1, 1), F32),),
        20 * count,
        28 * count,
        placed=True,
        out_specs=(outside,) * 12 + (pl.BlockSpec(memory_space=pltpu.VMEM),),
        scratch=[pltpu.VMEM(*kind) for kind in kinds]
        + [pltpu.SemaphoreType.DMA((4 * len(adam_chunks(size, grads[0].shape[0])),))],
    )


def body(
    encoded,
    targets,
    present,
    wide_master,
    down_master,
    gain_master,
    wide_first,
    down_first,
    gain_first,
    wide_second,
    down_second,
    gain_second,
):
    size = lax.axis_size("wide") // 2
    position = lax.axis_index("wide") % size
    core = lax.axis_index("seg") % 2
    own = encoded[0]
    far = {0: swap(own, "wide", size)}
    first, rest = pack(wide_master, down_master, gain_master, size)

    high = size // 2
    first_mine = jnp.stack([first] + [swap(first, "wide", mask) for mask in range(1, size)])
    low_mine = [rest] + [swap(rest, "wide", mask) for mask in range(1, high)]
    far[0], first_mine, *low_mine = tie(far[0], first_mine, *low_mine)
    first_other = swap(first_mine, "seg", 1)
    far[high] = swap(far[0], "wide", high)
    for mask in range(1, high):
        far[mask] = swap(far[0], "wide", mask)
    queries_t, own_unit_t, weights_t, gains, first_all = start(own, first_mine, first_other, size)

    high_mine = swap(jnp.stack(low_mine), "wide", high)
    order = [high, *range(1, high), *range(high + 1, size)]
    groups = [[0]] + [order[k : k + 2] for k in range(0, size - 1, 2)]

    carry = None
    saved, units = [], []
    for group in groups:
        if len(saved) == 1:
            near = [far[mask] for mask in range(1, high)]
            near, far[high], carry[0], *low_mine = tie(near, far[high], carry[0], *low_mine)
            far.update(zip(range(1, high), near))
            low_other = [swap(x, "seg", 1) for x in low_mine]
            for mask in range(1, high):
                far[high + mask] = swap(far[high], "wide", mask)
        probs, keys_t, values_t, unit, tops, *carry = attend(
            [far[mask] for mask in group], queries_t, weights_t, gains, carry
        )
        saved.append((probs, keys_t, values_t, tops))
        if len(saved) == 2:
            carry[0], *low_other = tie(carry[0], *low_other)
        units.append(unit)
    accum, top = carry
    accum, high_mine = tie(accum, high_mine)
    high_other = swap(high_mine, "seg", 1)
    pieces = (*low_mine, high_mine, *low_other, high_other)

    rest_all, down_all = unpack(pieces, size)
    started, own_parts, far_parts = (), [], []
    for part in range(2):
        *started, estimate = dense_forward(
            part, own, accum, rest_all, down_all, gains, started
        )
        own_parts.append(estimate)
        far_parts.append(swap(estimate, "wide", size))
    (attended_t, inverse_total, branch_out, third, third_inverse, normed_two, slope, hidden,
     ffn_out, out_rows) = started

    errors, energy = error_energy(own_parts, far_parts, targets[0])
    energy = exchange(energy, size)
    seg_count = lax.axis_size("seg")
    (grad_est, grad_ffn, grad_pre, grad_branch, grad_attended_t, delta, late_gains,
     loss) = dense_back(
        seg_count, present, energy, errors, rest_all, down_all, gains, attended_t, branch_out,
        third, third_inverse, slope, ffn_out,
    )
    keep, send = dense_weights(
        grad_est, grad_ffn, grad_pre, grad_branch, attended_t, normed_two, hidden,
        out_rows, size,
    )
    grad_attended_t, keep, send = tie(grad_attended_t, keep, send)

    early = core_step(keep, send)
    grad_queries, grads = None, []
    for k, item in enumerate(saved):
        grad_queries, grad_kv = attend_back(
            item, queries_t, delta, top, inverse_total, grad_attended_t, grad_queries
        )
        grads.append(grad_kv)
        if k == 0:
            grad_queries, early = tie(grad_queries, early)
            early = send_members(early, size)
    keep, send = finish(
        grad_queries, own_unit_t, first_all, gains, late_gains, grads, units, size
    )
    keep, send, *early = tie(keep, send, *early)
    late = core_step(keep, send)
    early = segment_step(sum_low(early))
    late, loss = tie(late, loss)
    for mask in bits(seg_count):
        loss = loss + swap(loss, "seg", mask)
    late = sum_low(send_members(late, size))
    late, loss, early = tie(late, loss, early)
    early_other = swap(early, "seg", 1)
    late = segment_step(late)
    late_other = swap(late, "seg", 1)

    squares, kept = square_sum(early, early_other, late, late_other)
    parts = branch_parts(squares, size)
    squares = even_sum([kept + parts[0]] + parts[1:])
    squares_other = swap(squares, "seg", 1)
    *updated, grad_norm = adam(
        (squares, squares_other),
        (early, early_other, late, late_other),
        (wide_master, down_master, gain_master, wide_first, down_first, gain_first,
         wide_second, down_second, gain_second),
        size,
    )
    return (
        loss[0, 0],
        grad_norm.reshape(()),
        *(x.reshape(-1) if k % 3 == 2 else x for k, x in enumerate(updated)),
    )


def solution(mesh):
    split, line = P("wide", None), P("wide")
    states = (split, split, line)
    return jax.shard_map(
        body,
        mesh=mesh,
        in_specs=(P("seg", "wide", None), P("seg", None, None), P("seg", None)) + states * 3,
        out_specs=(P(), P()) + states * 4,
        check_vma=False,
    )
```

```python
import functools
import math

import jax
import jax.numpy as jnp
from jax import lax
from jax.experimental import pallas as pl
from jax.experimental.pallas import tpu as pltpu
from jax.sharding import PartitionSpec as P

D = 384
HEADS = 8
HEAD = D // HEADS
FF = 1536
STEMS = 4
SAMPLES = 32
OUT = STEMS * SAMPLES
QKV = 3 * D
REST = D + FF + OUT
ADAM_STEP = 10
LANES = 128

NORM_EPS = 1e-05
ENERGY_EPS = 1e-05
BETA_ONE = 0.9
BETA_TWO = 0.999
ADAM_EPS = 1e-08
LEARN_RATE = 0.1
GAIN_RATE = 0.5
WEIGHT_DECAY = 0.01
CLIP_LIMIT = 0.001

BF = jnp.bfloat16
F32 = jnp.float32
SCALE = 1.0 / math.sqrt(HEAD)
LOG_TWO = math.log(2.0)
VMEM_LIMIT = 16 * 2**20


def swap(x, axis, mask):
    return lax.ppermute(x, axis, [(i, i ^ mask) for i in range(lax.axis_size(axis))])


def dot(left, right, left_dim=1, right_dim=0):
    return lax.dot_general(
        left,
        right,
        (((left_dim,), (right_dim,)), ((), ())),
        preferred_element_type=F32,
    )


def unit_rows(values):
    centred = values - jnp.mean(values, axis=-1, keepdims=True)
    spread = jnp.mean(centred * centred, axis=-1, keepdims=True)
    inverse = lax.rsqrt(spread + NORM_EPS)
    return centred * inverse, inverse


def call(kernel, operands, out_shape, flops, moved, placed=False, scratch=(), out_specs=None,
         aliases=None):
    here = pl.BlockSpec(memory_space=pltpu.VMEM)
    size = lax.axis_size("wide") // 2

    def body_of(*refs):
        if placed:
            place = lax.axis_index("seg") % 2, lax.axis_index("wide") % size
            kernel(place, *refs)
        else:
            kernel(*refs)

    return pl.pallas_call(
        body_of,
        out_shape=out_shape,
        in_specs=[here] * len(operands),
        out_specs=out_specs or jax.tree.map(lambda _: here, out_shape),
        scratch_shapes=scratch,
        input_output_aliases=aliases or {},
        compiler_params=pltpu.CompilerParams(vmem_limit_bytes=VMEM_LIMIT),
        cost_estimate=pl.CostEstimate(flops=flops, bytes_accessed=moved, transcendentals=0),
    )(*operands)


def sds(shape, dtype):
    return jax.ShapeDtypeStruct(shape, dtype)


def gain_shape(size):
    count = 8 * D // size
    width = math.gcd(count, LANES)
    return count // width, width


def gain_places(size):
    tall, across = gain_shape(size)
    for owner in range(size):
        for row in range(tall):
            flat = (owner * tall + row) * across
            yield owner, row, flat // D, flat % D, across


def pack_kernel(size, place, wide, down, gains, first, rest):
    half = first.shape[0]
    same = place[0] == 0
    picked = jnp.where(same, wide[:half], wide[half:]).astype(BF)
    first[:, :QKV] = picked[:, :QKV]
    rest[:, :REST] = picked[:, QKV:]
    for part in range(4):
        row, other = half * part, half * (4 + part)
        piece = jnp.where(same, down[row : row + half], down[other : other + half])
        rest[:, REST + D * part : REST + D * (part + 1)] = piece.astype(BF)
    first[:, QKV:] = jnp.zeros((half, LANES), BF)
    tall, across = gain_shape(size)
    first[:tall, QKV : QKV + across] = jnp.where(same, gains[...], 0.0).astype(BF)


def pack(wide, down, gains, size):
    half = wide.shape[0] // 2
    return call(
        functools.partial(pack_kernel, size),
        (wide, down, gains.reshape(gain_shape(size))),
        (sds((half, QKV + LANES), BF), sds((half, REST + 4 * D), BF)),
        1000,
        4 * (wide.size + down.size),
        placed=True,
    )


def start_kernel(size, place, own, mine, other, queries_t, own_unit_t, weights_t, gains,
                 joined):
    core, position = place[0], place[1]
    half = mine.shape[1]
    for owner in range(size):
        slot = owner ^ position
        near, far = mine[slot], other[slot]
        row = 2 * owner * half
        joined[row : row + half] = jnp.where(core == 0, near, far)
        joined[row + half : row + 2 * half] = jnp.where(core == 0, far, near)
    for owner, row, vector, lane, across in gain_places(size):
        at = 2 * owner * half + row
        gains[vector : vector + 1, lane : lane + across] = joined[
            at : at + 1, QKV : QKV + across
        ].astype(F32)
    weights_t[...] = joined[:, :QKV].T
    hat, _ = unit_rows(own[...].astype(F32))
    own_unit_t[...] = hat.astype(BF).T
    normed = (hat * gains[0:1] + gains[1:2]).astype(BF)
    found = dot(weights_t[:D], normed, 1, 1)
    queries_t[...] = (found * (SCALE / LOG_TWO)).astype(BF)


def start(own, mine, other, size):
    rows = own.shape[0]
    return call(
        functools.partial(start_kernel, size),
        (own, mine, other),
        (
            sds((D, rows), BF),
            sds((D, rows), BF),
            sds((QKV, D), BF),
            sds((8, D), F32),
            sds((D, QKV + LANES), BF),
        ),
        2 * rows * D * D,
        rows * D * 8,
        placed=True,
    )


def heads_in_step(first, second, third):
    ahead, behind = first(0), None
    for h in range(HEADS):
        found = ahead
        if h + 1 < HEADS:
            ahead = first(h + 1)
        found = second(h, found)
        if behind is not None:
            third(h - 1, behind)
        behind = found
    third(HEADS - 1, behind)


def head_rows(h, offset=0, height=HEAD):
    return slice(offset + height * h, offset + height * (h + 1))


def over_blocks(count, visit):
    if count == 1:
        visit(0)
    else:
        lax.fori_loop(0, count, lambda block, carry: (visit(block), carry)[1], 0)


def attend_kernel(count, carried, *refs):
    queries_t, weights_t, gains = refs[:3]
    blocks = refs[3 : 3 + count]
    refs = refs[3 + count :]
    if carried:
        accum_in, top_in = refs[:2]
        refs = refs[2:]
    probs, keys_t, values_t, unit_t, tops, accum, top, joined = refs
    if carried:
        accum[...] = accum_in[...]
        top[...] = top_in[...]
    else:
        accum[...] = jnp.zeros_like(accum)
        top[...] = jnp.full_like(top, -1e30)
    for block in range(count):
        joined[block] = blocks[block][...]

    def visit(block):
        hat, _ = unit_rows(joined[block].astype(F32))
        unit_t[block] = hat.astype(BF).T
        crossed = (hat * gains[2:3] + gains[3:4]).astype(BF)
        keys_t[block] = dot(weights_t[D : 2 * D], crossed, 1, 1).astype(BF)
        values_t[block] = dot(weights_t[2 * D :], crossed, 1, 1).astype(BF)
        ones = jnp.ones((16, crossed.shape[0]), BF)

        def score(h):
            return dot(keys_t[block, head_rows(h)], queries_t[head_rows(h)], 0, 0)

        def soften(h, scores):
            before = top[h : h + 1]
            newest = jnp.maximum(before, jnp.max(scores, axis=0, keepdims=True))
            top[h : h + 1] = newest
            weight = jnp.exp2(scores - newest).astype(BF)
            probs[block, h] = weight
            return weight, jnp.exp2(before - newest)

        def gather(h, found):
            weight, fade = found
            tall = head_rows(h, 0, 64)
            values = jnp.concatenate([values_t[block, head_rows(h)], ones], axis=0)
            accum[tall] = accum[tall] * fade + dot(values, weight)

        heads_in_step(score, soften, gather)
        tops[block] = top[...]

    over_blocks(count, visit)


def attend(blocks, queries_t, weights_t, gains, carry):
    count, rows = len(blocks), blocks[0].shape[0]
    tokens = queries_t.shape[1]
    return call(
        functools.partial(attend_kernel, count, carry is not None),
        (queries_t, weights_t, gains, *blocks, *(carry or ())),
        (
            sds((count, HEADS, rows, tokens), BF),
            sds((count, D, rows), BF),
            sds((count, D, rows), BF),
            sds((count, D, rows), BF),
            sds((count, HEADS, tokens), F32),
            sds((64 * HEADS, tokens), F32),
            sds((HEADS, tokens), F32),
        ),
        count * rows * tokens * D,
        count * rows * tokens,
        scratch=[pltpu.VMEM((count, rows, D), BF)],
    )


def unpack_kernel(size, place, *refs):
    high = size // 2
    rest, down, joined = refs[2 * high + 2 :]
    core, position = place[0], place[1]
    half = joined.shape[1]
    for side in range(2):
        pieces = refs[side * (high + 1) : (side + 1) * (high + 1)]
        for other in range(size):
            slot = 2 * (other ^ position) + (side ^ core)
            joined[slot] = pieces[other][...] if other < high else pieces[high][other - high]
    for owner in range(size):
        for side in range(2):
            slot = 2 * owner + side
            rest[slot * half : (slot + 1) * half] = joined[slot, :, :REST]
            for part in range(4):
                row = (4 * slot + part) * half
                down[row : row + half] = joined[
                    slot, :, REST + D * part : REST + D * (part + 1)
                ]


def unpack(pieces, size):
    half, across = pieces[0].shape
    return call(
        functools.partial(unpack_kernel, size),
        tuple(pieces),
        (sds((D, REST), BF), sds((FF, D), BF)),
        1000,
        4 * D * across,
        placed=True,
        scratch=[pltpu.VMEM((2 * size, half, across), BF)],
    )


def row_part(part, rows):
    split = 3 * rows // 4
    return slice(split, rows) if part else slice(0, split)


def dense_kernel(part, inputs, accum, rest, down, gains, *refs):
    (attended_t, inverse_total, branch_out, third, third_inverse, normed_two, slope, hidden,
     ffn_out, out_rows, estimate) = refs[-11:]
    rows = row_part(part, inputs.shape[0])
    for h in range(HEADS):
        inverse = 1.0 / accum[64 * h + HEAD : 64 * h + HEAD + 1, rows]
        inverse_total[h : h + 1, rows] = inverse
        attended_t[HEAD * h : HEAD * (h + 1), rows] = (
            accum[64 * h : 64 * h + HEAD, rows] * inverse
        )
    branch = dot(attended_t[:, rows].astype(BF), rest[:, :D], 0, 0)
    branch_out[rows] = branch
    mid = inputs[rows].astype(F32) + gains[6:7] * branch
    hat, inverse = unit_rows(mid)
    third[rows] = hat
    third_inverse[rows] = inverse
    normed = (hat * gains[4:5] + gains[5:6]).astype(BF)
    normed_two[rows] = normed
    pre = dot(normed, rest[:, D : D + FF])
    gate = 0.5 * (1.0 + lax.erf(pre * math.sqrt(0.5)))
    hid = (pre * gate).astype(BF)
    hidden[rows] = hid
    bell = jnp.exp(-0.5 * pre * pre) * (1.0 / math.sqrt(2.0 * math.pi))
    slope[rows] = gate + pre * bell
    ffn = dot(hid, down[...])
    ffn_out[rows] = ffn
    out = (mid + gains[7:8] * ffn).astype(BF)
    out_rows[rows] = out
    estimate[...] = dot(out, rest[:, D + FF :]).astype(BF)


def dense_forward(part, inputs, accum, rest, down, gains, started):
    rows = inputs.shape[0]
    taken = row_part(part, rows)
    return call(
        functools.partial(dense_kernel, part),
        (inputs, accum, rest, down, gains, *started),
        (
            sds((D, rows), F32),
            sds((HEADS, rows), F32),
            sds((rows, D), F32),
            sds((rows, D), F32),
            sds((rows, 1), F32),
            sds((rows, D), BF),
            sds((rows, FF), F32),
            sds((rows, FF), BF),
            sds((rows, D), F32),
            sds((rows, D), BF),
            sds((taken.stop - taken.start, OUT), BF),
        ),
        rows * D * (D + 2 * FF + OUT),
        rows * FF * 4,
        aliases={5 + k: k for k in range(len(started))},
    )


def error_kernel(place, *refs):
    own, far, (targets, errors, energy) = refs[:2], refs[2:4], refs[4:]
    rows = errors.shape[0]
    row = lax.broadcasted_iota(jnp.int32, (8, OUT), 0)
    total = jnp.zeros((8, OUT), F32)
    for part in range(2):
        taken = row_part(part, rows)
        first = pl.multiple_of(place[1] * rows + taken.start, 8)
        wanted = targets[pl.ds(first, taken.stop - taken.start)]
        error = wanted - (own[part][...].astype(F32) + far[part][...].astype(F32))
        errors[taken] = error
        found = jnp.sum(error * error, axis=0, keepdims=True)
        clean = jnp.sum(wanted * wanted, axis=0, keepdims=True)
        total = total + jnp.where(row == 0, found, jnp.where(row == 1, clean, 0.0))
    energy[...] = total


def error_energy(own, far, targets):
    rows = own[0].shape[0] + own[1].shape[0]
    return call(
        error_kernel,
        (*own, *far, targets),
        (sds((rows, OUT), F32), sds((8, OUT), F32)),
        rows * OUT * 8,
        rows * OUT * 12,
        placed=True,
    )


def even_sum(parts):
    while len(parts) > 1:
        parts = [first + second for first, second in zip(parts[0::2], parts[1::2])]
    return parts[0]


def stem_sums(values):
    stem = lax.broadcasted_iota(jnp.int32, values.shape, 1) // SAMPLES
    total = jnp.zeros_like(values)
    for k in range(STEMS):
        part = jnp.sum(jnp.where(stem == k, values, 0.0), axis=1, keepdims=True)
        total = jnp.where(stem == k, part, total)
    return total


def dense_back_kernel(segments, present, energies, errors, rest, down, gains, attended_t, branch_out,
                      third, third_inverse, slope, ffn_out, grad_est, grad_ffn, grad_pre,
                      grad_branch, grad_attended_t, delta, grad_gains, loss):
    energy = even_sum([energies[slot] for slot in range(energies.shape[0])])
    lane = lax.broadcasted_iota(jnp.int32, (1, OUT), 1)
    counted = jnp.zeros((1, OUT), F32)
    for k in range(STEMS):
        counted = jnp.where(lane // SAMPLES == k, present[:, k : k + 1].astype(F32), counted)
    counted = counted * (10.0 / math.log(10.0) / (segments * STEMS))
    found = stem_sums(energy[0:1]) + ENERGY_EPS
    clean = stem_sums(energy[1:2]) + ENERGY_EPS
    terms = counted * (jnp.log(found) - jnp.log(clean))
    terms = jnp.where(lane % SAMPLES == 0, terms, 0.0)
    loss[...] = jnp.broadcast_to(jnp.sum(terms, axis=1, keepdims=True), loss.shape)
    low = (errors[...] * (-2.0 * counted / found)).astype(BF)
    grad_est[...] = low
    grad_out = dot(low, rest[:, D + FF :], 1, 1)
    grad_gains[3:4] = jnp.sum(grad_out * ffn_out[...], axis=0, keepdims=True)
    ffn = (grad_out * gains[7:8]).astype(BF)
    grad_ffn[...] = ffn
    hidden = dot(ffn, down[...], 1, 1).astype(BF)
    pre = (hidden.astype(F32) * slope[...]).astype(BF)
    grad_pre[...] = pre
    normed = dot(pre, rest[:, D : D + FF], 1, 1)
    hat = third[...]
    grad_gains[0:1] = jnp.sum(normed * hat, axis=0, keepdims=True)
    grad_gains[1:2] = jnp.sum(normed, axis=0, keepdims=True)
    scaled = normed * gains[4:5]
    grad_mid = grad_out + third_inverse[...] * (
        scaled
        - jnp.mean(scaled, axis=-1, keepdims=True)
        - hat * jnp.mean(scaled * hat, axis=-1, keepdims=True)
    )
    grad_gains[2:3] = jnp.sum(grad_mid * branch_out[...], axis=0, keepdims=True)
    branch = (grad_mid * gains[6:7]).astype(BF)
    grad_branch[...] = branch
    attended = dot(rest[:, :D], branch, 1, 1).astype(BF)
    grad_attended_t[...] = attended
    product = attended.astype(F32) * attended_t[...]
    for h in range(HEADS):
        delta[h : h + 1] = jnp.sum(product[head_rows(h)], axis=0, keepdims=True)


def dense_back(segments, present, energies, errors, rest, down, gains, attended_t, branch_out, third,
               third_inverse, slope, ffn_out):
    rows = errors.shape[0]
    return call(
        functools.partial(dense_back_kernel, segments),
        (present, energies, errors, rest, down, gains, attended_t, branch_out, third,
         third_inverse, slope, ffn_out),
        (
            sds((rows, OUT), BF),
            sds((rows, D), BF),
            sds((rows, FF), BF),
            sds((rows, D), BF),
            sds((D, rows), BF),
            sds((HEADS, rows), F32),
            sds((4, D), F32),
            sds((8, LANES), F32),
        ),
        2 * rows * D * (D + 2 * FF + OUT),
        rows * FF * 8,
    )


def deal(size, place, first, second, keep, send, owner, at):
    slot = owner ^ place[1]
    same = place[0] == 0
    keep[slot, :, at] = jnp.where(same, first, second).astype(BF)
    send[slot, :, at] = jnp.where(same, second, first).astype(BF)


def dense_weights_kernel(size, place, grad_est, grad_ffn, grad_pre, grad_branch, attended_t,
                         normed_two, hidden, out_rows, keep, send, wide, tall):
    half = keep.shape[1]
    wide[:, D + FF :] = dot(out_rows[...], grad_est[...], 0, 0)
    wide[:, D : D + FF] = dot(normed_two[...], grad_pre[...], 0, 0)
    wide[:, :D] = dot(attended_t[...].astype(BF), grad_branch[...])
    tall[...] = dot(hidden[...], grad_ffn[...], 0, 0)
    for owner in range(size):
        row = 2 * owner * half
        deal(
            size, place, wide[row : row + half], wide[row + half : row + 2 * half],
            keep, send, owner, slice(0, REST),
        )
        for part in range(4):
            first = (8 * owner + part) * half
            second = (8 * owner + 4 + part) * half
            deal(
                size, place, tall[first : first + half], tall[second : second + half],
                keep, send, owner, slice(REST + D * part, REST + D * (part + 1)),
            )


def dense_weights(grad_est, grad_ffn, grad_pre, grad_branch, attended_t, normed_two,
                  hidden, out_rows, size):
    rows = grad_est.shape[0]
    piece = (size, D // size // 2, REST + 4 * D)
    return call(
        functools.partial(dense_weights_kernel, size),
        (grad_est, grad_ffn, grad_pre, grad_branch, attended_t, normed_two, hidden, out_rows),
        (sds(piece, BF), sds(piece, BF)),
        2 * rows * D * (D + 2 * FF + OUT),
        rows * FF * 8,
        placed=True,
        scratch=[pltpu.VMEM((D, REST), F32), pltpu.VMEM((FF, D), F32)],
    )


def attend_back_kernel(carried, probs, keys_t, values_t, tops, queries_t, delta, top,
                       inverse_total, grad_attended_t, *refs):
    if carried:
        refs[1][...] = refs[0][...]
    else:
        refs[0][...] = jnp.zeros_like(refs[0])
    grad_queries, grad_kv = refs[-2:]

    def visit(block):
        factor = jnp.exp2(tops[block] - top[...]) * inverse_total[...]
        shift = delta[...] * factor

        def begin(h):
            grad = grad_attended_t[head_rows(h)].astype(F32) * factor[h : h + 1]
            grad = grad.astype(BF)
            return grad, dot(values_t[block, head_rows(h)], grad, 0, 0)

        def turn(h, found):
            grad, grad_probs = found
            scores = probs[block, h].astype(F32) * (grad_probs - shift[h : h + 1])
            return grad, scores.astype(BF)

        def end(h, found):
            grad, scores = found
            at = head_rows(h)
            grad_queries[at] += dot(keys_t[block, at], scores)
            grad_kv[block, at] = (dot(queries_t[at], scores, 1, 1) * LOG_TWO).astype(BF)
            grad_kv[block, head_rows(h, D)] = dot(grad, probs[block, h], 1, 1).astype(BF)

        heads_in_step(begin, turn, end)

    over_blocks(probs.shape[0], visit)


def attend_back(saved, queries_t, delta, top, inverse_total, grad_attended_t, carry):
    probs, keys_t, values_t, tops = saved
    count, _, rows, tokens = probs.shape
    carry = () if carry is None else (carry,)
    return call(
        functools.partial(attend_back_kernel, len(carry)),
        (probs, keys_t, values_t, tops, queries_t, delta, top, inverse_total,
         grad_attended_t, *carry),
        (sds((D, tokens), F32), sds((count, 2 * D, rows), BF)),
        count * (8 * rows * tokens * D * 5),
        count * (HEADS * rows * tokens * 2),
    )


def unit_products(units, grads):
    total = None
    for k in range(0, len(units), 4):
        left = jnp.concatenate(units[k : k + 4], axis=1)
        left = jnp.concatenate([left, jnp.ones((16, left.shape[1]), BF)], axis=0)
        term = dot(left, jnp.concatenate(grads[k : k + 4], axis=1), 1, 1)
        total = term if total is None else total + term
    return total


def finish_kernel(size, groups, place, grad_queries, own_unit_t, weights, gains, late, *refs):
    grads, units = refs[:groups], refs[groups : 2 * groups]
    keep, send, full, grad_gains = refs[2 * groups :]
    query = (grad_queries[...] * SCALE).astype(BF)
    blocks = [(g, block) for g, grad in enumerate(grads) for block in range(grad.shape[0])]
    found = (
        unit_products([own_unit_t[...]], [query]),
        unit_products([units[g][b] for g, b in blocks], [grads[g][b] for g, b in blocks]),
    )
    columns = gains[...].T
    lane = lax.broadcasted_iota(jnp.int32, (D, LANES), 1)
    small = jnp.zeros((D, LANES), F32)
    for product, first, row in zip(found, (0, D), (0, 2)):
        at = slice(first, first + product.shape[1])
        moment, total = product[:D], product[D : D + 1]
        weight = weights[:, at].astype(F32)
        for k, terms in enumerate((weight * moment, weight * total)):
            small = jnp.where(lane == row + k, jnp.sum(terms, axis=1, keepdims=True), small)
        value = moment * columns[:, row : row + 1] + total * columns[:, row + 1 : row + 2]
        full[:, at] = value.astype(BF)
    grad_gains[:4] = small.T[:4]
    grad_gains[4:8] = late[...]
    half = keep.shape[1]
    for owner in range(size):
        row = 2 * owner * half
        deal(
            size, place, full[row : row + half], full[row + half : row + 2 * half],
            keep, send, owner, slice(0, QKV),
        )
    same = place[0] == 0
    tall, across = gain_shape(size)
    for owner in range(size):
        rows = [
            grad_gains[vector : vector + 1, lane : lane + across]
            for where, _, vector, lane, _ in gain_places(size)
            if where == owner
        ]
        block = jnp.concatenate(rows + [jnp.zeros((half - tall, across), F32)], axis=0)
        if across < LANES:
            block = jnp.concatenate([block, jnp.zeros((half, LANES - across), F32)], axis=1)
        slot = owner ^ place[1]
        keep[slot, :, QKV:] = jnp.where(same, block, 0.0).astype(BF)
        send[slot, :, QKV:] = jnp.where(same, 0.0, block).astype(BF)


def finish(grad_queries, own_unit_t, weights, gains, late, grads, units, size):
    rows = own_unit_t.shape[1]
    piece = (size, D // size // 2, QKV + LANES)
    return call(
        functools.partial(finish_kernel, size, len(grads)),
        (grad_queries, own_unit_t, weights, gains, late, *grads, *units),
        (sds(piece, BF), sds(piece, BF)),
        2 * rows * D * QKV * size,
        rows * D * 2 * size,
        placed=True,
        scratch=[
            pltpu.VMEM((D, QKV), BF),
            pltpu.VMEM((8, D), F32),
        ],
    )


def square_kernel(*refs):
    found = []
    for ref in refs[:4]:
        values = ref[...].astype(F32)
        rows = jnp.sum(values * values, axis=0, keepdims=True)
        found.append(jnp.sum(rows, axis=1, keepdims=True))
    refs[4][...] = jnp.broadcast_to(even_sum(found), refs[4].shape)


def square_sum(*parts):
    size = sum(x.size for x in parts)
    return call(square_kernel, parts, sds((8, LANES), F32), 2 * size, 2 * size)


def bits(size):
    return [1 << k for k in range(size.bit_length() - 1)]


def masks(size):
    return sorted(range(1, size), key=lambda mask: (mask.bit_count(), mask))


def tie(*values):
    return lax.optimization_barrier(values)


def add_low(left, right):
    return (left.astype(F32) + right.astype(F32)).astype(BF)


def core_step(keep, send):
    return add_low(keep, swap(send, "seg", 1))


def send_members(total, size):
    return [total[0]] + [swap(total[mask], "wide", mask) for mask in [2, 3, 1]]


def sum_low(parts):
    return functools.reduce(jnp.add, [x.astype(F32) for x in parts]).astype(BF)


def exchange(values, size):
    return jnp.stack([values] + [swap(values, "wide", mask) for mask in range(1, size)])


def segment_step(total):
    for mask in bits(lax.axis_size("seg"))[1:]:
        total = add_low(total, swap(total, "seg", mask))
    return total


def adam_update(weight, grad, moment, second, rate):
    moment = BETA_ONE * moment + (1 - BETA_ONE) * grad
    second = BETA_TWO * second + (1 - BETA_TWO) * (grad * grad)
    fixed_one = moment * (rate / (1 - BETA_ONE**ADAM_STEP))
    fixed_two = second * (1 / (1 - BETA_TWO**ADAM_STEP))
    weight = weight * (1 - rate * WEIGHT_DECAY) - fixed_one / (jnp.sqrt(fixed_two) + ADAM_EPS)
    return (weight, moment, second)


def adam_chunks(size, half):
    tall, across = gain_shape(size)
    chunks = []
    for side in range(2):
        rows, ends = slice(4 * side * half, 4 * (side + 1) * half), slice(0, D)
        parts = [
            (slice((4 * side + k) * half, (4 * side + k + 1) * half), ends, 0,
             slice(REST + D * k, REST + D * (k + 1)))
            for k in range(4)
        ]
        chunks.append((1, side, rows, ends, parts))
        rows = slice(side * half, (side + 1) * half)
        parts = [
            (rows, slice(0, QKV), 1, slice(0, QKV)),
            (rows, slice(QKV, QKV + REST), 0, slice(0, REST)),
        ]
        chunks.append((0, side, rows, slice(0, QKV + REST), parts))
    rows, lanes = slice(0, tall), slice(0, across)
    chunks.append((2, 0, rows, lanes, [(rows, lanes, 1, slice(QKV, QKV + across))]))
    return chunks


def tiles(rows, lanes, source):
    high, across = rows.stop - rows.start, lanes.stop - lanes.start
    for row in range(0, high, 16):
        tall = min(16, high - row)
        for lane in range(0, across, D):
            part = min(D, across - lane)
            yield (
                (slice(rows.start + row, rows.start + row + tall),
                 slice(lanes.start + lane, lanes.start + lane + part)),
                (slice(row, row + tall),
                 slice(source.start + lane, source.start + lane + part)),
            )


def adam_kernel(size, place, squares, squares_other, early, early_other, late, late_other,
                *refs):
    states, outs, norm = [refs[k : k + 3] for k in (0, 3, 6)], refs[9:21], refs[21]
    held, sems = refs[22:34], refs[34]
    same = place[0] == 0
    grad_norm = jnp.sqrt(squares[0:1, 0:1] + squares_other[0:1, 0:1])
    norm[...] = grad_norm
    factor = jnp.minimum(1.0, CLIP_LIMIT / (grad_norm + 1e-06))
    copies, aligned = [], early.shape[0] % 16 == 0

    def send(source, target):
        copies.append(pltpu.make_async_copy(source, target, sems.at[len(copies)]))
        copies[-1].start()

    for index, side, rows, lanes, parts in adam_chunks(size, early.shape[0]):
        rate = GAIN_RATE if index == 2 else LEARN_RATE
        for part_rows, part_lanes, which, source in parts:
            own, other = (late, late_other) if which else (early, early_other)
            if side:
                own, other = other, own
            for here, there in tiles(part_rows, part_lanes, source):
                grad = jnp.where(same, own[there].astype(F32), other[there].astype(F32))
                weight, moment, second = (x[index][here] for x in states)
                found = adam_update(weight, grad * factor, moment, second, rate)
                for kind, value in enumerate((*found, found[0].astype(BF))):
                    held[3 * kind + index][here] = value
        if aligned:
            for slot in range(index, 12, 3):
                send(held[slot].at[rows, lanes], outs[slot].at[rows, lanes])
    if not aligned:
        for slot in range(12):
            send(held[slot], outs[slot])
    for copy in copies:
        copy.wait()


def adam(squares, grads, states, size):
    flat = gain_shape(size)
    states = [x.reshape(flat) if x.ndim == 1 else x for x in states]
    shapes = [x.shape for x in states[:3]]
    count = sum(x.size for x in states[:3])
    kinds = [(shape, F32) for shape in shapes] * 3 + [(shape, BF) for shape in shapes]
    outside = pl.BlockSpec(memory_space=pl.ANY)
    return call(
        functools.partial(adam_kernel, size),
        (*squares, *grads, *states),
        tuple(sds(*kind) for kind in kinds) + (sds((1, 1), F32),),
        20 * count,
        28 * count,
        placed=True,
        out_specs=(outside,) * 12 + (pl.BlockSpec(memory_space=pltpu.VMEM),),
        scratch=[pltpu.VMEM(*kind) for kind in kinds]
        + [pltpu.SemaphoreType.DMA((4 * len(adam_chunks(size, grads[0].shape[0])),))],
    )


def body(
    encoded,
    targets,
    present,
    wide_master,
    down_master,
    gain_master,
    wide_first,
    down_first,
    gain_first,
    wide_second,
    down_second,
    gain_second,
):
    size = lax.axis_size("wide") // 2
    position = lax.axis_index("wide") % size
    core = lax.axis_index("seg") % 2
    own = encoded[0]
    far = {0: swap(own, "wide", size)}
    first, rest = pack(wide_master, down_master, gain_master, size)

    high = size // 2
    first_mine = jnp.stack([first] + [swap(first, "wide", mask) for mask in range(1, size)])
    low_mine = [rest] + [swap(rest, "wide", mask) for mask in range(1, high)]
    far[0], first_mine, *low_mine = tie(far[0], first_mine, *low_mine)
    first_other = swap(first_mine, "seg", 1)
    far[high] = swap(far[0], "wide", high)
    for mask in range(1, high):
        far[mask] = swap(far[0], "wide", mask)
    queries_t, own_unit_t, weights_t, gains, first_all = start(own, first_mine, first_other, size)

    high_mine = swap(jnp.stack(low_mine), "wide", high)
    order = [high, *range(1, high), *range(high + 1, size)]
    groups = [[0]] + [order[k : k + 2] for k in range(0, size - 1, 2)]

    carry = None
    saved, units = [], []
    for group in groups:
        if len(saved) == 1:
            near = [far[mask] for mask in range(1, high)]
            near, far[high], carry[0], *low_mine = tie(near, far[high], carry[0], *low_mine)
            far.update(zip(range(1, high), near))
            low_other = [swap(x, "seg", 1) for x in low_mine]
            for mask in range(1, high):
                far[high + mask] = swap(far[high], "wide", mask)
        probs, keys_t, values_t, unit, tops, *carry = attend(
            [far[mask] for mask in group], queries_t, weights_t, gains, carry
        )
        saved.append((probs, keys_t, values_t, tops))
        if len(saved) == 2:
            carry[0], *low_other = tie(carry[0], *low_other)
        units.append(unit)
    accum, top = carry
    accum, high_mine = tie(accum, high_mine)
    high_other = swap(high_mine, "seg", 1)
    pieces = (*low_mine, high_mine, *low_other, high_other)

    rest_all, down_all = unpack(pieces, size)
    started, own_parts, far_parts = (), [], []
    for part in range(2):
        *started, estimate = dense_forward(
            part, own, accum, rest_all, down_all, gains, started
        )
        own_parts.append(estimate)
        far_parts.append(swap(estimate, "wide", size))
    (attended_t, inverse_total, branch_out, third, third_inverse, normed_two, slope, hidden,
     ffn_out, out_rows) = started

    errors, energy = error_energy(own_parts, far_parts, targets[0])
    energy = exchange(energy, size)
    seg_count = lax.axis_size("seg")
    (grad_est, grad_ffn, grad_pre, grad_branch, grad_attended_t, delta, late_gains,
     loss) = dense_back(
        seg_count, present, energy, errors, rest_all, down_all, gains, attended_t, branch_out,
        third, third_inverse, slope, ffn_out,
    )
    keep, send = dense_weights(
        grad_est, grad_ffn, grad_pre, grad_branch, attended_t, normed_two, hidden,
        out_rows, size,
    )
    grad_attended_t, keep, send = tie(grad_attended_t, keep, send)

    early = core_step(keep, send)
    grad_queries, grads = None, []
    for k, item in enumerate(saved):
        grad_queries, grad_kv = attend_back(
            item, queries_t, delta, top, inverse_total, grad_attended_t, grad_queries
        )
        grads.append(grad_kv)
        if k == 0:
            grad_queries, early = tie(grad_queries, early)
            early = send_members(early, size)
    keep, send = finish(
        grad_queries, own_unit_t, first_all, gains, late_gains, grads, units, size
    )
    keep, send, *early = tie(keep, send, *early)
    late = core_step(keep, send)
    early = segment_step(sum_low(early))
    late, loss = tie(late, loss)
    for mask in bits(seg_count):
        loss = loss + swap(loss, "seg", mask)
    late = sum_low(send_members(late, size))
    late, loss, early = tie(late, loss, early)
    early_other = swap(early, "seg", 1)
    late = segment_step(late)
    late_other = swap(late, "seg", 1)

    squares = square_sum(early, early_other, late, late_other)
    squares = even_sum([squares] + [swap(squares, "wide", mask) for mask in range(1, size)])
    squares_other = swap(squares, "wide", size)
    *updated, grad_norm = adam(
        (squares, squares_other),
        (early, early_other, late, late_other),
        (wide_master, down_master, gain_master, wide_first, down_first, gain_first,
         wide_second, down_second, gain_second),
        size,
    )
    return (
        loss[0, 0],
        grad_norm.reshape(()),
        *(x.reshape(-1) if k % 3 == 2 else x for k, x in enumerate(updated)),
    )


def solution(mesh):
    split, line = P("wide", None), P("wide")
    states = (split, split, line)
    return jax.shard_map(
        body,
        mesh=mesh,
        in_specs=(P("seg", "wide", None), P("seg", None, None), P("seg", None)) + states * 3,
        out_specs=(P(), P()) + states * 4,
        check_vma=False,
    )
```

```python
import functools
import math

import jax
import jax.numpy as jnp
from jax import lax
from jax.experimental import pallas as pl
from jax.experimental.pallas import tpu as pltpu
from jax.sharding import PartitionSpec as P

D = 384
HEADS = 8
HEAD = D // HEADS
FF = 1536
STEMS = 4
SAMPLES = 32
OUT = STEMS * SAMPLES
QKV = 3 * D
REST = D + FF + OUT
ADAM_STEP = 10
LANES = 128

NORM_EPS = 1e-05
ENERGY_EPS = 1e-05
BETA_ONE = 0.9
BETA_TWO = 0.999
ADAM_EPS = 1e-08
LEARN_RATE = 0.1
GAIN_RATE = 0.5
WEIGHT_DECAY = 0.01
CLIP_LIMIT = 0.001

BF = jnp.bfloat16
F32 = jnp.float32
SCALE = 1.0 / math.sqrt(HEAD)
LOG_TWO = math.log(2.0)
VMEM_LIMIT = 16 * 2**20


def swap(x, axis, mask):
    return lax.ppermute(x, axis, [(i, i ^ mask) for i in range(lax.axis_size(axis))])


def dot(left, right, left_dim=1, right_dim=0):
    return lax.dot_general(
        left,
        right,
        (((left_dim,), (right_dim,)), ((), ())),
        preferred_element_type=F32,
    )


def unit_rows(values):
    centred = values - jnp.mean(values, axis=-1, keepdims=True)
    spread = jnp.mean(centred * centred, axis=-1, keepdims=True)
    inverse = lax.rsqrt(spread + NORM_EPS)
    return centred * inverse, inverse


def call(kernel, operands, out_shape, flops, moved, placed=False, scratch=(), out_specs=None,
         aliases=None):
    here = pl.BlockSpec(memory_space=pltpu.VMEM)
    size = lax.axis_size("wide") // 2

    def body_of(*refs):
        if placed:
            place = lax.axis_index("seg") % 2, lax.axis_index("wide") % size
            kernel(place, *refs)
        else:
            kernel(*refs)

    return pl.pallas_call(
        body_of,
        out_shape=out_shape,
        in_specs=[here] * len(operands),
        out_specs=out_specs or jax.tree.map(lambda _: here, out_shape),
        scratch_shapes=scratch,
        input_output_aliases=aliases or {},
        compiler_params=pltpu.CompilerParams(vmem_limit_bytes=VMEM_LIMIT),
        cost_estimate=pl.CostEstimate(flops=flops, bytes_accessed=moved, transcendentals=0),
    )(*operands)


def sds(shape, dtype):
    return jax.ShapeDtypeStruct(shape, dtype)


def gain_shape(size):
    count = 8 * D // size
    width = math.gcd(count, LANES)
    return count // width, width


def gain_places(size):
    tall, across = gain_shape(size)
    for owner in range(size):
        for row in range(tall):
            flat = (owner * tall + row) * across
            yield owner, row, flat // D, flat % D, across


def pack_kernel(size, place, wide, down, gains, first, rest):
    half = first.shape[0]
    same = place[0] == 0
    picked = jnp.where(same, wide[:half], wide[half:]).astype(BF)
    first[:, :QKV] = picked[:, :QKV]
    rest[:, :REST] = picked[:, QKV:]
    for part in range(4):
        row, other = half * part, half * (4 + part)
        piece = jnp.where(same, down[row : row + half], down[other : other + half])
        rest[:, REST + D * part : REST + D * (part + 1)] = piece.astype(BF)
    first[:, QKV:] = jnp.zeros((half, LANES), BF)
    tall, across = gain_shape(size)
    first[:tall, QKV : QKV + across] = jnp.where(same, gains[...], 0.0).astype(BF)


def pack(wide, down, gains, size):
    half = wide.shape[0] // 2
    return call(
        functools.partial(pack_kernel, size),
        (wide, down, gains.reshape(gain_shape(size))),
        (sds((half, QKV + LANES), BF), sds((half, REST + 4 * D), BF)),
        1000,
        4 * (wide.size + down.size),
        placed=True,
    )


def start_kernel(size, place, own, mine, other, queries_t, own_unit_t, weights_t, gains,
                 joined):
    core, position = place[0], place[1]
    half = mine.shape[1]
    for owner in range(size):
        slot = owner ^ position
        near, far = mine[slot], other[slot]
        row = 2 * owner * half
        joined[row : row + half] = jnp.where(core == 0, near, far)
        joined[row + half : row + 2 * half] = jnp.where(core == 0, far, near)
    for owner, row, vector, lane, across in gain_places(size):
        at = 2 * owner * half + row
        gains[vector : vector + 1, lane : lane + across] = joined[
            at : at + 1, QKV : QKV + across
        ].astype(F32)
    weights_t[...] = joined[:, :QKV].T
    hat, _ = unit_rows(own[...].astype(F32))
    own_unit_t[...] = hat.astype(BF).T
    normed = (hat * gains[0:1] + gains[1:2]).astype(BF)
    found = dot(weights_t[:D], normed, 1, 1)
    queries_t[...] = (found * (SCALE / LOG_TWO)).astype(BF)


def start(own, mine, other, size):
    rows = own.shape[0]
    return call(
        functools.partial(start_kernel, size),
        (own, mine, other),
        (
            sds((D, rows), BF),
            sds((D, rows), BF),
            sds((QKV, D), BF),
            sds((8, D), F32),
            sds((D, QKV + LANES), BF),
        ),
        2 * rows * D * D,
        rows * D * 8,
        placed=True,
    )


def heads_in_step(first, second, third):
    ahead, behind = first(0), None
    for h in range(HEADS):
        found = ahead
        if h + 1 < HEADS:
            ahead = first(h + 1)
        found = second(h, found)
        if behind is not None:
            third(h - 1, behind)
        behind = found
    third(HEADS - 1, behind)


def head_rows(h, offset=0, height=HEAD):
    return slice(offset + height * h, offset + height * (h + 1))


def over_blocks(count, visit):
    if count == 1:
        visit(0)
    else:
        lax.fori_loop(0, count, lambda block, carry: (visit(block), carry)[1], 0)


def attend_kernel(count, carried, *refs):
    queries_t, weights_t, gains = refs[:3]
    blocks = refs[3 : 3 + count]
    refs = refs[3 + count :]
    if carried:
        accum_in, top_in = refs[:2]
        refs = refs[2:]
    probs, keys_t, values_t, unit_t, tops, accum, top, joined = refs
    if carried:
        accum[...] = accum_in[...]
        top[...] = top_in[...]
    else:
        accum[...] = jnp.zeros_like(accum)
        top[...] = jnp.full_like(top, -1e30)
    for block in range(count):
        joined[block] = blocks[block][...]

    def visit(block):
        hat, _ = unit_rows(joined[block].astype(F32))
        unit_t[block] = hat.astype(BF).T
        crossed = (hat * gains[2:3] + gains[3:4]).astype(BF)
        keys_t[block] = dot(weights_t[D : 2 * D], crossed, 1, 1).astype(BF)
        values_t[block] = dot(weights_t[2 * D :], crossed, 1, 1).astype(BF)
        ones = jnp.ones((16, crossed.shape[0]), BF)

        def score(h):
            return dot(keys_t[block, head_rows(h)], queries_t[head_rows(h)], 0, 0)

        def soften(h, scores):
            before = top[h : h + 1]
            newest = jnp.maximum(before, jnp.max(scores, axis=0, keepdims=True))
            top[h : h + 1] = newest
            weight = jnp.exp2(scores - newest).astype(BF)
            probs[block, h] = weight
            return weight, jnp.exp2(before - newest)

        def gather(h, found):
            weight, fade = found
            tall = head_rows(h, 0, 64)
            values = jnp.concatenate([values_t[block, head_rows(h)], ones], axis=0)
            accum[tall] = accum[tall] * fade + dot(values, weight)

        heads_in_step(score, soften, gather)
        tops[block] = top[...]

    over_blocks(count, visit)


def attend(blocks, queries_t, weights_t, gains, carry):
    count, rows = len(blocks), blocks[0].shape[0]
    tokens = queries_t.shape[1]
    return call(
        functools.partial(attend_kernel, count, carry is not None),
        (queries_t, weights_t, gains, *blocks, *(carry or ())),
        (
            sds((count, HEADS, rows, tokens), BF),
            sds((count, D, rows), BF),
            sds((count, D, rows), BF),
            sds((count, D, rows), BF),
            sds((count, HEADS, tokens), F32),
            sds((64 * HEADS, tokens), F32),
            sds((HEADS, tokens), F32),
        ),
        count * rows * tokens * D,
        count * rows * tokens,
        scratch=[pltpu.VMEM((count, rows, D), BF)],
    )


def unpack_kernel(size, place, *refs):
    high = size // 2
    rest, down, joined = refs[2 * high + 2 :]
    core, position = place[0], place[1]
    half = joined.shape[1]
    for side in range(2):
        pieces = refs[side * (high + 1) : (side + 1) * (high + 1)]
        for other in range(size):
            slot = 2 * (other ^ position) + (side ^ core)
            joined[slot] = pieces[other][...] if other < high else pieces[high][other - high]
    for owner in range(size):
        for side in range(2):
            slot = 2 * owner + side
            rest[slot * half : (slot + 1) * half] = joined[slot, :, :REST]
            for part in range(4):
                row = (4 * slot + part) * half
                down[row : row + half] = joined[
                    slot, :, REST + D * part : REST + D * (part + 1)
                ]


def unpack(pieces, size):
    half, across = pieces[0].shape
    return call(
        functools.partial(unpack_kernel, size),
        tuple(pieces),
        (sds((D, REST), BF), sds((FF, D), BF)),
        1000,
        4 * D * across,
        placed=True,
        scratch=[pltpu.VMEM((2 * size, half, across), BF)],
    )


def row_part(part, rows):
    split = 3 * rows // 4
    return slice(split, rows) if part else slice(0, split)


def dense_kernel(part, inputs, accum, rest, down, gains, *refs):
    (attended_t, inverse_total, branch_out, third, third_inverse, normed_two, slope, hidden,
     ffn_out, out_rows, estimate) = refs[-11:]
    rows = row_part(part, inputs.shape[0])
    for h in range(HEADS):
        inverse = 1.0 / accum[64 * h + HEAD : 64 * h + HEAD + 1, rows]
        inverse_total[h : h + 1, rows] = inverse
        attended_t[HEAD * h : HEAD * (h + 1), rows] = (
            accum[64 * h : 64 * h + HEAD, rows] * inverse
        )
    branch = dot(attended_t[:, rows].astype(BF), rest[:, :D], 0, 0)
    branch_out[rows] = branch
    mid = inputs[rows].astype(F32) + gains[6:7] * branch
    hat, inverse = unit_rows(mid)
    third[rows] = hat
    third_inverse[rows] = inverse
    normed = (hat * gains[4:5] + gains[5:6]).astype(BF)
    normed_two[rows] = normed
    pre = dot(normed, rest[:, D : D + FF])
    gate = 0.5 * (1.0 + lax.erf(pre * math.sqrt(0.5)))
    hid = (pre * gate).astype(BF)
    hidden[rows] = hid
    bell = jnp.exp(-0.5 * pre * pre) * (1.0 / math.sqrt(2.0 * math.pi))
    slope[rows] = gate + pre * bell
    ffn = dot(hid, down[...])
    ffn_out[rows] = ffn
    out = (mid + gains[7:8] * ffn).astype(BF)
    out_rows[rows] = out
    estimate[...] = dot(out, rest[:, D + FF :]).astype(BF)


def dense_forward(part, inputs, accum, rest, down, gains, started):
    rows = inputs.shape[0]
    taken = row_part(part, rows)
    return call(
        functools.partial(dense_kernel, part),
        (inputs, accum, rest, down, gains, *started),
        (
            sds((D, rows), F32),
            sds((HEADS, rows), F32),
            sds((rows, D), F32),
            sds((rows, D), F32),
            sds((rows, 1), F32),
            sds((rows, D), BF),
            sds((rows, FF), F32),
            sds((rows, FF), BF),
            sds((rows, D), F32),
            sds((rows, D), BF),
            sds((taken.stop - taken.start, OUT), BF),
        ),
        rows * D * (D + 2 * FF + OUT),
        rows * FF * 4,
        aliases={5 + k: k for k in range(len(started))},
    )


def error_kernel(place, *refs):
    own, far, (targets, errors, energy) = refs[:2], refs[2:4], refs[4:]
    rows = errors.shape[0]
    row = lax.broadcasted_iota(jnp.int32, (8, OUT), 0)
    total = jnp.zeros((8, OUT), F32)
    for part in range(2):
        taken = row_part(part, rows)
        first = pl.multiple_of(place[1] * rows + taken.start, 8)
        wanted = targets[pl.ds(first, taken.stop - taken.start)]
        error = wanted - (own[part][...].astype(F32) + far[part][...].astype(F32))
        errors[taken] = error
        found = jnp.sum(error * error, axis=0, keepdims=True)
        clean = jnp.sum(wanted * wanted, axis=0, keepdims=True)
        total = total + jnp.where(row == 0, found, jnp.where(row == 1, clean, 0.0))
    energy[...] = total


def error_energy(own, far, targets):
    rows = own[0].shape[0] + own[1].shape[0]
    return call(
        error_kernel,
        (*own, *far, targets),
        (sds((rows, OUT), F32), sds((8, OUT), F32)),
        rows * OUT * 8,
        rows * OUT * 12,
        placed=True,
    )


def even_sum(parts):
    while len(parts) > 1:
        parts = [first + second for first, second in zip(parts[0::2], parts[1::2])]
    return parts[0]


def stem_sums(values):
    stem = lax.broadcasted_iota(jnp.int32, values.shape, 1) // SAMPLES
    total = jnp.zeros_like(values)
    for k in range(STEMS):
        part = jnp.sum(jnp.where(stem == k, values, 0.0), axis=1, keepdims=True)
        total = jnp.where(stem == k, part, total)
    return total


def dense_back_kernel(segments, present, energies, errors, rest, down, gains, attended_t, branch_out,
                      third, third_inverse, slope, ffn_out, grad_est, grad_ffn, grad_pre,
                      grad_branch, grad_attended_t, delta, grad_gains, loss):
    energy = even_sum([energies[slot] for slot in range(energies.shape[0])])
    lane = lax.broadcasted_iota(jnp.int32, (1, OUT), 1)
    counted = jnp.zeros((1, OUT), F32)
    for k in range(STEMS):
        counted = jnp.where(lane // SAMPLES == k, present[:, k : k + 1].astype(F32), counted)
    counted = counted * (10.0 / math.log(10.0) / (segments * STEMS))
    found = stem_sums(energy[0:1]) + ENERGY_EPS
    clean = stem_sums(energy[1:2]) + ENERGY_EPS
    terms = counted * (jnp.log(found) - jnp.log(clean))
    terms = jnp.where(lane % SAMPLES == 0, terms, 0.0)
    loss[...] = jnp.broadcast_to(jnp.sum(terms, axis=1, keepdims=True), loss.shape)
    low = (errors[...] * (-2.0 * counted / found)).astype(BF)
    grad_est[...] = low
    grad_out = dot(low, rest[:, D + FF :], 1, 1)
    grad_gains[3:4] = jnp.sum(grad_out * ffn_out[...], axis=0, keepdims=True)
    ffn = (grad_out * gains[7:8]).astype(BF)
    grad_ffn[...] = ffn
    hidden = dot(ffn, down[...], 1, 1).astype(BF)
    pre = (hidden.astype(F32) * slope[...]).astype(BF)
    grad_pre[...] = pre
    normed = dot(pre, rest[:, D : D + FF], 1, 1)
    hat = third[...]
    grad_gains[0:1] = jnp.sum(normed * hat, axis=0, keepdims=True)
    grad_gains[1:2] = jnp.sum(normed, axis=0, keepdims=True)
    scaled = normed * gains[4:5]
    grad_mid = grad_out + third_inverse[...] * (
        scaled
        - jnp.mean(scaled, axis=-1, keepdims=True)
        - hat * jnp.mean(scaled * hat, axis=-1, keepdims=True)
    )
    grad_gains[2:3] = jnp.sum(grad_mid * branch_out[...], axis=0, keepdims=True)
    branch = (grad_mid * gains[6:7]).astype(BF)
    grad_branch[...] = branch
    attended = dot(rest[:, :D], branch, 1, 1).astype(BF)
    grad_attended_t[...] = attended
    product = attended.astype(F32) * attended_t[...]
    for h in range(HEADS):
        delta[h : h + 1] = jnp.sum(product[head_rows(h)], axis=0, keepdims=True)


def dense_back(segments, present, energies, errors, rest, down, gains, attended_t, branch_out, third,
               third_inverse, slope, ffn_out):
    rows = errors.shape[0]
    return call(
        functools.partial(dense_back_kernel, segments),
        (present, energies, errors, rest, down, gains, attended_t, branch_out, third,
         third_inverse, slope, ffn_out),
        (
            sds((rows, OUT), BF),
            sds((rows, D), BF),
            sds((rows, FF), BF),
            sds((rows, D), BF),
            sds((D, rows), BF),
            sds((HEADS, rows), F32),
            sds((4, D), F32),
            sds((8, LANES), F32),
        ),
        2 * rows * D * (D + 2 * FF + OUT),
        rows * FF * 8,
    )


def deal(size, place, first, second, keep, send, owner, at):
    slot = owner ^ place[1]
    same = place[0] == 0
    keep[slot, :, at] = jnp.where(same, first, second).astype(BF)
    send[slot, :, at] = jnp.where(same, second, first).astype(BF)


def dense_weights_kernel(size, place, grad_est, grad_ffn, grad_pre, grad_branch, attended_t,
                         normed_two, hidden, out_rows, keep, send, wide, tall):
    half = keep.shape[1]
    wide[:, D + FF :] = dot(out_rows[...], grad_est[...], 0, 0)
    wide[:, D : D + FF] = dot(normed_two[...], grad_pre[...], 0, 0)
    wide[:, :D] = dot(attended_t[...].astype(BF), grad_branch[...])
    tall[...] = dot(hidden[...], grad_ffn[...], 0, 0)
    for owner in range(size):
        row = 2 * owner * half
        deal(
            size, place, wide[row : row + half], wide[row + half : row + 2 * half],
            keep, send, owner, slice(0, REST),
        )
        for part in range(4):
            first = (8 * owner + part) * half
            second = (8 * owner + 4 + part) * half
            deal(
                size, place, tall[first : first + half], tall[second : second + half],
                keep, send, owner, slice(REST + D * part, REST + D * (part + 1)),
            )


def dense_weights(grad_est, grad_ffn, grad_pre, grad_branch, attended_t, normed_two,
                  hidden, out_rows, size):
    rows = grad_est.shape[0]
    piece = (size, D // size // 2, REST + 4 * D)
    return call(
        functools.partial(dense_weights_kernel, size),
        (grad_est, grad_ffn, grad_pre, grad_branch, attended_t, normed_two, hidden, out_rows),
        (sds(piece, BF), sds(piece, BF)),
        2 * rows * D * (D + 2 * FF + OUT),
        rows * FF * 8,
        placed=True,
        scratch=[pltpu.VMEM((D, REST), F32), pltpu.VMEM((FF, D), F32)],
    )


def attend_back_kernel(carried, probs, keys_t, values_t, tops, queries_t, delta, top,
                       inverse_total, grad_attended_t, *refs):
    if carried:
        refs[1][...] = refs[0][...]
    else:
        refs[0][...] = jnp.zeros_like(refs[0])
    grad_queries, grad_kv = refs[-2:]

    def visit(block):
        factor = jnp.exp2(tops[block] - top[...]) * inverse_total[...]
        shift = delta[...] * factor

        def begin(h):
            grad = grad_attended_t[head_rows(h)].astype(F32) * factor[h : h + 1]
            grad = grad.astype(BF)
            return grad, dot(values_t[block, head_rows(h)], grad, 0, 0)

        def turn(h, found):
            grad, grad_probs = found
            scores = probs[block, h].astype(F32) * (grad_probs - shift[h : h + 1])
            return grad, scores.astype(BF)

        def end(h, found):
            grad, scores = found
            at = head_rows(h)
            grad_queries[at] += dot(keys_t[block, at], scores)
            grad_kv[block, at] = (dot(queries_t[at], scores, 1, 1) * LOG_TWO).astype(BF)
            grad_kv[block, head_rows(h, D)] = dot(grad, probs[block, h], 1, 1).astype(BF)

        heads_in_step(begin, turn, end)

    over_blocks(probs.shape[0], visit)


def attend_back(saved, queries_t, delta, top, inverse_total, grad_attended_t, carry):
    probs, keys_t, values_t, tops = saved
    count, _, rows, tokens = probs.shape
    carry = () if carry is None else (carry,)
    return call(
        functools.partial(attend_back_kernel, len(carry)),
        (probs, keys_t, values_t, tops, queries_t, delta, top, inverse_total,
         grad_attended_t, *carry),
        (sds((D, tokens), F32), sds((count, 2 * D, rows), BF)),
        count * (8 * rows * tokens * D * 5),
        count * (HEADS * rows * tokens * 2),
    )


def unit_products(units, grads):
    total = None
    for k in range(0, len(units), 4):
        left = jnp.concatenate(units[k : k + 4], axis=1)
        left = jnp.concatenate([left, jnp.ones((16, left.shape[1]), BF)], axis=0)
        term = dot(left, jnp.concatenate(grads[k : k + 4], axis=1), 1, 1)
        total = term if total is None else total + term
    return total


def finish_kernel(size, groups, place, grad_queries, own_unit_t, weights, gains, late, *refs):
    grads, units = refs[:groups], refs[groups : 2 * groups]
    keep, send, full, grad_gains = refs[2 * groups :]
    query = (grad_queries[...] * SCALE).astype(BF)
    blocks = [(g, block) for g, grad in enumerate(grads) for block in range(grad.shape[0])]
    found = (
        unit_products([own_unit_t[...]], [query]),
        unit_products([units[g][b] for g, b in blocks], [grads[g][b] for g, b in blocks]),
    )
    columns = gains[...].T
    lane = lax.broadcasted_iota(jnp.int32, (D, LANES), 1)
    small = jnp.zeros((D, LANES), F32)
    for product, first, row in zip(found, (0, D), (0, 2)):
        at = slice(first, first + product.shape[1])
        moment, total = product[:D], product[D : D + 1]
        weight = weights[:, at].astype(F32)
        for k, terms in enumerate((weight * moment, weight * total)):
            small = jnp.where(lane == row + k, jnp.sum(terms, axis=1, keepdims=True), small)
        value = moment * columns[:, row : row + 1] + total * columns[:, row + 1 : row + 2]
        full[:, at] = value.astype(BF)
    grad_gains[:4] = small.T[:4]
    grad_gains[4:8] = late[...]
    half = keep.shape[1]
    for owner in range(size):
        row = 2 * owner * half
        deal(
            size, place, full[row : row + half], full[row + half : row + 2 * half],
            keep, send, owner, slice(0, QKV),
        )
    same = place[0] == 0
    tall, across = gain_shape(size)
    for owner in range(size):
        rows = [
            grad_gains[vector : vector + 1, lane : lane + across]
            for where, _, vector, lane, _ in gain_places(size)
            if where == owner
        ]
        block = jnp.concatenate(rows + [jnp.zeros((half - tall, across), F32)], axis=0)
        if across < LANES:
            block = jnp.concatenate([block, jnp.zeros((half, LANES - across), F32)], axis=1)
        slot = owner ^ place[1]
        keep[slot, :, QKV:] = jnp.where(same, block, 0.0).astype(BF)
        send[slot, :, QKV:] = jnp.where(same, 0.0, block).astype(BF)


def finish(grad_queries, own_unit_t, weights, gains, late, grads, units, size):
    rows = own_unit_t.shape[1]
    piece = (size, D // size // 2, QKV + LANES)
    return call(
        functools.partial(finish_kernel, size, len(grads)),
        (grad_queries, own_unit_t, weights, gains, late, *grads, *units),
        (sds(piece, BF), sds(piece, BF)),
        2 * rows * D * QKV * size,
        rows * D * 2 * size,
        placed=True,
        scratch=[
            pltpu.VMEM((D, QKV), BF),
            pltpu.VMEM((8, D), F32),
        ],
    )


def square_kernel(*refs):
    found = []
    for ref in refs[:4]:
        values = ref[...].astype(F32)
        rows = jnp.sum(values * values, axis=0, keepdims=True)
        found.append(jnp.sum(rows, axis=1, keepdims=True))
    refs[4][...] = jnp.broadcast_to(even_sum(found), refs[4].shape)


def square_sum(*parts):
    size = sum(x.size for x in parts)
    return call(square_kernel, parts, sds((8, LANES), F32), 2 * size, 2 * size)


def bits(size):
    return [1 << k for k in range(size.bit_length() - 1)]


def masks(size):
    return sorted(range(1, size), key=lambda mask: (mask.bit_count(), mask))


def tie(*values):
    return lax.optimization_barrier(values)


def add_low(left, right):
    return (left.astype(F32) + right.astype(F32)).astype(BF)


def core_step(keep, send):
    return add_low(keep, swap(send, "seg", 1))


def send_members(total, size):
    return [total[0]] + [swap(total[mask], "wide", mask) for mask in range(1, size)]


def sum_low(parts):
    return functools.reduce(jnp.add, [x.astype(F32) for x in parts]).astype(BF)


def exchange(values, size):
    return jnp.stack([values] + [swap(values, "wide", mask) for mask in range(1, size)])


def segment_step(total):
    for mask in bits(lax.axis_size("seg"))[1:]:
        total = add_low(total, swap(total, "seg", mask))
    return total


def adam_update(weight, grad, moment, second, rate):
    moment = BETA_ONE * moment + (1 - BETA_ONE) * grad
    second = BETA_TWO * second + (1 - BETA_TWO) * (grad * grad)
    fixed_one = moment * (rate / (1 - BETA_ONE**ADAM_STEP))
    fixed_two = second * (1 / (1 - BETA_TWO**ADAM_STEP))
    weight = weight * (1 - rate * WEIGHT_DECAY) - fixed_one / (jnp.sqrt(fixed_two) + ADAM_EPS)
    return (weight, moment, second)


def adam_chunks(size, half):
    tall, across = gain_shape(size)
    chunks = []
    for side in range(2):
        rows, ends = slice(4 * side * half, 4 * (side + 1) * half), slice(0, D)
        parts = [
            (slice((4 * side + k) * half, (4 * side + k + 1) * half), ends, 0,
             slice(REST + D * k, REST + D * (k + 1)))
            for k in range(4)
        ]
        chunks.append((1, side, rows, ends, parts))
        rows = slice(side * half, (side + 1) * half)
        parts = [
            (rows, slice(0, QKV), 1, slice(0, QKV)),
            (rows, slice(QKV, QKV + REST), 0, slice(0, REST)),
        ]
        chunks.append((0, side, rows, slice(0, QKV + REST), parts))
    rows, lanes = slice(0, tall), slice(0, across)
    chunks.append((2, 0, rows, lanes, [(rows, lanes, 1, slice(QKV, QKV + across))]))
    return chunks


def tiles(rows, lanes, source):
    high, across = rows.stop - rows.start, lanes.stop - lanes.start
    for row in range(0, high, 16):
        tall = min(16, high - row)
        for lane in range(0, across, D):
            part = min(D, across - lane)
            yield (
                (slice(rows.start + row, rows.start + row + tall),
                 slice(lanes.start + lane, lanes.start + lane + part)),
                (slice(row, row + tall),
                 slice(source.start + lane, source.start + lane + part)),
            )


def adam_kernel(size, place, squares, squares_other, early, early_other, late, late_other,
                *refs):
    states, outs, norm = [refs[k : k + 3] for k in (0, 3, 6)], refs[9:21], refs[21]
    held, sems = refs[22:34], refs[34]
    same = place[0] == 0
    grad_norm = jnp.sqrt(squares[0:1, 0:1] + squares_other[0:1, 0:1])
    norm[...] = grad_norm
    factor = jnp.minimum(1.0, CLIP_LIMIT / (grad_norm + 1e-06))
    copies, aligned = [], early.shape[0] % 16 == 0

    def send(source, target):
        copies.append(pltpu.make_async_copy(source, target, sems.at[len(copies)]))
        copies[-1].start()

    for index, side, rows, lanes, parts in adam_chunks(size, early.shape[0]):
        rate = GAIN_RATE if index == 2 else LEARN_RATE
        for part_rows, part_lanes, which, source in parts:
            own, other = (late, late_other) if which else (early, early_other)
            if side:
                own, other = other, own
            for here, there in tiles(part_rows, part_lanes, source):
                grad = jnp.where(same, own[there].astype(F32), other[there].astype(F32))
                weight, moment, second = (x[index][here] for x in states)
                found = adam_update(weight, grad * factor, moment, second, rate)
                for kind, value in enumerate((*found, found[0].astype(BF))):
                    held[3 * kind + index][here] = value
        if aligned:
            for slot in range(index, 12, 3):
                send(held[slot].at[rows, lanes], outs[slot].at[rows, lanes])
    if not aligned:
        for slot in range(12):
            send(held[slot], outs[slot])
    for copy in copies:
        copy.wait()


def adam(squares, grads, states, size):
    flat = gain_shape(size)
    states = [x.reshape(flat) if x.ndim == 1 else x for x in states]
    shapes = [x.shape for x in states[:3]]
    count = sum(x.size for x in states[:3])
    kinds = [(shape, F32) for shape in shapes] * 3 + [(shape, BF) for shape in shapes]
    outside = pl.BlockSpec(memory_space=pl.ANY)
    return call(
        functools.partial(adam_kernel, size),
        (*squares, *grads, *states),
        tuple(sds(*kind) for kind in kinds) + (sds((1, 1), F32),),
        20 * count,
        28 * count,
        placed=True,
        out_specs=(outside,) * 12 + (pl.BlockSpec(memory_space=pltpu.VMEM),),
        scratch=[pltpu.VMEM(*kind) for kind in kinds]
        + [pltpu.SemaphoreType.DMA((4 * len(adam_chunks(size, grads[0].shape[0])),))],
    )


def body(
    encoded,
    targets,
    present,
    wide_master,
    down_master,
    gain_master,
    wide_first,
    down_first,
    gain_first,
    wide_second,
    down_second,
    gain_second,
):
    size = lax.axis_size("wide") // 2
    position = lax.axis_index("wide") % size
    core = lax.axis_index("seg") % 2
    own = encoded[0]
    far = {0: swap(own, "wide", size)}
    first, rest = pack(wide_master, down_master, gain_master, size)

    high = size // 2
    first_mine = jnp.stack([first] + [swap(first, "wide", mask) for mask in range(1, size)])
    low_mine = [rest] + [swap(rest, "wide", mask) for mask in range(1, high)]
    far[0], first_mine, *low_mine = tie(far[0], first_mine, *low_mine)
    first_other = swap(first_mine, "seg", 1)
    far[high] = swap(far[0], "wide", high)
    for mask in range(1, high):
        far[mask] = swap(far[0], "wide", mask)
    queries_t, own_unit_t, weights_t, gains, first_all = start(own, first_mine, first_other, size)

    high_mine = swap(jnp.stack(low_mine), "wide", high)
    order = [high, *range(1, high), *range(high + 1, size)]
    groups = [[0]] + [order[k : k + 2] for k in range(0, size - 1, 2)]

    carry = None
    saved, units = [], []
    for group in groups:
        if len(saved) == 1:
            near = [far[mask] for mask in range(1, high)]
            near, far[high], carry[0], *low_mine = tie(near, far[high], carry[0], *low_mine)
            far.update(zip(range(1, high), near))
            low_other = [swap(x, "seg", 1) for x in low_mine]
            for mask in range(1, high):
                far[high + mask] = swap(far[high], "wide", mask)
        probs, keys_t, values_t, unit, tops, *carry = attend(
            [far[mask] for mask in group], queries_t, weights_t, gains, carry
        )
        saved.append((probs, keys_t, values_t, tops))
        if len(saved) == 2:
            carry[0], *low_other = tie(carry[0], *low_other)
        units.append(unit)
    accum, top = carry
    accum, high_mine = tie(accum, high_mine)
    high_other = swap(high_mine, "seg", 1)
    pieces = (*low_mine, high_mine, *low_other, high_other)

    rest_all, down_all = unpack(pieces, size)
    started, own_parts, far_parts = (), [], []
    for part in range(2):
        *started, estimate = dense_forward(
            part, own, accum, rest_all, down_all, gains, started
        )
        own_parts.append(estimate)
        far_parts.append(swap(estimate, "wide", size))
    (attended_t, inverse_total, branch_out, third, third_inverse, normed_two, slope, hidden,
     ffn_out, out_rows) = started

    errors, energy = error_energy(own_parts, far_parts, targets[0])
    energy = exchange(energy, size)
    seg_count = lax.axis_size("seg")
    (grad_est, grad_ffn, grad_pre, grad_branch, grad_attended_t, delta, late_gains,
     loss) = dense_back(
        seg_count, present, energy, errors, rest_all, down_all, gains, attended_t, branch_out,
        third, third_inverse, slope, ffn_out,
    )
    keep, send = dense_weights(
        grad_est, grad_ffn, grad_pre, grad_branch, attended_t, normed_two, hidden,
        out_rows, size,
    )
    grad_attended_t, keep, send = tie(grad_attended_t, keep, send)

    early = core_step(keep, send)
    grad_queries, grads = None, []
    for k, item in enumerate(saved):
        grad_queries, grad_kv = attend_back(
            item, queries_t, delta, top, inverse_total, grad_attended_t, grad_queries
        )
        grads.append(grad_kv)
        if k == 0:
            grad_queries, early = tie(grad_queries, early)
            early = send_members(early, size)
    keep, send = finish(
        grad_queries, own_unit_t, first_all, gains, late_gains, grads, units, size
    )
    keep, send, *early = tie(keep, send, *early)
    late = core_step(keep, send)
    early = segment_step(sum_low(early))
    late, loss = tie(late, loss)
    for mask in bits(seg_count):
        loss = loss + swap(loss, "seg", mask)
    late = sum_low(send_members(late, size))
    late, loss, early = tie(late, loss, early)
    early_other = swap(early, "seg", 1)
    late = segment_step(late)
    late_other = swap(late, "seg", 1)

    squares = square_sum(early, early_other, late, late_other)
    squares = even_sum([squares] + [swap(squares, "wide", mask) for mask in range(1, size)])
    squares_other = swap(squares, "wide", size)
    *updated, grad_norm = adam(
        (squares, squares_other),
        (early, early_other, late, late_other),
        (wide_master, down_master, gain_master, wide_first, down_first, gain_first,
         wide_second, down_second, gain_second),
        size,
    )
    return (
        loss[0, 0],
        grad_norm.reshape(()),
        *(x.reshape(-1) if k % 3 == 2 else x for k, x in enumerate(updated)),
    )


def solution(mesh):
    split, line = P("wide", None), P("wide")
    states = (split, split, line)
    return jax.shard_map(
        body,
        mesh=mesh,
        in_specs=(P("seg", "wide", None), P("seg", None, None), P("seg", None)) + states * 3,
        out_specs=(P(), P()) + states * 4,
        check_vma=False,
    )
```
